32 devices in a mesh: dp: 4 (over z), expert: 8 (over y, x, core).
Axes of the slice: x: 2, y: 2, z: 4, core: 2. Of those that a mesh axis runs over, the one named last changes fastest.
Arguments:
- hidden_in: bfloat16 [8192, 1536], P(('dp', 'expert')), may hold values from -6 to 6
- teacher: bfloat16 [8192, 1536], P(('dp', 'expert')), may hold values from -6 to 6
- valid: int32 [8192], P(('dp', 'expert')), may hold values from 0 to 1, as said below
- routes: int32 [8192, 8], P(('dp', 'expert')), may hold values from 0 to 23, all different within a row; in each aligned block of 256 rows (0 to 255, 256 to 511, ...) at most 104 rows name the same one
- gain_attn: bfloat16 [1536], P('dp'), may hold values from 0.5 to 1.5
- gain_moe: bfloat16 [1536], P('dp'), may hold values from 0.5 to 1.5
- w_query: bfloat16 [1536, 1536], P('dp'), may hold values from -0.625 to 0.625
- w_key: bfloat16 [1536, 512], P('dp'), may hold values from -0.625 to 0.625
- w_value: bfloat16 [1536, 512], P('dp'), may hold values from -0.15625 to 0.15625
- w_out: bfloat16 [1536, 1536], P('dp'), may hold values from -4 to 4
- w_router: bfloat16 [1536, 24], P('dp'), may hold values from -0.078125 to 0.078125
- w_gate_up: bfloat16 [24, 1536, 1024], P('expert', 'dp'), may hold values from -0.15625 to 0.15625
- w_down: bfloat16 [24, 512, 1536], P('expert', 'dp'), may hold values from -6 to 6
Outputs:
- activations: bfloat16 [8192, 1536], P(('dp', 'expert'))
- loss: float32 [], replicated
- grad_in: float32 [8192, 1536], P(('dp', 'expert'))
- grad_gain_attn: float32 [1536], P('dp')
- grad_gain_moe: float32 [1536], P('dp')
- grad_query: float32 [1536, 1536], P('dp')
- grad_key: float32 [1536, 512], P('dp')
- grad_value: float32 [1536, 512], P('dp')
- grad_out: float32 [1536, 1536], P('dp')
- grad_router: float32 [1536, 24], P('dp')
- grad_gate_up: float32 [24, 1536, 1024], P('expert', 'dp')
- grad_down: float32 [24, 512, 1536], P('expert', 'dp')
The draws below stay inside these ranges and needn't reach their ends.
Inputs may be any that keep to these rules, and one draw needn't show every extreme that they name: `valid`: 1 marks a token that counts in the loss; token 0 always counts. `routes`: each row names 8 different experts. Among the rows of one device no expert is named more than 104 times, a bound that some block reaches.
All inputs are finite; a program needn't handle non-finite values.
Results may differ from the reference program's by a relative error of at most 0.02.
Values may be sent and summed in bfloat16 or wider, within the bound.
A program may use at most 256 MiB of HBM per device.

```python
import math
import jax
import jax.numpy as jnp
import numpy as np
from jax import lax

D = 1536
H = 24
KVH = 8
HD = 64
FF = 512
TOP = 8
TOK_DEV = 256
EXPERTS = 24
LENGTH = 1024
MOST = 104
TOKENS = 8192


def draw_valid(key, part):
    ranks = jnp.arange(TOKENS, dtype=jnp.int32)
    drawn = jax.random.randint(key, (TOKENS,), 0, 2 * TOKENS, dtype=jnp.int32)
    chosen = (drawn < TOKENS // 2 + ranks) | (ranks == 0)
    return chosen.astype(jnp.int32)


def level_of(key, shape, cuts, low, top_value):
    loudness, own = 1.0, jax.random.fold_in(key, 6)
    for position, parts in cuts:
        draws = jnp.exp(jax.random.uniform(jax.random.fold_in(own, position), (parts,), jnp.float32, low / len(cuts), top_value / len(cuts)))
        loudness = loudness * jnp.repeat(draws, shape[position] // parts).reshape([-1 if axis == position else 1 for axis in range(len(shape))])
    return loudness


def routed_block(own_key, own, number, rows, count, top, limit, slope):
    sequence = jax.random.permutation(own_key, count)
    heavy_load, ordinary = shares(count, rows * top, limit, slope, True), shares(count, rows * top, limit, slope, False)
    places = jnp.arange(count)

    def named(tallies, rotation):
        used = int((tallies > 0).sum())
        fixed = max(1, used // 4)
        shifted = fixed + (places - fixed + rotation * (used - fixed)) % max(1, count - fixed)
        return jnp.zeros((count,), jnp.int32).at[sequence[jnp.where(places < fixed, places, shifted)]].set(jnp.asarray(tallies, jnp.int32))

    tallies = jnp.where(number % 4 == 0, named(heavy_load, number // 4), named(ordinary, number - number // 4 - 1))
    mixed = jax.random.permutation(jax.random.fold_in(own, 3), count)
    source_of, receiver = mixed[0:count // 2 * 2:2], mixed[1:count // 2 * 2:2]
    room = jnp.minimum(tallies[source_of] - 1, limit - tallies[receiver]) // 2
    room = jnp.where((source_of == sequence[0]) | (receiver == sequence[0]) | (tallies[receiver] == 0), 0, jnp.maximum(room, 0))
    shifted = jax.random.randint(jax.random.fold_in(own, 4), (count // 2,), 0, 1 << 20) % (room + 1)
    tallies = tallies.at[source_of].add(-shifted).at[receiver].add(shifted)
    items = jnp.searchsorted(jnp.cumsum(tallies), jnp.arange(rows * top), side="right").astype(jnp.int32)
    grid = items.reshape(top, rows).T
    grid = grid[jax.random.permutation(jax.random.fold_in(own, 1), rows)]
    rotation = jax.random.randint(jax.random.fold_in(own, 2), (rows, 1), 0, top)
    return jnp.take_along_axis(grid, (jnp.arange(top)[None, :] + rotation) % top, axis=1)


def shares(number_of, total, reach, lean, full):
    loads = [(1 << 20) // math.isqrt(grade ** lean) + 1 for grade in range(1, number_of + 1)]
    largest = reach if full else min(reach, max(-(-total // number_of), total * loads[0] // sum(loads)))
    least = 1 if total - largest >= number_of - 1 else 0
    counts, spare = [largest] + [least] * (number_of - 1), total - largest - least * (number_of - 1)
    while spare > 0:
        free = [i for i in range(1, number_of) if counts[i] < largest] or [i for i in range(1, number_of) if counts[i] < reach]
        mass, remaining = sum([loads[i] for i in free]), spare
        for i in free:
            more = min(reach - counts[i], max(1, remaining * loads[i] // mass), spare)
            counts[i] = counts[i] + more
            spare = spare - more
    return np.array(counts)


def gaussian(key, shape, scale, bound, cuts=(), kind=jnp.bfloat16):
    entries = scale * jax.random.normal(key, shape, jnp.float32)
    if cuts:
        entries = entries * level_of(key, shape, cuts, -0.22, 0.18)
    return jnp.clip(entries, -bound, bound).astype(kind)


def setup_inputs(seed: int = 0) -> dict:
    streams_of = jax.random.split(jax.random.key(seed), 14)
    hidden_in = gaussian(streams_of[0], (TOKENS, D), 1.0, 6.0, ((0, 32),))
    teacher = gaussian(streams_of[1], (TOKENS, D), 1.0, 6.0, ((0, 32),))
    valid = draw_valid(jax.random.fold_in(streams_of[13], 71), 0)
    routes_keys = jax.random.split(jax.random.fold_in(streams_of[3], 1), TOKENS // TOK_DEV)
    routes_turns = jax.random.permutation(jax.random.fold_in(streams_of[3], 3), TOKENS // TOK_DEV)
    routes = jax.vmap(lambda own, number: routed_block(jax.random.fold_in(streams_of[3], 2), own, number, TOK_DEV, EXPERTS, TOP, MOST, 1))(routes_keys, routes_turns).reshape((TOKENS, TOP))
    gain_attn = jnp.clip(1.0 + 0.1 * jax.random.normal(streams_of[4], (D,), jnp.float32), 0.5, 1.5).astype(jnp.bfloat16)
    gain_moe = jnp.clip(1.0 + 0.1 * jax.random.normal(streams_of[5], (D,), jnp.float32), 0.5, 1.5).astype(jnp.bfloat16)
    w_query = gaussian(streams_of[6], (D, H * HD), (D // 16) ** -0.5, 0.625, ((0, 4),))
    w_key = gaussian(streams_of[7], (D, KVH * HD), (D // 16) ** -0.5, 0.625, ((0, 4),))
    w_value = gaussian(streams_of[8], (D, KVH * HD), D ** -0.5, 0.15625, ((0, 4),))
    w_out = gaussian(streams_of[9], (H * HD, D), 2 ** -0.5, 4.0, ((0, 4),))
    w_router = gaussian(streams_of[10], (D, EXPERTS), (4 * D) ** -0.5, 0.078125, ((0, 4),))
    w_gate_up = gaussian(streams_of[11], (EXPERTS, D, 2 * FF), D ** -0.5, 0.15625, ((0, 8), (1, 4)))
    w_down = gaussian(streams_of[12], (EXPERTS, FF, D), 1 ** -0.5, 6.0, ((0, 8), (1, 4)))
    return dict(hidden_in=hidden_in, teacher=teacher, valid=valid, routes=routes, gain_attn=gain_attn, gain_moe=gain_moe, w_query=w_query, w_key=w_key, w_value=w_value, w_out=w_out, w_router=w_router, w_gate_up=w_gate_up, w_down=w_down)


EPS = 1e-05
RESIDUAL = 0.22
SCORE_SCALE = 1.0 / 64.0
ROPE_BASE = 10000.0
NEG = -1000000000.0
HIGH = lax.Precision.HIGHEST

@jax.custom_vjp
def low(v):
    return lax.optimization_barrier(v.astype(jnp.bfloat16)).astype(jnp.float32)

@jax.custom_vjp
def low_back(v):
    return v

def low_keep(v):
    return (low(v), None)

def low_pass(kept, grad):
    return (grad,)

def back_keep(v):
    return (v, None)

def back_low(kept, grad):
    return (low(grad),)
low.defvjp(low_keep, low_pass)
low_back.defvjp(back_keep, back_low)

def rms_norm(states, gain):
    return states * lax.rsqrt(lax.optimization_barrier(jnp.mean(states * states, axis=-1, keepdims=True)) + EPS) * gain

def rope_tables(positions):
    half_dim = HD // 2
    frequencies = ROPE_BASE ** (-(2.0 * jnp.arange(half_dim, dtype=jnp.float32)) / HD)
    angles = positions[:, None] * frequencies[None, :]
    return (jnp.cos(angles)[:, None, :], jnp.sin(angles)[:, None, :])

def rotary(heads_in, cosine_table, sine_table):
    half_dim = heads_in.shape[-1] // 2
    first_half = heads_in[..., :half_dim]
    second_half = heads_in[..., half_dim:]
    return jnp.concatenate([first_half * cosine_table - second_half * sine_table, second_half * cosine_table + first_half * sine_table], axis=-1)

def swiglu(gate_part, up_part):
    return gate_part * jax.nn.sigmoid(gate_part) * up_part

def soft_weights(scores):
    return jnp.exp(scores - jax.nn.logsumexp(scores, axis=-1, keepdims=True))

def attend(pieces):
    queries, key_heads, value_heads = pieces
    grouped = queries.reshape(LENGTH, KVH, H // KVH, HD)
    raw_scores = jnp.einsum('qhgd,khd->hgqk', grouped, key_heads, precision=HIGH) * SCORE_SCALE
    causal = jnp.arange(LENGTH)[:, None] >= jnp.arange(LENGTH)[None, :]
    scores = low_back(jnp.where(causal[None, None], raw_scores, NEG))
    attn_probs = low(soft_weights(scores))
    context = jnp.einsum('hgqk,khd->qhgd', attn_probs, value_heads, precision=HIGH)
    return context.reshape(LENGTH, H * HD)

def block_forward(params, inputs, target, valid_rows, block_routes):
    gain_one, gain_two, w_query, w_key, w_value, w_out, w_router, w_gate_up, w_down = params
    row_count = inputs.shape[0]
    normed = low(rms_norm(inputs, gain_one))
    query_lin = low_back(jnp.dot(normed, w_query, precision=HIGH))
    key_lin = low_back(jnp.dot(normed, w_key, precision=HIGH))
    value_lin = low_back(jnp.dot(normed, w_value, precision=HIGH))
    positions = (jnp.arange(row_count, dtype=jnp.int32) % LENGTH).astype(jnp.float32)
    cosine_table, sine_table = rope_tables(positions)
    queries = low(rotary(query_lin.reshape(row_count, H, HD), cosine_table, sine_table))
    key_heads = low(rotary(key_lin.reshape(row_count, KVH, HD), cosine_table, sine_table))
    value_heads = low(value_lin.reshape(row_count, KVH, HD))
    seq_count = row_count // LENGTH
    context = lax.map(jax.checkpoint(attend), (queries.reshape(seq_count, LENGTH, H, HD), key_heads.reshape(seq_count, LENGTH, KVH, HD), value_heads.reshape(seq_count, LENGTH, KVH, HD)))
    context = low(low_back(context.reshape(row_count, H * HD)))
    mid = inputs + RESIDUAL * low_back(jnp.dot(context, w_out, precision=HIGH))
    moe_input = low(rms_norm(mid, gain_two))
    logits = low_back(jnp.dot(moe_input, w_router, precision=HIGH))
    route_hot = block_routes[:, :, None] == jnp.arange(EXPERTS, dtype=jnp.int32)[None, None, :]
    chosen = lax.optimization_barrier(jnp.sum(jnp.where(route_hot, logits[:, None, :], 0.0), axis=-1))
    gate_weights = soft_weights(chosen)

    def expert_span(pieces):
        span_rows, span_routes, span_gates = pieces
        flat_routes = span_routes.reshape(-1).astype(jnp.int32)
        flat_hot = (flat_routes[:, None] == jnp.arange(EXPERTS, dtype=jnp.int32)[None, :]).astype(jnp.int32)
        ranking = lax.optimization_barrier(jnp.sum((jnp.cumsum(flat_hot, axis=0) - flat_hot) * flat_hot, axis=1)).astype(jnp.int32)
        slot_index = (flat_routes * MOST + ranking).astype(jnp.int32)
        row_of_slot = jnp.zeros((EXPERTS * MOST,), jnp.int32).at[slot_index].set(jnp.arange(TOK_DEV * TOP, dtype=jnp.int32))
        filled = jnp.zeros((EXPERTS * MOST,), jnp.float32).at[slot_index].set(1.0)
        arrived = low_back(span_rows[row_of_slot // TOP] * filled[:, None]).reshape(EXPERTS, MOST, D)
        gate_up = low_back(jnp.einsum('ecd,edf->ecf', arrived, w_gate_up, precision=HIGH))
        hidden = low(swiglu(gate_up[..., :FF], gate_up[..., FF:]))
        produced = low(low_back(jnp.einsum('ecf,efd->ecd', hidden, w_down, precision=HIGH)))
        picked = produced.reshape(EXPERTS * MOST, D)[slot_index].reshape(TOK_DEV, TOP, D)
        return lax.optimization_barrier(jnp.sum(span_gates[:, :, None] * picked, axis=1))
    spans = row_count // TOK_DEV
    experts_sum = lax.map(expert_span, (moe_input.reshape(spans, TOK_DEV, D), block_routes.reshape(spans, TOK_DEV, TOP), gate_weights.reshape(spans, TOK_DEV, TOP))).reshape(row_count, D)
    final_state = mid + RESIDUAL * experts_sum
    mismatch = final_state - target
    squares = 0.5 * jnp.sum(valid_rows[:, None] * mismatch * mismatch)
    return (final_state, squares)

def reference(hidden_in, teacher, valid, routes, gain_attn, gain_moe, w_query, w_key, w_value, w_out, w_router, w_gate_up, w_down):
    params = tuple((weight.astype(jnp.float32) for weight in (gain_attn, gain_moe, w_query, w_key, w_value, w_out, w_router, w_gate_up, w_down)))
    valid_float = valid.astype(jnp.float32)
    valid_count = jnp.sum(valid_float)
    grad_scale = TOKENS / valid_count
    seq_total = TOKENS // LENGTH
    per_block = math.gcd(seq_total, max(1, 4096 // LENGTH))
    block_rows = per_block * LENGTH
    blocks = TOKENS // block_rows

    def block_step(carried, block_index):
        grad_sums, squares = carried
        row_start = (block_index * block_rows).astype(jnp.int32)
        inputs = lax.dynamic_slice_in_dim(hidden_in, row_start, block_rows, 0).astype(jnp.float32)
        target = lax.dynamic_slice_in_dim(teacher, row_start, block_rows, 0).astype(jnp.float32)
        valid_rows = lax.dynamic_slice_in_dim(valid_float, row_start, block_rows, 0)
        block_routes = lax.dynamic_slice_in_dim(routes, row_start, block_rows, 0)

        def forward(weights, states):
            return block_forward(weights, states, target, valid_rows, block_routes)
        (final_state, squares_part), pullback = jax.vjp(forward, params, inputs)
        gradients, grad_inputs = pullback((jnp.zeros_like(final_state), grad_scale.astype(jnp.float32)))
        grad_sums = jax.tree.map(lambda left, right: left + right, grad_sums, gradients)
        return ((grad_sums, squares + squares_part), (final_state.astype(jnp.bfloat16), grad_inputs))
    zero_grads = tuple((jnp.zeros_like(weight) for weight in params))
    (grad_sums, squares), (finals, grads_in) = lax.scan(block_step, (zero_grads, jnp.zeros((), jnp.float32)), jnp.arange(blocks, dtype=jnp.int32))
    loss_value = squares / (valid_count * D)
    g_one, g_two, g_query, g_key, g_value, g_out, g_router, g_gate_up, g_down = grad_sums
    return (finals.reshape(TOKENS, D), loss_value, grads_in.reshape(TOKENS, D), g_one, g_two, g_query, g_key, g_value, g_out, g_router, g_gate_up, g_down)
```

```python
import jax
import jax.numpy as jnp
from jax import lax
from jax.sharding import PartitionSpec as P

H = 24
KVH = 8
HD = 64
FF = 512
TOP = 8
EXP_DEV = 3
SEQ_MIN = 1024

EPS = 1e-05
RESIDUAL = 0.22
SCORE_SCALE = 1.0 / 64.0
ROPE_BASE = 10000.0
NEG = -1000000000.0

f32 = jnp.float32
bf16 = jnp.bfloat16


def mm(spec, a, b):
    return jnp.einsum(spec, a, b, preferred_element_type=f32)


def rms_norm(states, gain):
    return states * lax.rsqrt(jnp.mean(states * states, axis=-1, keepdims=True) + EPS) * gain


def rope_tables(positions):
    half_dim = HD // 2
    frequencies = ROPE_BASE ** (-(2.0 * jnp.arange(half_dim, dtype=f32)) / HD)
    angles = positions[:, None] * frequencies[None, :]
    return (jnp.cos(angles)[:, None, :], jnp.sin(angles)[:, None, :])


def rotary(heads_in, cosine_table, sine_table):
    half_dim = heads_in.shape[-1] // 2
    first = heads_in[..., :half_dim]
    second = heads_in[..., half_dim:]
    return jnp.concatenate(
        [first * cosine_table - second * sine_table, second * cosine_table + first * sine_table],
        axis=-1,
    )


def send(x, axis, mask):
    count = lax.axis_size(axis)
    return lax.ppermute(x, axis, [(i, i ^ mask) for i in range(count)])


def gather_blocks(x, count):
    blocks = [x]
    for j in range(1, count):
        blocks.append(send(blocks[j - 1], "expert", 1) if j % 2 else send(x, "expert", j))
    return blocks


def scatter_sum(parts):
    total = None
    for j in range(0, len(parts), 2):
        chip = parts[j].astype(f32) + send(parts[j + 1], "expert", 1).astype(f32)
        if j:
            chip = send(chip.astype(bf16), "expert", j).astype(f32)
        total = chip if total is None else total + chip
    return total


def total_over(x, axis):
    mask = 1
    while mask < lax.axis_size(axis):
        x = x + send(x, axis, mask)
        mask *= 2
    return x


def place(blocks, starts, axis, size):
    width = blocks[0].shape[axis]
    shape = list(blocks[0].shape)
    shape[axis] = size * width
    out = jnp.zeros(shape, blocks[0].dtype)
    for block, start in zip(blocks, starts):
        out = lax.dynamic_update_slice_in_dim(out, block, start * width, axis)
    return out


def pick(x, index, width, axis):
    return lax.dynamic_slice_in_dim(x, index * width, width, axis)


def attend(queries, keys, values):
    count = queries.shape[0]
    raw = mm("qhgd,khd->hgqk", queries, keys) * SCORE_SCALE
    causal = jnp.arange(count)[:, None] >= jnp.arange(count)[None, :]
    scores = jnp.where(causal[None, None], raw, NEG)
    top = jnp.max(scores, axis=-1, keepdims=True)
    log_total = top + jnp.log(jnp.sum(jnp.exp(scores - top), axis=-1, keepdims=True))
    probs = jnp.exp(scores - log_total).astype(bf16)
    context = mm("hgqk,khd->qhgd", probs, values).astype(bf16)
    return context, log_total


def attend_back(queries, keys, values, log_total, grad_context):
    count = queries.shape[0]
    raw = mm("qhgd,khd->hgqk", queries, keys) * SCORE_SCALE
    causal = jnp.arange(count)[:, None] >= jnp.arange(count)[None, :]
    probs = jnp.exp(jnp.where(causal[None, None], raw, NEG) - log_total)
    grad_probs = mm("qhgd,khd->hgqk", grad_context, values)
    delta = jnp.sum(probs * grad_probs, axis=-1, keepdims=True)
    grad_scores = (probs * (grad_probs - delta)).astype(bf16)
    grad_queries = mm("hgqk,khd->qhgd", grad_scores, keys) * SCORE_SCALE
    grad_keys = mm("hgqk,qhgd->khd", grad_scores, queries) * SCORE_SCALE
    grad_values = mm("hgqk,qhgd->khd", probs.astype(bf16), grad_context)
    return grad_queries, grad_keys, grad_values


def body(
    hidden_in,
    teacher,
    valid,
    routes,
    gain_attn,
    gain_moe,
    w_query,
    w_key,
    w_value,
    w_out,
    w_router,
    w_gate_up,
    w_down,
):
    tok, width = hidden_in.shape
    owners = lax.axis_size("expert")
    replicas = lax.axis_size("dp")
    me = lax.axis_index("expert")
    plane = lax.axis_index("dp")
    length = min(SEQ_MIN, owners * tok)
    group = length // tok
    head = me % group
    experts_all = EXP_DEV * owners
    slots = 8 * ((tok * TOP + experts_all * 7 - 1) // (experts_all * 7))
    half = replicas // 2
    side = plane // half
    ff_half = FF // 2
    slab = width // replicas
    q_cols = H * HD // group
    kv_cols = KVH * HD // group
    kv_dev = KVH // group
    per_kv = H // KVH

    def over_dp(x, axis):
        return place(
            [x] + [send(x, "dp", m) for m in range(1, replicas)],
            [plane ^ m for m in range(replicas)],
            axis,
            replicas,
        )

    gains = over_dp(jnp.stack([gain_attn, gain_moe]), 1)
    gain_one, gain_two = gains[0], gains[1]
    router_full = over_dp(w_router, 0)
    qkv_slice = jnp.concatenate(
        [
            pick(w_query, head, q_cols, 1),
            pick(w_key, head, kv_cols, 1),
            pick(w_value, head, kv_cols, 1),
        ],
        axis=1,
    )
    qkv = over_dp(qkv_slice, 0)

    def on_grid(x, pairs):
        return lax.ppermute(x, ("dp", "expert"), pairs)

    if replicas == group:
        out_slice = jnp.where(plane == head, w_out, jnp.zeros((), bf16))
        for step in range(1, replicas):
            pairs = [
                (
                    (i % group) * owners + i,
                    ((i % group + step) % replicas) * owners + i,
                )
                for i in range(owners)
            ]
            out_slice = out_slice + on_grid(w_out, pairs)
    else:
        out_slice = pick(lax.all_gather(w_out, "dp", axis=0, tiled=True), head, q_cols, 0)

    def columns(which):
        return jnp.concatenate(
            [
                pick(w_gate_up[:, :, :FF], which, ff_half, 2),
                pick(w_gate_up[:, :, FF:], which, ff_half, 2),
            ],
            axis=2,
        )

    mine = columns(side)
    other = send(columns(1 - side), "dp", half)
    gate_up_w = place(
        [mine, other]
        + [send(mine, "dp", m) for m in range(1, half)]
        + [send(other, "dp", m) for m in range(1, half)],
        [plane, plane ^ half]
        + [plane ^ m for m in range(1, half)]
        + [plane ^ half ^ m for m in range(1, half)],
        1,
        replicas,
    )
    down_w = place(
        [w_down] + [send(w_down, "dp", m) for m in range(1, half)],
        [(plane % half) ^ m for m in range(half)],
        1,
        half,
    )

    both_routes = jnp.stack([routes, send(routes, "dp", half)])
    route_blocks = jnp.stack(gather_blocks(both_routes, owners), axis=1).reshape(
        2 * owners, tok, TOP
    )
    sources = 2 * owners
    routed = jnp.any(
        route_blocks[:, :, :, None] == jnp.arange(experts_all, dtype=jnp.int32), axis=2
    )
    hot = pick(routed.astype(bf16), me, EXP_DEV, 2)
    earlier = (jnp.arange(tok)[:, None] > jnp.arange(tok)[None, :]).astype(bf16)
    rank = mm("tu,sue->set", earlier, hot).astype(jnp.int32)
    hot_t = jnp.transpose(hot, (0, 2, 1)) > 0
    chooses = hot_t[:, :, None, :] & (
        rank[:, :, None, :] == jnp.arange(slots, dtype=jnp.int32)[None, None, :, None]
    )
    select = chooses.astype(bf16)

    valid_float = valid.astype(f32)
    valid_count = jnp.sum(valid_float)
    valid_count = total_over(total_over(jnp.full((8, 128), valid_count), "expert"), "dp")[0, 0]

    inputs = hidden_in.astype(f32)
    normed_f, norm_one_pull = jax.vjp(rms_norm, inputs, gain_one.astype(f32))
    normed = normed_f.astype(bf16)
    order = [head ^ j for j in range(group)]
    seq = place(gather_blocks(normed, group), order, 0, group)
    lin = mm("td,dc->tc", seq, qkv)
    cosine, sine = rope_tables(jnp.arange(length, dtype=f32))
    queries = (
        rotary(lin[:, :q_cols].reshape(length, kv_dev * per_kv, HD), cosine, sine)
        .astype(bf16)
        .reshape(length, kv_dev, per_kv, HD)
    )
    keys = rotary(
        lin[:, q_cols : q_cols + kv_cols].reshape(length, kv_dev, HD), cosine, sine
    ).astype(bf16)
    values = lin[:, q_cols + kv_cols :].reshape(length, kv_dev, HD).astype(bf16)
    context, log_total = attend(queries, keys, values)
    context = context.reshape(length, q_cols)
    branch = mm("tc,cd->td", context, out_slice).astype(bf16)
    mid = inputs + RESIDUAL * scatter_sum([pick(branch, order[j], tok, 0) for j in range(group)])
    moe_f, norm_two_pull = jax.vjp(rms_norm, mid, gain_two.astype(f32))
    moe_input = moe_f.astype(bf16)

    def share(x):
        far = send(x, "dp", half)
        return jnp.stack(gather_blocks(x, owners) + gather_blocks(far, owners))

    def collect(parts):
        far = scatter_sum([parts[owners + j] for j in range(owners)]).astype(bf16)
        near = scatter_sum([parts[j] for j in range(owners)])
        return near + send(far, "dp", half).astype(f32)

    rows = sources * slots
    states = share(moe_input)
    arrived = mm("sect,std->escd", select, states).astype(bf16).reshape(EXP_DEV, rows, width)
    logits = mm("std,de->ste", states, router_full)
    logits = jnp.where(routed, logits, NEG)
    gates = jnp.where(routed, jnp.exp(logits - jax.nn.logsumexp(logits, axis=-1, keepdims=True)), 0.0)
    gates_t = jnp.transpose(pick(gates, me, EXP_DEV, 2), (0, 2, 1))
    row_gate = jnp.sum(jnp.where(chooses, gates_t[:, :, None, :], 0.0), axis=-1)
    row_gate = jnp.transpose(row_gate, (1, 0, 2)).reshape(EXP_DEV, rows, 1)
    gate_up = mm("erd,edf->erf", arrived, gate_up_w)
    gate_part, up_part = gate_up[..., :ff_half], gate_up[..., ff_half:]
    sig = jax.nn.sigmoid(gate_part)
    hidden = gate_part * sig * up_part
    weighted = (row_gate * hidden).astype(bf16)
    produced = mm("erf,efd->erd", weighted, down_w).astype(bf16)
    parts = mm(
        "sect,escd->std", select, produced.reshape(EXP_DEV, sources, slots, width)
    ).astype(bf16)
    final_state = mid + RESIDUAL * collect(parts)
    activations = final_state.astype(bf16)
    mismatch = final_state - teacher.astype(f32)
    squares = jnp.sum(0.5 * valid_float[:, None] * mismatch * mismatch)
    squares = total_over(total_over(jnp.full((8, 128), squares), "expert"), "dp")[0, 0]
    loss_value = squares / (valid_count * width)
    tokens_all = tok * replicas * owners
    grad_final = tokens_all / valid_count * valid_float[:, None] * mismatch

    grad_states = share(grad_final.astype(bf16))
    arrived_grad = (
        mm("sect,std->escd", select, grad_states).astype(bf16).reshape(EXP_DEV, rows, width)
    )
    hidden_pull = mm("erd,efd->erf", arrived_grad, down_w)
    row_gg = RESIDUAL * jnp.sum(hidden * hidden_pull, axis=-1)
    hidden_grad = RESIDUAL * row_gate * hidden_pull
    silu_grad = sig * (1.0 + gate_part * (1.0 - sig))
    lin_grad = jnp.concatenate(
        [hidden_grad * up_part * silu_grad, hidden_grad * gate_part * sig], axis=-1
    ).astype(bf16)
    row_grad = mm("erf,edf->erd", lin_grad, gate_up_w).astype(bf16)
    grad_parts = mm(
        "sect,escd->std", select, row_grad.reshape(EXP_DEV, sources, slots, width)
    ).astype(bf16)
    grad_down = (RESIDUAL * mm("erf,erd->efd", weighted, arrived_grad)).astype(bf16)
    grad_gate_up = mm("erd,erf->edf", arrived, lin_grad).astype(bf16)

    ff_slab = FF // replicas
    low = plane % half
    down_out = pick(grad_down, low, ff_slab, 1).astype(f32)
    for m in range(1, half):
        down_out = down_out + send(pick(grad_down, low ^ m, ff_slab, 1), "dp", m).astype(f32)
    near_cols = pick(grad_gate_up, plane, slab, 1).astype(f32)
    far_cols = pick(grad_gate_up, plane ^ half, slab, 1).astype(f32)
    for m in range(1, half):
        near_cols = near_cols + send(pick(grad_gate_up, plane ^ m, slab, 1), "dp", m).astype(f32)
        far_cols = far_cols + send(
            pick(grad_gate_up, plane ^ half ^ m, slab, 1), "dp", m
        ).astype(f32)
    far_cols = send(far_cols.astype(bf16), "dp", half).astype(f32)
    first = jnp.where(side == 0, near_cols, far_cols)
    last = jnp.where(side == 0, far_cols, near_cols)
    gate_up_out = jnp.concatenate(
        [
            first[:, :, :ff_half],
            last[:, :, :ff_half],
            first[:, :, ff_half:],
            last[:, :, ff_half:],
        ],
        axis=2,
    )

    token_gg = jnp.sum(
        jnp.where(
            chooses,
            jnp.transpose(row_gg.reshape(EXP_DEV, sources, slots), (1, 0, 2))[..., None],
            0.0,
        ),
        axis=2,
    )
    plane_gg = token_gg[:owners] + send(token_gg[owners:], "dp", half)
    gg_blocks = [plane_gg[0]] + [send(plane_gg[j], "expert", j) for j in range(1, owners)]
    grad_gates = jnp.transpose(
        place(gg_blocks, [me ^ j for j in range(owners)], 0, owners), (1, 0)
    )
    own_gates = gates[0]
    grad_logits = (
        own_gates * (grad_gates - jnp.sum(own_gates * grad_gates, axis=-1, keepdims=True))
    ).astype(bf16)
    grad_router_t = mm("td,te->ed", moe_input, grad_logits)
    grad_moe_input = collect(grad_parts) + mm("te,de->td", grad_logits, router_full)
    grad_mid_norm, grad_gain_two = norm_two_pull(grad_moe_input)
    grad_mid = grad_final + grad_mid_norm
    grad_branch = (RESIDUAL * grad_mid).astype(bf16)

    seq_grad = place(gather_blocks(grad_branch, group), order, 0, group)
    grad_out = mm("tc,td->cd", context, seq_grad).astype(bf16)
    grad_context = (
        mm("td,cd->tc", seq_grad, out_slice).astype(bf16).reshape(length, kv_dev, per_kv, HD)
    )
    grad_q, grad_k, grad_v = attend_back(queries, keys, values, log_total, grad_context)
    grad_lin = jnp.concatenate(
        [
            rotary(grad_q.reshape(length, kv_dev * per_kv, HD), cosine, -sine).reshape(
                length, q_cols
            ),
            rotary(grad_k, cosine, -sine).reshape(length, kv_cols),
            grad_v.reshape(length, kv_cols),
        ],
        axis=1,
    ).astype(bf16)
    grad_qkv = mm("td,tc->dc", seq, grad_lin).astype(bf16)
    normed_parts = mm("tc,dc->td", grad_lin, qkv).astype(bf16)
    grad_normed = scatter_sum([pick(normed_parts, order[j], tok, 0) for j in range(group)])
    grad_in_norm, grad_gain_one = norm_one_pull(grad_normed)
    grad_in = grad_mid + grad_in_norm

    def other_sequences(x):
        total = x.astype(f32)
        mask = group
        while mask < owners:
            total = total + send(total.astype(bf16), "expert", mask).astype(f32)
            mask *= 2
        return total

    qkv_sum = pick(grad_qkv, plane, slab, 0).astype(f32)
    for m in range(1, replicas):
        qkv_sum = qkv_sum + send(pick(grad_qkv, plane ^ m, slab, 0), "dp", m).astype(f32)
    qkv_sum = other_sequences(qkv_sum).astype(bf16)
    qkv_blocks = gather_blocks(qkv_sum, group)
    g_query = place([b[:, :q_cols] for b in qkv_blocks], order, 1, group).astype(f32)
    g_key = place([b[:, q_cols : q_cols + kv_cols] for b in qkv_blocks], order, 1, group).astype(f32)
    g_value = place([b[:, q_cols + kv_cols :] for b in qkv_blocks], order, 1, group).astype(f32)

    if replicas == group:
        out_sum = grad_out.astype(f32)
        for step in range(1, replicas):
            pairs = [
                (
                    ((i % group + step) % replicas) * owners + i,
                    (i % group) * owners + i,
                )
                for i in range(owners)
            ]
            out_sum = out_sum + on_grid(grad_out, pairs).astype(f32)
        out_sum = other_sequences(out_sum).astype(bf16)
        g_out = jnp.where(plane == head, out_sum, jnp.zeros((), bf16))
        for m in range(1, group):
            pairs = [
                ((i % group) * owners + i, (i % group) * owners + (i ^ m)) for i in range(owners)
            ]
            g_out = g_out + on_grid(out_sum, pairs)
        g_out = g_out.astype(f32)
    else:
        out_sum = other_sequences(lax.psum(grad_out, "dp")).astype(bf16)
        g_out = pick(
            place(gather_blocks(out_sum, group), order, 0, group), plane, slab, 0
        ).astype(f32)

    def small_sum(x):
        x = x.reshape(x.shape[0], replicas, slab)
        total = jnp.squeeze(pick(x, plane, 1, 1), 1)
        for m in range(1, replicas):
            total = total + send(jnp.squeeze(pick(x, plane ^ m, 1, 1), 1), "dp", m)
        return total_over(total, "expert")

    early = small_sum(jnp.concatenate([grad_router_t, grad_gain_two[None]], axis=0))
    g_router, g_two = jnp.transpose(early[:experts_all]), early[experts_all]
    g_one = small_sum(grad_gain_one[None])[0]
    return (
        activations,
        loss_value,
        grad_in,
        g_one,
        g_two,
        g_query,
        g_key,
        g_value,
        g_out,
        g_router,
        gate_up_out,
        down_out,
    )


def solution(mesh):
    placed = (
        P(("dp", "expert"), None),
        P(("dp", "expert"), None),
        P(("dp", "expert")),
        P(("dp", "expert"), None),
        P("dp"),
        P("dp"),
        P("dp", None),
        P("dp", None),
        P("dp", None),
        P("dp", None),
        P("dp", None),
        P("expert", "dp", None),
        P("expert", "dp", None),
    )
    return jax.shard_map(
        body,
        mesh=mesh,
        in_specs=placed,
        out_specs=(
            P(("dp", "expert"), None),
            P(),
            P(("dp", "expert"), None),
            P("dp"),
            P("dp"),
            P("dp", None),
            P("dp", None),
            P("dp", None),
            P("dp", None),
            P("dp", None),
            P("expert", "dp", None),
            P("expert", "dp", None),
        ),
        check_vma=False,
    )
```

```python
import functools

import jax
import jax.numpy as jnp
from jax import lax
from jax.experimental import pallas as pl
from jax.experimental.pallas import tpu as pltpu
from jax.sharding import PartitionSpec as P

H = 24
KVH = 8
HD = 64
FF = 512
TOP = 8
EXP_DEV = 3
SEQ_MIN = 1024

EPS = 1e-05
RESIDUAL = 0.22
SCORE_SCALE = 1.0 / 64.0
ROPE_BASE = 10000.0
NEG = -1000000000.0

f32 = jnp.float32
bf16 = jnp.bfloat16


def mm(spec, a, b):
    return jnp.einsum(spec, a, b, preferred_element_type=f32)


def rms_norm(states, gain):
    return states * lax.rsqrt(jnp.mean(states * states, axis=-1, keepdims=True) + EPS) * gain


def rope_tables(positions):
    half_dim = HD // 2
    frequencies = ROPE_BASE ** (-(2.0 * jnp.arange(half_dim, dtype=f32)) / HD)
    angles = positions[:, None] * frequencies[None, :]
    return (jnp.cos(angles)[:, None, :], jnp.sin(angles)[:, None, :])


def rotary(heads_in, cosine_table, sine_table):
    half_dim = heads_in.shape[-1] // 2
    first = heads_in[..., :half_dim]
    second = heads_in[..., half_dim:]
    return jnp.concatenate(
        [first * cosine_table - second * sine_table, second * cosine_table + first * sine_table],
        axis=-1,
    )


def send(x, axis, mask):
    count = lax.axis_size(axis)
    return lax.ppermute(x, axis, [(i, i ^ mask) for i in range(count)])


def gather_blocks(x, count):
    blocks = [x]
    for j in range(1, count):
        blocks.append(send(blocks[j - 1], "expert", 1) if j % 2 else send(x, "expert", j))
    return blocks


def scatter_sum(parts):
    total = None
    for j in range(0, len(parts), 2):
        chip = parts[j].astype(f32) + send(parts[j + 1], "expert", 1).astype(f32)
        if j:
            chip = send(chip.astype(bf16), "expert", j).astype(f32)
        total = chip if total is None else total + chip
    return total


def total_over(x, axis):
    mask = 1
    while mask < lax.axis_size(axis):
        x = x + send(x, axis, mask)
        mask *= 2
    return x


def place(blocks, starts, axis, size):
    width = blocks[0].shape[axis]
    shape = list(blocks[0].shape)
    shape[axis] = size * width
    out = jnp.zeros(shape, blocks[0].dtype)
    for block, start in zip(blocks, starts):
        out = lax.dynamic_update_slice_in_dim(out, block, start * width, axis)
    return out


def pick(x, index, width, axis):
    return lax.dynamic_slice_in_dim(x, index * width, width, axis)


def never(x):
    return (x != x).astype(jnp.int32)


def attend(queries, keys, values):
    count = queries.shape[0]
    raw = mm("qhgd,khd->hgqk", queries, keys) * SCORE_SCALE
    causal = jnp.arange(count)[:, None] >= jnp.arange(count)[None, :]
    scores = jnp.where(causal[None, None], raw, NEG)
    top = jnp.max(scores, axis=-1, keepdims=True)
    log_total = top + jnp.log(jnp.sum(jnp.exp(scores - top), axis=-1, keepdims=True))
    probs = jnp.exp(scores - log_total).astype(bf16)
    context = mm("hgqk,khd->qhgd", probs, values).astype(bf16)
    return context, log_total


def attend_back(queries, keys, values, log_total, grad_context):
    count = queries.shape[0]
    raw = mm("qhgd,khd->hgqk", queries, keys) * SCORE_SCALE
    causal = jnp.arange(count)[:, None] >= jnp.arange(count)[None, :]
    probs = jnp.exp(jnp.where(causal[None, None], raw, NEG) - log_total)
    grad_probs = mm("qhgd,khd->hgqk", grad_context, values)
    delta = jnp.sum(probs * grad_probs, axis=-1, keepdims=True)
    grad_scores = (probs * (grad_probs - delta)).astype(bf16)
    grad_queries = mm("hgqk,khd->qhgd", grad_scores, keys) * SCORE_SCALE
    grad_keys = mm("hgqk,qhgd->khd", grad_scores, queries) * SCORE_SCALE
    grad_values = mm("hgqk,qhgd->khd", probs.astype(bf16), grad_context)
    return grad_queries, grad_keys, grad_values


CAP = 112
GATE_COLUMNS = 128
NT = (((1,), (1,)), ((), ()))
TN = (((0,), (0,)), ((), ()))
NN = (((1,), (0,)), ((), ()))


def dg(a, b, dims):
    return lax.dot_general(a, b, dims, preferred_element_type=f32)


def whole(shape):
    return pl.BlockSpec(shape, lambda *_: (0,) * len(shape))


def params(mib):
    return pltpu.CompilerParams(vmem_limit_bytes=mib << 20)


def select_rows(slot_row):
    row = lax.broadcasted_iota(jnp.int32, (CAP, slot_row.shape[1]), 0).astype(f32)
    return row == slot_row


def experts_kernel(me_ref, routes_ref, router_ref, gate_up_ref, down_ref, *refs):
    blocks, refs = refs[:8], refs[8:]
    parts, refs = refs[:8], refs[8:]
    arrived_ref, lin_ref, weighted_ref, slot_ref, gate_ref, sel, made = refs
    step = pl.program_id(0)
    tok, width = blocks[0].shape

    @pl.when(step == 0)
    def _():
        first = me_ref[0] * EXP_DEV
        experts = router_ref.shape[0]
        which = lax.broadcasted_iota(jnp.int32, (experts, tok), 0)
        before = (
            lax.broadcasted_iota(jnp.int32, (tok, tok), 0)
            < lax.broadcasted_iota(jnp.int32, (tok, tok), 1)
        ).astype(bf16)
        for s in range(8):
            logits = dg(router_ref[...], blocks[s][...], NT)
            names = routes_ref[s]
            routed = which == names[0:1, :]
            for k in range(1, TOP):
                routed = routed | (which == names[k : k + 1, :])
            logits = jnp.where(routed, logits, NEG)
            top = jnp.max(logits, axis=0, keepdims=True)
            grown = jnp.where(routed, jnp.exp(logits - top), 0.0)
            gates = grown / jnp.sum(grown, axis=0, keepdims=True)
            hots, picked = [], []
            for i in range(EXP_DEV):
                own = which == first + i
                hots.append(jnp.sum(jnp.where(own & routed, 1.0, 0.0), axis=0, keepdims=True))
                picked.append(jnp.sum(jnp.where(own, gates, 0.0), axis=0, keepdims=True))
            filler = jnp.zeros((8 - EXP_DEV, tok), f32)
            hot = jnp.concatenate(hots + [filler], axis=0)
            rank = dg(hot.astype(bf16), before, NN)
            slot = jnp.where(hot > 0.0, rank, -1.0)
            slot_ref[s] = slot
            gate_ref[s] = jnp.concatenate(picked + [filler], axis=0)
            for i in range(EXP_DEV):
                sel[s, i * CAP : (i + 1) * CAP, :] = select_rows(slot[i : i + 1, :]).astype(bf16)

    at = pl.ds(pl.multiple_of(step * CAP, CAP), CAP)
    for s in range(8):
        arrived_ref[s, 0] = dg(sel[s, at, :], blocks[s][...], NN).astype(bf16)
    lin = dg(arrived_ref[:, 0].reshape(8 * CAP, width), gate_up_ref[0], NN)
    lin_ref[:, 0] = lin.reshape(8, CAP, lin.shape[1])
    half = lin.shape[1] // 2
    gate_part, up_part = lin[:, :half], lin[:, half:]
    hidden = gate_part * jax.nn.sigmoid(gate_part) * up_part
    for s in range(8):
        gate_row = gate_ref[s, pl.ds(step, 1), :]
        row_gate = jnp.sum(
            jnp.where(sel[s, at, :] > 0, gate_row, 0.0), axis=1, keepdims=True
        )
        weighted_ref[s, 0] = (row_gate * hidden[s * CAP : (s + 1) * CAP]).astype(bf16)
    out = dg(weighted_ref[:, 0].reshape(8 * CAP, half), down_ref[0], NN)
    made[:, at, :] = out.reshape(8, CAP, width).astype(bf16)

    @pl.when(step == EXP_DEV - 1)
    def _():
        for s in range(8):
            parts[s][...] = dg(sel[s], made[s], TN).astype(bf16)


def experts_forward(me, routes_t, router_t, blocks, gate_up_w, down_w):
    tok, width = blocks[0].shape
    cols, half = gate_up_w.shape[2], down_w.shape[1]
    by_expert = lambda w: pl.BlockSpec((8, 1, CAP, w), lambda e, *_: (0, e, 0, 0))
    rows = lambda w, t: jax.ShapeDtypeStruct((8, EXP_DEV, CAP, w), t)
    out = pl.pallas_call(
        experts_kernel,
        grid_spec=pltpu.PrefetchScalarGridSpec(
            num_scalar_prefetch=1,
            grid=(EXP_DEV,),
            in_specs=[
                whole(routes_t.shape),
                whole(router_t.shape),
                pl.BlockSpec((1, width, cols), lambda e, *_: (e, 0, 0)),
                pl.BlockSpec((1, half, width), lambda e, *_: (e, 0, 0)),
            ]
            + [whole((tok, width))] * 8,
            out_specs=[whole((tok, width))] * 8
            + [by_expert(width), by_expert(cols), by_expert(half)]
            + [whole((8, 8, tok))] * 2,
            scratch_shapes=[
                pltpu.VMEM((8, EXP_DEV * CAP, tok), bf16),
                pltpu.VMEM((8, EXP_DEV * CAP, width), bf16),
            ],
        ),
        out_shape=[jax.ShapeDtypeStruct((tok, width), bf16)] * 8
        + [rows(width, bf16), rows(cols, f32), rows(half, bf16)]
        + [jax.ShapeDtypeStruct((8, 8, tok), f32)] * 2,
        compiler_params=params(60),
        cost_estimate=pl.CostEstimate(
            flops=11 * 10**9, bytes_accessed=40 * 10**6, transcendentals=10**6
        ),
        name="experts_forward",
    )(me, routes_t, router_t, gate_up_w, down_w, *blocks)
    return list(out[:8]), out[8:]


def experts_back_kernel(me_ref, slot_ref, gate_ref, lin_ref, gate_up_ref, down_ref, *refs):
    blocks, refs = refs[:8], refs[8:]
    parts, refs = refs[:8], refs[8:]
    arrived_ref, lin_grad_ref, sel, made = refs
    step = pl.program_id(0)
    tok, width = blocks[0].shape
    half = down_ref.shape[1]
    at = pl.ds(pl.multiple_of(step * CAP, CAP), CAP)

    for s in range(8):
        sel[s, at, :] = select_rows(slot_ref[s, pl.ds(step, 1), :]).astype(bf16)
        arrived_ref[s, 0] = dg(sel[s, at, :], blocks[s][...], NN).astype(bf16)
    pull = dg(arrived_ref[:, 0].reshape(8 * CAP, width), down_ref[0], NT)
    lin = lin_ref[:, 0].reshape(8 * CAP, 2 * half)
    gate_part, up_part = lin[:, :half], lin[:, half:]
    sig = jax.nn.sigmoid(gate_part)
    act = gate_part * sig
    row_gg = RESIDUAL * jnp.sum(act * up_part * pull, axis=1, keepdims=True)
    slope = sig * (1.0 + gate_part * (1.0 - sig))
    own = me_ref[0] * EXP_DEV + step
    column = lax.broadcasted_iota(jnp.int32, (CAP, made.shape[2] - width), 1)
    for s in range(8):
        mine = slice(s * CAP, (s + 1) * CAP)
        chosen = sel[s, at, :] > 0
        gate_row = gate_ref[s, pl.ds(step, 1), :]
        row_gate = jnp.sum(jnp.where(chosen, gate_row, 0.0), axis=1, keepdims=True)
        made[s, at, width:] = jnp.where(column == own, row_gg[mine], 0.0).astype(bf16)
        hidden_grad = RESIDUAL * row_gate * pull[mine]
        lin_grad_ref[s, 0, :, :half] = (hidden_grad * up_part[mine] * slope[mine]).astype(bf16)
        lin_grad_ref[s, 0, :, half:] = (hidden_grad * act[mine]).astype(bf16)
    out = dg(lin_grad_ref[:, 0].reshape(8 * CAP, 2 * half), gate_up_ref[0], NT)
    made[:, at, :width] = out.reshape(8, CAP, width).astype(bf16)

    @pl.when(step == EXP_DEV - 1)
    def _():
        for s in range(8):
            parts[s][...] = dg(sel[s], made[s], TN).astype(bf16)


def experts_backward(me, slot, gate, lin, blocks, gate_up_w, down_w):
    tok, width = blocks[0].shape
    cols, half = gate_up_w.shape[2], down_w.shape[1]
    wide = width + GATE_COLUMNS
    by_expert = lambda w: pl.BlockSpec((8, 1, CAP, w), lambda e, *_: (0, e, 0, 0))
    rows = lambda w: jax.ShapeDtypeStruct((8, EXP_DEV, CAP, w), bf16)
    out = pl.pallas_call(
        experts_back_kernel,
        grid_spec=pltpu.PrefetchScalarGridSpec(
            num_scalar_prefetch=1,
            grid=(EXP_DEV,),
            in_specs=[
                whole(slot.shape),
                whole(gate.shape),
                by_expert(cols),
                pl.BlockSpec((1, width, cols), lambda e, *_: (e, 0, 0)),
                pl.BlockSpec((1, half, width), lambda e, *_: (e, 0, 0)),
            ]
            + [whole((tok, width))] * 8,
            out_specs=[whole((tok, wide))] * 8 + [by_expert(width), by_expert(cols)],
            scratch_shapes=[
                pltpu.VMEM((8, EXP_DEV * CAP, tok), bf16),
                pltpu.VMEM((8, EXP_DEV * CAP, wide), bf16),
            ],
        ),
        out_shape=[jax.ShapeDtypeStruct((tok, wide), bf16)] * 8 + [rows(width), rows(cols)],
        compiler_params=params(60),
        cost_estimate=pl.CostEstimate(
            flops=11 * 10**9, bytes_accessed=40 * 10**6, transcendentals=10**6
        ),
        name="experts_backward",
    )(me, slot, gate, lin, gate_up_w, down_w, *blocks)
    return list(out[:8]), out[8:]


def expert_weights_kernel(after_ref, *refs):
    chunks = len(refs) // 4
    gate_up_ref, down_ref = refs[-2:]
    gate_up, down = None, None
    for c in range(chunks):
        states, lin_grad, weighted, grads = [
            r[:, 0].reshape(8 * CAP, r.shape[3]) for r in refs[4 * c : 4 * c + 4]
        ]
        one, two = dg(states, lin_grad, TN), dg(weighted, grads, TN)
        gate_up = one if gate_up is None else gate_up + one
        down = two if down is None else down + two
    gate_up_ref[0] = gate_up.astype(bf16)
    down_ref[0] = (RESIDUAL * down).astype(bf16)


def expert_weights(after, chunks):
    width, cols, half = [chunks[0][i].shape[3] for i in range(3)]
    by_expert = lambda w: pl.BlockSpec((8, 1, CAP, w), lambda e, *_: (0, e, 0, 0))
    flat = [x for chunk in chunks for x in chunk]
    return pl.pallas_call(
        expert_weights_kernel,
        grid_spec=pltpu.PrefetchScalarGridSpec(
            num_scalar_prefetch=1,
            grid=(EXP_DEV,),
            in_specs=[by_expert(x.shape[3]) for x in flat],
            out_specs=[
                pl.BlockSpec((1, width, cols), lambda e, *_: (e, 0, 0)),
                pl.BlockSpec((1, half, width), lambda e, *_: (e, 0, 0)),
            ],
        ),
        out_shape=[
            jax.ShapeDtypeStruct((EXP_DEV, width, cols), bf16),
            jax.ShapeDtypeStruct((EXP_DEV, half, width), bf16),
        ],
        compiler_params=params(60),
        cost_estimate=pl.CostEstimate(
            flops=14 * 10**9, bytes_accessed=40 * 10**6, transcendentals=0
        ),
        name="expert_weights",
    )(after, *flat)


MESH = pl.DeviceIdType.MESH


def flip(index, mask):
    return index + mask - 2 * mask * lax.rem(lax.div(index, mask), 2)


def greet(partners):
    barrier = pltpu.get_barrier_semaphore()
    for partner in partners:
        pl.semaphore_signal(barrier, inc=1, device_id=partner, device_id_type=MESH)
    pl.semaphore_wait(barrier, len(partners))


class Wire:
    def __init__(self, send_sem, recv_sem):
        self.send_sem, self.recv_sem, self.copies = send_sem, recv_sem, []

    def start(self, src, dst, partner):
        i = len(self.copies)
        copy = pltpu.make_async_remote_copy(
            src_ref=src,
            dst_ref=dst,
            send_sem=self.send_sem.at[i],
            recv_sem=self.recv_sem.at[i],
            device_id=partner,
            device_id_type=MESH,
        )
        copy.start()
        self.copies.append(copy)
        return copy

    def finish(self):
        for copy in self.copies:
            copy.wait_send()


def comm_call(kernel, name, number, copies, in_specs, out_specs, out_shape, scratch, cost):
    return pl.pallas_call(
        kernel,
        in_specs=in_specs,
        out_specs=out_specs,
        out_shape=out_shape,
        scratch_shapes=list(scratch) + [pltpu.SemaphoreType.DMA((copies,))] * 2,
        compiler_params=pltpu.CompilerParams(
            vmem_limit_bytes=60 << 20, collective_id=number, has_side_effects=True
        ),
        cost_estimate=pl.CostEstimate(flops=cost, bytes_accessed=cost, transcendentals=0),
        name=name,
    )


ANYWHERE = pl.BlockSpec(memory_space=pl.ANY)
ON_CHIP = pl.BlockSpec(memory_space=pltpu.VMEM)


def add_into(rows, out, first, *others, step=32):
    @pl.loop(0, rows // step)
    def _(i):
        at = pl.ds(pl.multiple_of(i * step, step), step)
        total = first[at].astype(f32)
        for other in others:
            total = total + other[at].astype(f32)
        out[at] = total.astype(out.dtype)


def neighbours(half):
    e, z = lax.axis_index("expert"), lax.axis_index("dp")
    across = lax.rem(z + half, lax.axis_size("dp"))
    return [{"expert": flip(e, m)} for m in (1, 2, 4)] + [{"dp": across}]


def exchange_plane(wire, partners, x_ref, near, far):
    core, side_x, side_y, across = partners
    cut = x_ref.shape[0] // 2
    low, high = pl.ds(0, cut), pl.ds(cut, cut)

    def direct(b, at):
        return (
            wire.start(b[0].at[at], b[2].at[at], side_x),
            wire.start(b[0].at[at], b[4].at[at], side_y),
        )

    z_low = wire.start(x_ref.at[low], far[0].at[low], across)
    z_high = wire.start(x_ref.at[high], far[0].at[high], across)
    near_x_low = wire.start(near[0].at[low], near[2].at[low], side_x)
    near_y_high = wire.start(near[0].at[high], near[4].at[high], side_y)
    near_x_high = wire.start(near[0].at[high], near[2].at[high], side_x)
    near_y_low = wire.start(near[0].at[low], near[4].at[low], side_y)
    last = [wire.start(near[0], near[1], core)]
    near_x_low.wait_recv()
    near_diag_low = wire.start(near[2].at[low], near[6].at[low], side_y)
    near_y_high.wait_recv()
    near_diag_high = wire.start(near[4].at[high], near[6].at[high], side_x)
    near_x_high.wait_recv()
    last.append(wire.start(near[2], near[3], core))
    near_y_low.wait_recv()
    last.append(wire.start(near[4], near[5], core))
    z_low.wait_recv()
    far_x_low, far_y_low = direct(far, low)
    near_diag_low.wait_recv()
    near_diag_high.wait_recv()
    last.append(wire.start(near[6], near[7], core))
    z_high.wait_recv()
    far_x_high, far_y_high = direct(far, high)
    last.append(wire.start(far[0], far[1], core))
    far_x_low.wait_recv()
    far_diag_low = wire.start(far[2].at[low], far[6].at[low], side_y)
    far_y_low.wait_recv()
    far_y_high.wait_recv()
    far_diag_high = wire.start(far[4].at[high], far[6].at[high], side_x)
    last.append(wire.start(far[4], far[5], core))
    far_x_high.wait_recv()
    last.append(wire.start(far[2], far[3], core))
    far_diag_low.wait_recv()
    far_diag_high.wait_recv()
    last.append(wire.start(far[6], far[7], core))
    for copy in last:
        copy.wait_recv()


def plane_gather_kernel(half, x_ref, *refs):
    wire = Wire(*refs[15:])
    partners = neighbours(half)
    greet(partners)
    exchange_plane(wire, partners, x_ref, (x_ref,) + refs[:7], refs[7:15])
    wire.finish()


def plane_gather(x, half, number, name):
    block = jax.ShapeDtypeStruct(x.shape, x.dtype)
    out = comm_call(
        functools.partial(plane_gather_kernel, half),
        name,
        number,
        22,
        [ANYWHERE],
        [ANYWHERE] * 15,
        [block] * 15,
        [],
        50 * x.size,
    )(x)
    return [x] + list(out[:7]), list(out[7:])


def plane_scatter_kernel(half, *refs):
    parts = {"near": refs[:8], "far": refs[8:16]}
    out, core_in, sums, diag_in, last_in, z_out, z_in = refs[16:23]
    wire = Wire(*refs[23:])
    core, side_x, side_y, across = partners = neighbours(half)
    rows = out.shape[0] // 2
    cut = rows // 2
    low, high = pl.ds(0, cut), pl.ds(cut, cut)
    greet(partners)
    segments = [(kind, h) for kind in ("far", "near") for h in range(2)]
    from_core, from_diag, from_last, from_z = {}, {}, {}, {}

    def part(s, j):
        kind, h = segments[s]
        return parts[kind][j].at[pl.ds(h * rows, rows)]

    for s in range(4):
        for k in (3, 1, 2, 0):
            from_core[s, k] = wire.start(part(s, 2 * k + 1), core_in.at[s, k], core)

    def chip_sum(s, k):
        from_core[s, k].wait_recv()
        add_into(rows, sums.at[s, k], part(s, 2 * k), core_in.at[s, k])

    def enter(s):
        chip_sum(s, 3)
        from_diag[s, 0] = wire.start(sums.at[s, 3, low], diag_in.at[s, 0], side_x)
        from_diag[s, 1] = wire.start(sums.at[s, 3, high], diag_in.at[s, 1], side_y)
        chip_sum(s, 1)
        from_last[s, 0] = wire.start(sums.at[s, 1, low], last_in.at[s, 0, low], side_x)
        chip_sum(s, 2)
        from_last[s, 1] = wire.start(sums.at[s, 2, high], last_in.at[s, 1, high], side_y)

    def turn(s):
        from_diag[s, 1].wait_recv()
        add_into(cut, sums.at[s, 1, high], sums.at[s, 1, high], diag_in.at[s, 1])
        from_last[s, 2] = wire.start(sums.at[s, 1, high], last_in.at[s, 0, high], side_x)
        from_diag[s, 0].wait_recv()
        add_into(cut, sums.at[s, 2, low], sums.at[s, 2, low], diag_in.at[s, 0])
        from_last[s, 3] = wire.start(sums.at[s, 2, low], last_in.at[s, 1, low], side_y)

    def leave(s):
        kind, h = segments[s]
        from_core[s, 0].wait_recv()
        for i in range(4):
            from_last[s, i].wait_recv()
        target = z_out.at[h] if kind == "far" else out.at[pl.ds(h * rows, rows)]
        add_into(rows, target, part(s, 0), core_in.at[s, 0], last_in.at[s, 0], last_in.at[s, 1])
        if kind == "far":
            from_z[h] = wire.start(z_out.at[h], z_in.at[h], across)

    for step, s in (
        (enter, 0),
        (enter, 1),
        (turn, 0),
        (enter, 2),
        (turn, 1),
        (leave, 0),
        (enter, 3),
        (leave, 1),
        (turn, 2),
        (turn, 3),
        (leave, 2),
        (leave, 3),
    ):
        step(s)
    for h in range(2):
        from_z[h].wait_recv()
        target = out.at[pl.ds(h * rows, rows)]
        add_into(rows, target, target, z_in.at[h])
    wire.finish()


def plane_scatter(near, far, half, number, name):
    rows, width = near[0].shape
    specs = [ON_CHIP, ANYWHERE] * 8
    block = (rows // 2, width)
    return comm_call(
        functools.partial(plane_scatter_kernel, half),
        name,
        number,
        42,
        specs,
        ON_CHIP,
        jax.ShapeDtypeStruct((rows, width), f32),
        [
            pltpu.VMEM((4, 4) + block, bf16),
            pltpu.VMEM((4, 4) + block, bf16),
            pltpu.VMEM((4, 2, rows // 4, width), bf16),
            pltpu.VMEM((4, 2) + block, bf16),
            pltpu.VMEM((2,) + block, bf16),
            pltpu.VMEM((2,) + block, bf16),
        ],
        50 * rows * width,
    )(*near, *far)


def seq_gather_kernel(group, x_ref, out, send_sem, recv_sem):
    wire = Wire(send_sem, recv_sem)
    e = lax.axis_index("expert")
    head = lax.rem(e, group)
    core, side_x = [{"expert": flip(e, m)} for m in (1, 2)]
    rows = x_ref.shape[0]
    cut = rows // 2
    mine = pl.multiple_of(head * rows, rows)
    other = pl.multiple_of(flip(head, 2) * rows, rows)
    greet([core, side_x])
    crossing = [
        wire.start(x_ref.at[pl.ds(h * cut, cut)], out.at[pl.ds(mine + h * cut, cut)], side_x)
        for h in range(2)
    ]
    last = [wire.start(x_ref, out.at[pl.ds(mine, rows)], core)]
    out[pl.ds(mine, rows), :] = x_ref[...]
    for h in range(2):
        crossing[h].wait_recv()
        piece = out.at[pl.ds(other + h * cut, cut)]
        last.append(wire.start(piece, piece, core))
    for copy in last:
        copy.wait_recv()
    wire.finish()


def seq_gather(x, group, number, name):
    rows, width = x.shape
    return comm_call(
        functools.partial(seq_gather_kernel, group),
        name,
        number,
        5,
        [ON_CHIP],
        ON_CHIP,
        jax.ShapeDtypeStruct((group * rows, width), x.dtype),
        [],
        20 * x.size,
    )(x)


def seq_scatter_kernel(group, x_ref, out, core_in, sums, last_in, send_sem, recv_sem):
    wire = Wire(send_sem, recv_sem)
    e = lax.axis_index("expert")
    head = lax.rem(e, group)
    core, side_x = [{"expert": flip(e, m)} for m in (1, 2)]
    rows = out.shape[0]
    cut = rows // 2

    def part(block, h):
        return x_ref.at[pl.ds(pl.multiple_of(block * rows + h * cut, cut), cut)]

    greet([core, side_x])
    crossing = [
        wire.start(part(flip(flip(head, 2), 1), h), core_in.at[1, h], core) for h in range(2)
    ]
    near = [wire.start(part(flip(head, 1), h), core_in.at[0, h], core) for h in range(2)]
    last = []
    for h in range(2):
        crossing[h].wait_recv()
        add_into(cut, sums.at[h], part(flip(head, 2), h), core_in.at[1, h])
        last.append(wire.start(sums.at[h], last_in.at[h], side_x))
    for h in range(2):
        near[h].wait_recv()
        last[h].wait_recv()
        add_into(
            cut, out.at[pl.ds(h * cut, cut)], part(head, h), core_in.at[0, h], last_in.at[h]
        )
    wire.finish()


def seq_scatter(x, group, number, name):
    rows, width = x.shape[0] // group, x.shape[1]
    piece = (rows // 2, width)
    return comm_call(
        functools.partial(seq_scatter_kernel, group),
        name,
        number,
        6,
        [ON_CHIP],
        ON_CHIP,
        jax.ShapeDtypeStruct((rows, width), f32),
        [
            pltpu.VMEM((2, 2) + piece, bf16),
            pltpu.VMEM((2,) + piece, bf16),
            pltpu.VMEM((2,) + piece, bf16),
        ],
        20 * rows * width,
    )(x)


def start_kernel(half, replicas, x_ref, small_ref, *refs):
    near, far, small_out = (x_ref,) + refs[:7], refs[7:15], refs[15]
    wire = Wire(*refs[16:])
    z = lax.axis_index("dp")
    partners = neighbours(half)
    planes = [{"dp": lax.rem(z + k, replicas)} for k in range(1, replicas)]
    greet(partners[:3] + planes)
    spread = [wire.start(small_ref, small_out.at[z], plane) for plane in planes]
    small_out[z] = small_ref[...]
    exchange_plane(wire, partners, x_ref, near, far)
    for copy in spread:
        copy.wait_recv()
    wire.finish()


def start_exchange(x, small, half, replicas):
    block = jax.ShapeDtypeStruct(x.shape, x.dtype)
    out = comm_call(
        functools.partial(start_kernel, half, replicas),
        "start_exchange",
        1,
        22 + replicas - 1,
        [ANYWHERE, ON_CHIP],
        [ANYWHERE] * 15 + [ON_CHIP],
        [block] * 15 + [jax.ShapeDtypeStruct((replicas,) + small.shape, small.dtype)],
        [],
        10**6,
    )(x, small)
    return [x] + list(out[:7]), list(out[7:15]), out[15]


def dense_kernel(replicas, grads, small, out, small_out, *refs):
    y_in, z_out, z_in, small_in, small_sum, turn_in = refs[:6]
    wire = Wire(*refs[6:])
    e, z = lax.axis_index("expert"), lax.axis_index("dp")
    head, row = lax.rem(e, 4), lax.div(e, 4)
    partners = [{"expert": flip(e, m)} for m in (1, 2, 4)]
    core, side_x, side_y = partners
    slab, width = grads.shape[0] // replicas, grads.shape[1]
    cut = slab // 2
    quarter = cut // 2
    order = [2, 1, 3, 0]
    block = {k: lax.rem(z + k, replicas) for k in range(replicas)}
    plane = {k: {"dp": block[k]} for k in range(1, replicas)}
    greet(partners + list(plane.values()))

    def half_of(k, which):
        return grads.at[pl.ds(pl.multiple_of(block[k] * slab + which * cut, cut), cut)]

    small_copies = [wire.start(small.at[block[k]], small_in.at[k - 1], plane[k]) for k in plane]
    from_y = {k: wire.start(half_of(k, 1 - row), y_in.at[k], side_y) for k in order}
    for copy in small_copies:
        copy.wait_recv()
    small_sum[0] = small[z] + small_in[0] + small_in[1] + small_in[2]
    turn = wire.start(small_sum.at[0], turn_in.at[0], core)
    from_z = {}
    for step, k in enumerate(order):
        from_y[k].wait_recv()
        add_into(cut, z_out.at[k], half_of(k, row), y_in.at[k])
        if k:
            from_z[k] = wire.start(z_out.at[k], z_in.at[k - 1], plane[k])
        if step == 0:
            turn.wait_recv()
            small_sum[1] = small_sum[0] + turn_in[0]
            turn = wire.start(small_sum.at[1], turn_in.at[1], side_x)
        if step == 1:
            turn.wait_recv()
            small_sum[2] = small_sum[1] + turn_in[1]
            turn = wire.start(small_sum.at[2], turn_in.at[2], side_y)
    turn.wait_recv()
    small_out[...] = small_sum[2] + turn_in[2]
    for k in from_z:
        from_z[k].wait_recv()

    def place(which_head, which_row, first=0, size=cut):
        start = pl.multiple_of(which_row * cut + first, quarter)
        columns = pl.ds(pl.multiple_of(which_head * width, 128), width)
        return out.at[pl.ds(start, size), columns]

    mine = place(head, row)
    add_into(cut, mine, z_out.at[0], z_in.at[0], z_in.at[1], z_in.at[2])
    other = flip(head, 2)
    pieces = [place(head, row, h * quarter, quarter) for h in range(2)]
    over_x = [wire.start(piece, piece, side_x) for piece in pieces]
    over_y = [wire.start(piece, piece, side_y) for piece in reversed(pieces)]
    last = [wire.start(mine, mine, core)]
    over_x[0].wait_recv()
    piece = place(other, row, 0, quarter)
    diag = [wire.start(piece, piece, side_y)]
    over_y[0].wait_recv()
    piece = place(head, 1 - row, quarter, quarter)
    diag.append(wire.start(piece, piece, side_x))
    over_x[1].wait_recv()
    last.append(wire.start(place(other, row), place(other, row), core))
    over_y[1].wait_recv()
    last.append(wire.start(place(head, 1 - row), place(head, 1 - row), core))
    for copy in diag:
        copy.wait_recv()
    last.append(wire.start(place(other, 1 - row), place(other, 1 - row), core))
    for copy in last:
        copy.wait_recv()
    wire.finish()


def dense_reduce(grads, small, replicas):
    slab, width = grads.shape[0] // replicas, grads.shape[1]
    piece = (slab // 2, width)
    lot = small.shape[1:]
    return comm_call(
        functools.partial(dense_kernel, replicas),
        "dense_reduce",
        2,
        23,
        [ON_CHIP] * 2,
        [ON_CHIP] * 2,
        [jax.ShapeDtypeStruct((slab, 4 * width), bf16), jax.ShapeDtypeStruct(lot, f32)],
        [
            pltpu.VMEM((4,) + piece, bf16),
            pltpu.VMEM((4,) + piece, bf16),
            pltpu.VMEM((3,) + piece, bf16),
            pltpu.VMEM((3,) + lot, f32),
            pltpu.VMEM((3,) + lot, f32),
            pltpu.VMEM((3,) + lot, f32),
        ],
        10**8,
    )(grads, small)


def body(
    hidden_in,
    teacher,
    valid,
    routes,
    gain_attn,
    gain_moe,
    w_query,
    w_key,
    w_value,
    w_out,
    w_router,
    w_gate_up,
    w_down,
):
    tok, width = hidden_in.shape
    owners = lax.axis_size("expert")
    replicas = lax.axis_size("dp")
    me = lax.axis_index("expert")
    plane = lax.axis_index("dp")
    length = min(SEQ_MIN, owners * tok)
    group = length // tok
    head = me % group
    experts_all = EXP_DEV * owners
    slots = 8 * ((tok * TOP + experts_all * 7 - 1) // (experts_all * 7))
    half = replicas // 2
    side = plane // half
    ff_half = FF // 2
    slab = width // replicas
    q_cols = H * HD // group
    kv_cols = KVH * HD // group
    kv_dev = KVH // group
    per_kv = H // KVH

    def over_dp(x, axis):
        if replicas > group:
            return lax.all_gather(x, "dp", axis=axis, tiled=True)
        return place(
            [x] + [send(x, "dp", m) for m in range(1, replicas)],
            [plane ^ m for m in range(replicas)],
            axis,
            replicas,
        )

    routes_t = jnp.transpose(routes)
    count = jnp.full_like(routes_t, jnp.sum(valid))
    small = jnp.concatenate(
        [gain_attn[None], gain_moe[None], jnp.transpose(w_router), jnp.zeros((6, slab), bf16)]
    )
    near_names, far_names, small = start_exchange(
        jnp.concatenate([routes_t, count]), small, half, replicas
    )
    small = jnp.transpose(small, (1, 0, 2)).reshape(small.shape[1], width)
    gain_one, gain_two, router_t = small[0], small[1], small[2 : 2 + experts_all]
    near_routes = jnp.stack([r[:TOP] for r in near_names])
    far_routes = jnp.stack([r[:TOP] for r in far_names])
    me_ref = jnp.reshape(me, (1,)).astype(jnp.int32)
    valid_float = valid.astype(f32)
    valid_count = sum(r[TOP, :1] for r in near_names + far_names)
    mask = 1
    while mask < half:
        valid_count = valid_count + send(valid_count, "dp", mask)
        mask *= 2
    valid_count = valid_count[0].astype(f32)
    hold = (valid_count < 0).astype(jnp.int32)
    qkv_slice = jnp.concatenate(
        [
            pick(w_query, head + hold, q_cols, 1),
            pick(w_key, head + hold, kv_cols, 1),
            pick(w_value, head + hold, kv_cols, 1),
        ],
        axis=1,
    )
    qkv = over_dp(qkv_slice, 0)

    inputs = hidden_in.astype(f32)
    normed_f, norm_one_pull = jax.vjp(rms_norm, inputs, gain_one.astype(f32))
    normed = normed_f.astype(bf16)
    seq = seq_gather(normed, group, 3, "gather_normed")
    hold = never(seq[0, 0])
    w_out, w_down = [jnp.where(hold == 0, w, jnp.zeros((), bf16)) for w in (w_out, w_down)]

    def on_grid(x, pairs):
        return lax.ppermute(x, ("dp", "expert"), pairs)

    if replicas == group:
        out_slice = jnp.where(plane == head, w_out, jnp.zeros((), bf16))
        for step in range(1, replicas):
            pairs = [
                (
                    (i % group) * owners + i,
                    ((i % group + step) % replicas) * owners + i,
                )
                for i in range(owners)
            ]
            out_slice = out_slice + on_grid(w_out, pairs)
    else:
        out_slice = pick(lax.all_gather(w_out, "dp", axis=0, tiled=True), head, q_cols, 0)

    def columns(which):
        return jnp.concatenate(
            [
                pick(w_gate_up[:, :, :FF], which, ff_half, 2),
                pick(w_gate_up[:, :, FF:], which, ff_half, 2),
            ],
            axis=2,
        )

    mine = columns(side + hold)
    if replicas > group:
        gate_up_w = jnp.where(
            side == 0,
            lax.all_gather(columns(0), "dp", axis=1, tiled=True),
            lax.all_gather(columns(1), "dp", axis=1, tiled=True),
        )
        down_w = pick(lax.all_gather(w_down, "dp", axis=1, tiled=True), side, ff_half, 1)
    else:
        other = send(columns(1 - side + hold), "dp", half)
        gate_up_w = place(
            [mine, other]
            + [send(mine, "dp", m) for m in range(1, half)]
            + [send(other, "dp", m) for m in range(1, half)],
            [plane, plane ^ half]
            + [plane ^ m for m in range(1, half)]
            + [plane ^ half ^ m for m in range(1, half)],
            1,
            replicas,
        )
        down_w = place(
            [w_down] + [send(w_down, "dp", m) for m in range(1, half)],
            [(plane % half) ^ m for m in range(half)],
            1,
            half,
        )

    lin = mm("td,dc->tc", seq, qkv)
    cosine, sine = rope_tables(jnp.arange(length, dtype=f32))
    queries = (
        rotary(lin[:, :q_cols].reshape(length, kv_dev * per_kv, HD), cosine, sine)
        .astype(bf16)
        .reshape(length, kv_dev, per_kv, HD)
    )
    keys = rotary(
        lin[:, q_cols : q_cols + kv_cols].reshape(length, kv_dev, HD), cosine, sine
    ).astype(bf16)
    values = lin[:, q_cols + kv_cols :].reshape(length, kv_dev, HD).astype(bf16)
    context, log_total = attend(queries, keys, values)
    context = context.reshape(length, q_cols)
    branch = mm("tc,cd->td", context, out_slice).astype(bf16)
    mid = inputs + RESIDUAL * seq_scatter(branch, group, 4, "scatter_branch")
    moe_f, norm_two_pull = jax.vjp(rms_norm, mid, gain_two.astype(f32))
    moe_input = moe_f.astype(bf16)

    near, far = plane_gather(moe_input, half, 5, "gather_tokens")
    near_parts, near_kept = experts_forward(me_ref, near_routes, router_t, near, gate_up_w, down_w)
    far_parts, far_kept = experts_forward(me_ref, far_routes, router_t, far, gate_up_w, down_w)
    final_state = mid + RESIDUAL * plane_scatter(near_parts, far_parts, half, 6, "scatter_outputs")
    activations = final_state.astype(bf16)
    mismatch = final_state - teacher.astype(f32)
    squares = jnp.sum(0.5 * valid_float[:, None] * mismatch * mismatch)
    tokens_all = tok * replicas * owners
    grad_final = tokens_all / valid_count * valid_float[:, None] * mismatch

    grad_near, grad_far = plane_gather(grad_final.astype(bf16), half, 5, "gather_tokens")

    def back(kept, blocks):
        arrived, lin, weighted, slot, gate = kept
        parts, (grads, lin_grad) = experts_backward(
            me_ref, slot, gate, lin, blocks, gate_up_w, down_w
        )
        return parts, (arrived, lin_grad, weighted, grads)

    near_grads, near_chunk = back(near_kept, grad_near)
    far_grads, far_chunk = back(far_kept, grad_far)
    returned = plane_scatter(near_grads, far_grads, half, 7, "scatter_grads")
    after = jnp.reshape(never(returned[0, 0]), (1,))
    grad_gate_up, grad_down = expert_weights(after, [near_chunk, far_chunk])
    branch_scale = jnp.where(never(grad_down[0, 0, 0]) == 0, RESIDUAL, 0.0)

    ff_slab = FF // replicas
    low = plane % half
    if replicas > group:
        spread = lambda x: lax.psum_scatter(
            x.astype(f32), "dp", scatter_dimension=1, tiled=True
        )
        blank = jnp.zeros_like(grad_down)
        down_out = spread(
            jnp.where(
                side == 0,
                jnp.concatenate([grad_down, blank], axis=1),
                jnp.concatenate([blank, grad_down], axis=1),
            )
        )
        own_side = spread(jnp.where(side == 0, grad_gate_up, jnp.zeros((), bf16)))
        other_side = spread(jnp.where(side == 1, grad_gate_up, jnp.zeros((), bf16)))
        near_cols = jnp.where(side == 0, own_side, other_side)
        far_cols = jnp.where(side == 0, other_side, own_side)
    else:
        down_out = pick(grad_down, low, ff_slab, 1).astype(f32)
        for m in range(1, half):
            down_out = down_out + send(pick(grad_down, low ^ m, ff_slab, 1), "dp", m).astype(f32)
        near_cols = pick(grad_gate_up, plane, slab, 1).astype(f32)
        far_cols = pick(grad_gate_up, plane ^ half, slab, 1).astype(f32)
        for m in range(1, half):
            near_cols = near_cols + send(
                pick(grad_gate_up, plane ^ m, slab, 1), "dp", m
            ).astype(f32)
            far_cols = far_cols + send(
                pick(grad_gate_up, plane ^ half ^ m, slab, 1), "dp", m
            ).astype(f32)
        far_cols = send(far_cols.astype(bf16), "dp", half).astype(f32)
    first = jnp.where(side == 0, near_cols, far_cols)
    last = jnp.where(side == 0, far_cols, near_cols)
    gate_up_out = jnp.concatenate(
        [
            first[:, :, :ff_half],
            last[:, :, :ff_half],
            first[:, :, ff_half:],
            last[:, :, ff_half:],
        ],
        axis=2,
    )

    grad_gates = returned[:, width : width + experts_all]
    own_routed = jnp.any(
        routes[:, :, None] == jnp.arange(experts_all, dtype=jnp.int32), axis=1
    )
    own_logits = jnp.where(own_routed, mm("td,ed->te", moe_input, router_t), NEG)
    own_gates = jnp.where(own_routed, jax.nn.softmax(own_logits, axis=-1), 0.0)
    grad_logits = (
        own_gates * (grad_gates - jnp.sum(own_gates * grad_gates, axis=-1, keepdims=True))
    ).astype(bf16)
    grad_router_t = mm("td,te->ed", moe_input, grad_logits)
    grad_moe_input = returned[:, :width] + mm("te,ed->td", grad_logits, router_t)
    grad_mid_norm, grad_gain_two = norm_two_pull(grad_moe_input)
    grad_mid = grad_final + grad_mid_norm
    grad_branch = (branch_scale * grad_mid).astype(bf16)

    seq_grad = seq_gather(grad_branch, group, 3, "gather_normed")
    grad_out = mm("tc,td->cd", context, seq_grad).astype(bf16)
    grad_context = (
        mm("td,cd->tc", seq_grad, out_slice).astype(bf16).reshape(length, kv_dev, per_kv, HD)
    )
    grad_q, grad_k, grad_v = attend_back(queries, keys, values, log_total, grad_context)
    grad_lin = jnp.concatenate(
        [
            rotary(grad_q.reshape(length, kv_dev * per_kv, HD), cosine, -sine).reshape(
                length, q_cols
            ),
            rotary(grad_k, cosine, -sine).reshape(length, kv_cols),
            grad_v.reshape(length, kv_cols),
        ],
        axis=1,
    ).astype(bf16)
    grad_qkv = mm("td,tc->dc", seq, grad_lin).astype(bf16)
    normed_parts = mm("tc,dc->td", grad_lin, qkv).astype(bf16)
    grad_normed = seq_scatter(normed_parts, group, 4, "scatter_branch")
    grad_in_norm, grad_gain_one = norm_one_pull(grad_normed)
    grad_in = grad_mid + grad_in_norm

    def other_sequences(x):
        total = x.astype(f32)
        mask = group
        while mask < owners:
            total = total + send(total.astype(bf16), "expert", mask).astype(f32)
            mask *= 2
        return total

    lot = jnp.concatenate(
        [
            grad_router_t,
            grad_gain_one[None],
            grad_gain_two[None],
            jnp.full((6, width), squares),
        ]
    )
    if replicas == group:
        lot = jnp.transpose(lot.reshape(32, replicas, slab), (1, 0, 2))
        by_head, lot = dense_reduce(grad_qkv, lot, replicas)
    else:
        lot = lax.psum_scatter(lot, "dp", scatter_dimension=1, tiled=True)
        lot = lax.psum(lot, "expert")
        qkv_sum = lax.psum_scatter(
            grad_qkv.astype(f32), "dp", scatter_dimension=0, tiled=True
        )
        qkv_sum = other_sequences(qkv_sum).astype(bf16)
        by_head = place(
            gather_blocks(qkv_sum, group),
            [head ^ j for j in range(group)],
            1,
            group,
        )
    def of_heads(first, count):
        wide = q_cols + 2 * kv_cols
        return jnp.concatenate(
            [by_head[:, h * wide + first : h * wide + first + count] for h in range(group)], axis=1
        ).astype(f32)

    g_query = of_heads(0, q_cols)
    g_key = of_heads(q_cols, kv_cols)
    g_value = of_heads(q_cols + kv_cols, kv_cols)
    g_router, g_one, g_two = (
        jnp.transpose(lot[:experts_all]),
        lot[experts_all],
        lot[experts_all + 1],
    )
    loss_value = lot[experts_all + 2, 0] / (valid_count * width)

    if replicas == group:
        out_sum = grad_out.astype(f32)
        for step in range(1, replicas):
            pairs = [
                (
                    ((i % group + step) % replicas) * owners + i,
                    (i % group) * owners + i,
                )
                for i in range(owners)
            ]
            out_sum = out_sum + on_grid(grad_out, pairs).astype(f32)
        out_sum = other_sequences(out_sum).astype(bf16)
        g_out = jnp.where(plane == head, out_sum, jnp.zeros((), bf16))
        for m in range(1, group):
            pairs = [
                ((i % group) * owners + i, (i % group) * owners + (i ^ m)) for i in range(owners)
            ]
            g_out = g_out + on_grid(out_sum, pairs)
        g_out = g_out.astype(f32)
    else:
        out_sum = other_sequences(lax.psum(grad_out, "dp")).astype(bf16)
        g_out = pick(
            place(
                gather_blocks(out_sum, group), [head ^ j for j in range(group)], 0, group
            ),
            plane,
            slab,
            0,
        ).astype(f32)

    return (
        activations,
        loss_value,
        grad_in,
        g_one,
        g_two,
        g_query,
        g_key,
        g_value,
        g_out,
        g_router,
        gate_up_out,
        down_out,
    )


def solution(mesh):
    placed = (
        P(("dp", "expert"), None),
        P(("dp", "expert"), None),
        P(("dp", "expert")),
        P(("dp", "expert"), None),
        P("dp"),
        P("dp"),
        P("dp", None),
        P("dp", None),
        P("dp", None),
        P("dp", None),
        P("dp", None),
        P("expert", "dp", None),
        P("expert", "dp", None),
    )
    return jax.shard_map(
        body,
        mesh=mesh,
        in_specs=placed,
        out_specs=(
            P(("dp", "expert"), None),
            P(),
            P(("dp", "expert"), None),
            P("dp"),
            P("dp"),
            P("dp", None),
            P("dp", None),
            P("dp", None),
            P("dp", None),
            P("dp", None),
            P("expert", "dp", None),
            P("expert", "dp", None),
        ),
        check_vma=False,
    )
```

```python
import functools

import jax
import jax.numpy as jnp
from jax import lax
from jax.experimental import pallas as pl
from jax.experimental.pallas import tpu as pltpu
from jax.sharding import PartitionSpec as P

H = 24
KVH = 8
HD = 64
FF = 512
TOP = 8
EXP_DEV = 3
SEQ_MIN = 1024

EPS = 1e-05
RESIDUAL = 0.22
SCORE_SCALE = 1.0 / 64.0
ROPE_BASE = 10000.0
NEG = -1000000000.0

f32 = jnp.float32
bf16 = jnp.bfloat16


def mm(spec, a, b):
    return jnp.einsum(spec, a, b, preferred_element_type=f32)


def rms_norm(states, gain):
    return states * lax.rsqrt(jnp.mean(states * states, axis=-1, keepdims=True) + EPS) * gain


def rope_tables(positions):
    half_dim = HD // 2
    frequencies = ROPE_BASE ** (-(2.0 * jnp.arange(half_dim, dtype=f32)) / HD)
    angles = positions[:, None] * frequencies[None, :]
    return (jnp.cos(angles)[:, None, :], jnp.sin(angles)[:, None, :])


def rotary(heads_in, cosine_table, sine_table):
    half_dim = heads_in.shape[-1] // 2
    first = heads_in[..., :half_dim]
    second = heads_in[..., half_dim:]
    return jnp.concatenate(
        [first * cosine_table - second * sine_table, second * cosine_table + first * sine_table],
        axis=-1,
    )


def send(x, axis, mask):
    count = lax.axis_size(axis)
    return lax.ppermute(x, axis, [(i, i ^ mask) for i in range(count)])


def gather_blocks(x, count):
    blocks = [x]
    for j in range(1, count):
        blocks.append(send(blocks[j - 1], "expert", 1) if j % 2 else send(x, "expert", j))
    return blocks


def scatter_sum(parts):
    total = None
    for j in range(0, len(parts), 2):
        chip = parts[j].astype(f32) + send(parts[j + 1], "expert", 1).astype(f32)
        if j:
            chip = send(chip.astype(bf16), "expert", j).astype(f32)
        total = chip if total is None else total + chip
    return total


def total_over(x, axis):
    mask = 1
    while mask < lax.axis_size(axis):
        x = x + send(x, axis, mask)
        mask *= 2
    return x


def place(blocks, starts, axis, size):
    width = blocks[0].shape[axis]
    shape = list(blocks[0].shape)
    shape[axis] = size * width
    out = jnp.zeros(shape, blocks[0].dtype)
    for block, start in zip(blocks, starts):
        out = lax.dynamic_update_slice_in_dim(out, block, start * width, axis)
    return out


def pick(x, index, width, axis):
    return lax.dynamic_slice_in_dim(x, index * width, width, axis)


def never(x):
    return (x != x).astype(jnp.int32)


def attend(queries, keys, values):
    count = queries.shape[0]
    raw = mm("qhgd,khd->hgqk", queries, keys) * SCORE_SCALE
    causal = jnp.arange(count)[:, None] >= jnp.arange(count)[None, :]
    scores = jnp.where(causal[None, None], raw, NEG)
    top = jnp.max(scores, axis=-1, keepdims=True)
    log_total = top + jnp.log(jnp.sum(jnp.exp(scores - top), axis=-1, keepdims=True))
    probs = jnp.exp(scores - log_total).astype(bf16)
    context = mm("hgqk,khd->qhgd", probs, values).astype(bf16)
    return context, log_total


def attend_back(queries, keys, values, log_total, grad_context):
    count = queries.shape[0]
    raw = mm("qhgd,khd->hgqk", queries, keys) * SCORE_SCALE
    causal = jnp.arange(count)[:, None] >= jnp.arange(count)[None, :]
    probs = jnp.exp(jnp.where(causal[None, None], raw, NEG) - log_total)
    grad_probs = mm("qhgd,khd->hgqk", grad_context, values)
    delta = jnp.sum(probs * grad_probs, axis=-1, keepdims=True)
    grad_scores = (probs * (grad_probs - delta)).astype(bf16)
    grad_queries = mm("hgqk,khd->qhgd", grad_scores, keys) * SCORE_SCALE
    grad_keys = mm("hgqk,qhgd->khd", grad_scores, queries) * SCORE_SCALE
    grad_values = mm("hgqk,qhgd->khd", probs.astype(bf16), grad_context)
    return grad_queries, grad_keys, grad_values


CAP = 112
GATE_COLUMNS = 128
NT = (((1,), (1,)), ((), ()))
TN = (((0,), (0,)), ((), ()))
NN = (((1,), (0,)), ((), ()))


def dg(a, b, dims):
    return lax.dot_general(a, b, dims, preferred_element_type=f32)


def whole(shape):
    return pl.BlockSpec(shape, lambda *_: (0,) * len(shape))


def params(mib):
    return pltpu.CompilerParams(vmem_limit_bytes=mib << 20)


def select_rows(slot_row):
    row = lax.broadcasted_iota(jnp.int32, (CAP, slot_row.shape[1]), 0).astype(f32)
    return row == slot_row


def experts_kernel(me_ref, router_ref, gate_up_ref, down_ref, *refs):
    blocks, routes, refs = refs[:8], refs[8:16], refs[16:]
    parts, refs = refs[:8], refs[8:]
    arrived_ref, lin_ref, weighted_ref, slot_ref, gate_ref, count_ref, sel, made = refs
    step = pl.program_id(0)
    tok, width = blocks[0].shape

    @pl.when(step == 0)
    def _():
        first = me_ref[0] * EXP_DEV
        experts = router_ref.shape[0]
        which = lax.broadcasted_iota(jnp.int32, (experts, tok), 0)
        before = (
            lax.broadcasted_iota(jnp.int32, (tok, tok), 0)
            < lax.broadcasted_iota(jnp.int32, (tok, tok), 1)
        ).astype(bf16)
        count = jnp.zeros(count_ref.shape, jnp.int32)
        for s in range(8):
            logits = dg(router_ref[...], blocks[s][...], NT)
            names = routes[s][...]
            count = count + names[TOP:]
            routed = which == names[0:1, :]
            for k in range(1, TOP):
                routed = routed | (which == names[k : k + 1, :])
            logits = jnp.where(routed, logits, NEG)
            top = jnp.max(logits, axis=0, keepdims=True)
            grown = jnp.where(routed, jnp.exp(logits - top), 0.0)
            gates = grown / jnp.sum(grown, axis=0, keepdims=True)
            hots, picked = [], []
            for i in range(EXP_DEV):
                own = which == first + i
                hots.append(jnp.sum(jnp.where(own & routed, 1.0, 0.0), axis=0, keepdims=True))
                picked.append(jnp.sum(jnp.where(own, gates, 0.0), axis=0, keepdims=True))
            filler = jnp.zeros((8 - EXP_DEV, tok), f32)
            hot = jnp.concatenate(hots + [filler], axis=0)
            rank = dg(hot.astype(bf16), before, NN)
            slot = jnp.where(hot > 0.0, rank, -1.0)
            slot_ref[s] = slot
            gate_ref[s] = jnp.concatenate(picked + [filler], axis=0)
            for i in range(EXP_DEV):
                sel[s, i * CAP : (i + 1) * CAP, :] = select_rows(slot[i : i + 1, :]).astype(bf16)
        count_ref[...] = count

    at = pl.ds(pl.multiple_of(step * CAP, CAP), CAP)
    for s in range(8):
        arrived_ref[s, 0] = dg(sel[s, at, :], blocks[s][...], NN).astype(bf16)
    lin = dg(arrived_ref[:, 0].reshape(8 * CAP, width), gate_up_ref[0], NN)
    lin_ref[:, 0] = lin.reshape(8, CAP, lin.shape[1])
    half = lin.shape[1] // 2
    gate_part, up_part = lin[:, :half], lin[:, half:]
    hidden = gate_part * jax.nn.sigmoid(gate_part) * up_part
    for s in range(8):
        gate_row = gate_ref[s, pl.ds(step, 1), :]
        row_gate = jnp.sum(
            jnp.where(sel[s, at, :] > 0, gate_row, 0.0), axis=1, keepdims=True
        )
        weighted_ref[s, 0] = (row_gate * hidden[s * CAP : (s + 1) * CAP]).astype(bf16)
    out = dg(weighted_ref[:, 0].reshape(8 * CAP, half), down_ref[0], NN)
    made[:, at, :] = out.reshape(8, CAP, width).astype(bf16)

    @pl.when(step == EXP_DEV - 1)
    def _():
        for s in range(8):
            parts[s][...] = dg(sel[s], made[s], TN).astype(bf16)


def experts_forward(me, routes, router_t, blocks, gate_up_w, down_w):
    tok, width = blocks[0].shape
    cols, half = gate_up_w.shape[2], down_w.shape[1]
    by_expert = lambda w: pl.BlockSpec((8, 1, CAP, w), lambda e, *_: (0, e, 0, 0))
    rows = lambda w, t: jax.ShapeDtypeStruct((8, EXP_DEV, CAP, w), t)
    out = pl.pallas_call(
        experts_kernel,
        grid_spec=pltpu.PrefetchScalarGridSpec(
            num_scalar_prefetch=1,
            grid=(EXP_DEV,),
            in_specs=[
                whole(router_t.shape),
                pl.BlockSpec((1, width, cols), lambda e, *_: (e, 0, 0)),
                pl.BlockSpec((1, half, width), lambda e, *_: (e, 0, 0)),
            ]
            + [whole((tok, width))] * 8
            + [whole(routes[0].shape)] * 8,
            out_specs=[whole((tok, width))] * 8
            + [by_expert(width), by_expert(cols), by_expert(half)]
            + [whole((8, 8, tok))] * 2
            + [whole((8, tok))],
            scratch_shapes=[
                pltpu.VMEM((8, EXP_DEV * CAP, tok), bf16),
                pltpu.VMEM((8, EXP_DEV * CAP, width), bf16),
            ],
        ),
        out_shape=[jax.ShapeDtypeStruct((tok, width), bf16)] * 8
        + [rows(width, bf16), rows(cols, f32), rows(half, bf16)]
        + [jax.ShapeDtypeStruct((8, 8, tok), f32)] * 2
        + [jax.ShapeDtypeStruct((8, tok), jnp.int32)],
        compiler_params=params(60),
        cost_estimate=pl.CostEstimate(
            flops=11 * 10**9, bytes_accessed=40 * 10**6, transcendentals=10**6
        ),
        name="experts_forward",
    )(me, router_t, gate_up_w, down_w, *blocks, *routes)
    return list(out[:8]), out[8:13], out[13]


def experts_back_kernel(me_ref, slot_ref, gate_ref, lin_ref, gate_up_ref, down_ref, *refs):
    blocks, refs = refs[:8], refs[8:]
    parts, refs = refs[:8], refs[8:]
    arrived_ref, lin_grad_ref, sel, made = refs
    step = pl.program_id(0)
    tok, width = blocks[0].shape
    half = down_ref.shape[1]
    at = pl.ds(pl.multiple_of(step * CAP, CAP), CAP)

    for s in range(8):
        sel[s, at, :] = select_rows(slot_ref[s, pl.ds(step, 1), :]).astype(bf16)
        arrived_ref[s, 0] = dg(sel[s, at, :], blocks[s][...], NN).astype(bf16)
    pull = dg(arrived_ref[:, 0].reshape(8 * CAP, width), down_ref[0], NT)
    lin = lin_ref[:, 0].reshape(8 * CAP, 2 * half)
    gate_part, up_part = lin[:, :half], lin[:, half:]
    sig = jax.nn.sigmoid(gate_part)
    act = gate_part * sig
    row_gg = RESIDUAL * jnp.sum(act * up_part * pull, axis=1, keepdims=True)
    slope = sig * (1.0 + gate_part * (1.0 - sig))
    own = me_ref[0] * EXP_DEV + step
    column = lax.broadcasted_iota(jnp.int32, (CAP, made.shape[2] - width), 1)
    for s in range(8):
        mine = slice(s * CAP, (s + 1) * CAP)
        chosen = sel[s, at, :] > 0
        gate_row = gate_ref[s, pl.ds(step, 1), :]
        row_gate = jnp.sum(jnp.where(chosen, gate_row, 0.0), axis=1, keepdims=True)
        made[s, at, width:] = jnp.where(column == own, row_gg[mine], 0.0).astype(bf16)
        hidden_grad = RESIDUAL * row_gate * pull[mine]
        lin_grad_ref[s, 0, :, :half] = (hidden_grad * up_part[mine] * slope[mine]).astype(bf16)
        lin_grad_ref[s, 0, :, half:] = (hidden_grad * act[mine]).astype(bf16)
    out = dg(lin_grad_ref[:, 0].reshape(8 * CAP, 2 * half), gate_up_ref[0], NT)
    made[:, at, :width] = out.reshape(8, CAP, width).astype(bf16)

    @pl.when(step == EXP_DEV - 1)
    def _():
        for s in range(8):
            parts[s][...] = dg(sel[s], made[s], TN).astype(bf16)


def experts_backward(me, slot, gate, lin, blocks, gate_up_w, down_w):
    tok, width = blocks[0].shape
    cols, half = gate_up_w.shape[2], down_w.shape[1]
    wide = width + GATE_COLUMNS
    by_expert = lambda w: pl.BlockSpec((8, 1, CAP, w), lambda e, *_: (0, e, 0, 0))
    rows = lambda w: jax.ShapeDtypeStruct((8, EXP_DEV, CAP, w), bf16)
    out = pl.pallas_call(
        experts_back_kernel,
        grid_spec=pltpu.PrefetchScalarGridSpec(
            num_scalar_prefetch=1,
            grid=(EXP_DEV,),
            in_specs=[
                whole(slot.shape),
                whole(gate.shape),
                by_expert(cols),
                pl.BlockSpec((1, width, cols), lambda e, *_: (e, 0, 0)),
                pl.BlockSpec((1, half, width), lambda e, *_: (e, 0, 0)),
            ]
            + [whole((tok, width))] * 8,
            out_specs=[whole((tok, wide))] * 8 + [by_expert(width), by_expert(cols)],
            scratch_shapes=[
                pltpu.VMEM((8, EXP_DEV * CAP, tok), bf16),
                pltpu.VMEM((8, EXP_DEV * CAP, wide), bf16),
            ],
        ),
        out_shape=[jax.ShapeDtypeStruct((tok, wide), bf16)] * 8 + [rows(width), rows(cols)],
        compiler_params=params(60),
        cost_estimate=pl.CostEstimate(
            flops=11 * 10**9, bytes_accessed=40 * 10**6, transcendentals=10**6
        ),
        name="experts_backward",
    )(me, slot, gate, lin, gate_up_w, down_w, *blocks)
    return list(out[:8]), out[8:]


def expert_weights_kernel(after_ref, *refs):
    chunks = len(refs) // 4
    gate_up_ref, down_ref = refs[-2:]
    gate_up, down = None, None
    for c in range(chunks):
        states, lin_grad, weighted, grads = [
            r[:, 0].reshape(8 * CAP, r.shape[3]) for r in refs[4 * c : 4 * c + 4]
        ]
        one, two = dg(states, lin_grad, TN), dg(weighted, grads, TN)
        gate_up = one if gate_up is None else gate_up + one
        down = two if down is None else down + two
    gate_up_ref[0] = gate_up.astype(bf16)
    down_ref[0] = (RESIDUAL * down).astype(bf16)


def expert_weights(after, chunks):
    width, cols, half = [chunks[0][i].shape[3] for i in range(3)]
    by_expert = lambda w: pl.BlockSpec((8, 1, CAP, w), lambda e, *_: (0, e, 0, 0))
    flat = [x for chunk in chunks for x in chunk]
    return pl.pallas_call(
        expert_weights_kernel,
        grid_spec=pltpu.PrefetchScalarGridSpec(
            num_scalar_prefetch=1,
            grid=(EXP_DEV,),
            in_specs=[by_expert(x.shape[3]) for x in flat],
            out_specs=[
                pl.BlockSpec((1, width, cols), lambda e, *_: (e, 0, 0)),
                pl.BlockSpec((1, half, width), lambda e, *_: (e, 0, 0)),
            ],
        ),
        out_shape=[
            jax.ShapeDtypeStruct((EXP_DEV, width, cols), bf16),
            jax.ShapeDtypeStruct((EXP_DEV, half, width), bf16),
        ],
        compiler_params=params(60),
        cost_estimate=pl.CostEstimate(
            flops=14 * 10**9, bytes_accessed=40 * 10**6, transcendentals=0
        ),
        name="expert_weights",
    )(after, *flat)


MESH = pl.DeviceIdType.MESH


def flip(index, mask):
    return index + mask - 2 * mask * lax.rem(lax.div(index, mask), 2)


def greet(partners):
    barrier = pltpu.get_barrier_semaphore()
    for partner in partners:
        pl.semaphore_signal(barrier, inc=1, device_id=partner, device_id_type=MESH)
    pl.semaphore_wait(barrier, len(partners))


class Wire:
    def __init__(self, send_sem, recv_sem):
        self.send_sem, self.recv_sem, self.copies = send_sem, recv_sem, []

    def start(self, src, dst, partner):
        i = len(self.copies)
        copy = pltpu.make_async_remote_copy(
            src_ref=src,
            dst_ref=dst,
            send_sem=self.send_sem.at[i],
            recv_sem=self.recv_sem.at[i],
            device_id=partner,
            device_id_type=MESH,
        )
        copy.start()
        self.copies.append(copy)
        return copy

    def finish(self):
        for copy in self.copies:
            copy.wait_send()


def comm_call(
    kernel, name, number, copies, in_specs, out_specs, out_shape, scratch, cost, aliases={}
):
    return pl.pallas_call(
        kernel,
        in_specs=in_specs,
        out_specs=out_specs,
        out_shape=out_shape,
        scratch_shapes=list(scratch) + [pltpu.SemaphoreType.DMA((copies,))] * 2,
        compiler_params=pltpu.CompilerParams(
            vmem_limit_bytes=60 << 20, collective_id=number, has_side_effects=True
        ),
        cost_estimate=pl.CostEstimate(flops=cost, bytes_accessed=cost, transcendentals=0),
        input_output_aliases=aliases,
        name=name,
    )


ANYWHERE = pl.BlockSpec(memory_space=pl.ANY)
ON_CHIP = pl.BlockSpec(memory_space=pltpu.VMEM)


def add_into(rows, out, first, *others, step=32):
    @pl.loop(0, rows // step)
    def _(i):
        at = pl.ds(pl.multiple_of(i * step, step), step)
        total = first[at].astype(f32)
        for other in others:
            total = total + other[at].astype(f32)
        out[at] = total.astype(out.dtype)


def plane_places():
    z = lax.axis_index("dp")
    return z, flip(z, 1), lax.rem(z + 2, 4), lax.div(z, 2), lax.rem(z, 2)


def stripe(index, size):
    return pl.ds(pl.multiple_of(index * size, size), size)


class WeightsIn:
    def __init__(self, wire, experts, w_gate_up, w_down, gate_up, down, stage, stage_down, sems):
        z, beside, opposite, side, low = plane_places()
        slab, part = w_gate_up.shape[1], gate_up.shape[2] // 2
        rows = w_down.shape[1]
        self.wire, self.gate_up, self.slab, self.opposite = wire, gate_up, slab, opposite
        self.beside = {"dp": beside}
        self.crossing, self.arriving, self.stores = [], [], []

        def columns(i, which, p):
            return w_gate_up.at[i, :, stripe(2 * p + which, part)]

        def spot(i, p):
            return gate_up.at[i, stripe(z, slab), pl.ds(p * part, part)]

        self.loads = loads = []
        for n, i in enumerate(experts):
            for p in range(2):
                loads.append(
                    pltpu.make_async_copy(
                        columns(i, side, p),
                        stage.at[n, :, pl.ds(p * part, part)],
                        sems.at[n, p],
                    )
                )
            loads.append(pltpu.make_async_copy(w_down.at[i], stage_down.at[n], sems.at[n, 2]))
            for load in loads[-3:]:
                load.start()
            self.crossing.append(
                (
                    i,
                    [
                        wire.start(columns(i, 1 - side, p), spot(i, p), {"dp": opposite})
                        for p in range(2)
                    ],
                )
            )
            for p in range(2):
                self.arriving.append(wire.start(columns(i, side, p), spot(i, p), self.beside))
            here = down.at[i, stripe(low, rows)]
            self.arriving.append(wire.start(w_down.at[i], here, self.beside))
            self.stores.append(
                pltpu.make_async_copy(
                    stage.at[n], gate_up.at[i, stripe(z, slab)], sems.at[n, 3]
                )
            )
            self.stores.append(pltpu.make_async_copy(stage_down.at[n], here, sems.at[n, 4]))

    def finish(self):
        for load in self.loads:
            load.wait()
        for store in self.stores:
            store.start()
        for i, copies in self.crossing:
            for copy in copies:
                copy.wait_recv()
            piece = self.gate_up.at[i, stripe(self.opposite, self.slab)]
            self.arriving.append(self.wire.start(piece, piece, self.beside))
        for copy in self.arriving:
            copy.wait_recv()
        for store in self.stores:
            store.wait()


def weights_scratch(count, slab, columns, rows, width):
    return [
        pltpu.VMEM((count, slab, columns), bf16),
        pltpu.VMEM((count, rows, width), bf16),
        pltpu.SemaphoreType.DMA((count, 5)),
    ]


class GradsOut:
    def __init__(self, wire, i, grad_gate_up, grad_down, out, out_down, got, own, downs, sems):
        z, beside, opposite, side, low = plane_places()
        slab, rows = out.shape[0], out_down.shape[0]
        self.wire, self.side, self.across = wire, side, {"dp": opposite}
        self.out, self.out_down, self.got, self.own, self.downs = out, out_down, got, own, downs

        def slab_of(plane):
            return grad_gate_up.at[i, stripe(plane, slab)]

        def rows_of(which):
            return grad_down.at[i, stripe(which, rows)]

        to = {"dp": beside}
        self.loads = [
            pltpu.make_async_copy(slab_of(opposite), own.at[0], sems.at[0]),
            pltpu.make_async_copy(slab_of(z), own.at[1], sems.at[1]),
            pltpu.make_async_copy(rows_of(low), downs.at[0], sems.at[2]),
        ]
        for load in self.loads:
            load.start()
        self.copies = [
            wire.start(slab_of(flip(opposite, 1)), got.at[0], to),
            wire.start(slab_of(beside), got.at[1], to),
            wire.start(rows_of(1 - low), downs.at[1], to),
        ]

    def cross(self):
        self.loads[0].wait()
        self.copies[0].wait_recv()
        slab = self.out.shape[0]
        add_into(slab, self.own.at[2], self.own.at[0], self.got.at[0])
        self.copies.append(self.wire.start(self.own.at[2], self.got.at[2], self.across))

    def finish(self):
        part = self.out.shape[1] // 4
        slab = self.out.shape[0]
        self.loads[1].wait()
        self.copies[1].wait_recv()
        self.copies[3].wait_recv()
        out, got, own, side = self.out, self.got, self.own, self.side

        @pl.loop(0, slab // 32)
        def _(r):
            at = pl.ds(pl.multiple_of(r * 32, 32), 32)
            for p in range(2):
                lanes = pl.ds(p * part, part)
                total = own[1, at, lanes].astype(f32) + got[1, at, lanes].astype(f32)
                out[at, stripe(2 * p + side, part)] = total.astype(bf16)
                out[at, stripe(2 * p + 1 - side, part)] = got[2, at, lanes]

        self.loads[2].wait()
        self.copies[2].wait_recv()
        add_into(self.out_down.shape[0], self.out_down, self.downs.at[0], self.downs.at[1])


def grads_scratch(slab, columns, rows, width):
    return [
        pltpu.VMEM((3, slab, columns), bf16),
        pltpu.VMEM((3, slab, columns), bf16),
        pltpu.VMEM((2, rows, width), bf16),
        pltpu.SemaphoreType.DMA((3,)),
    ]


def grads_shapes(grad_gate_up, grad_down):
    slab, columns = grad_gate_up.shape[1] // 4, grad_gate_up.shape[2]
    rows, width = grad_down.shape[1] // 2, grad_down.shape[2]
    return (
        [jax.ShapeDtypeStruct((slab, 2 * columns), bf16), jax.ShapeDtypeStruct((rows, width), bf16)],
        grads_scratch(slab, columns, rows, width),
    )


def neighbours(half):
    e, z = lax.axis_index("expert"), lax.axis_index("dp")
    across = lax.rem(z + half, lax.axis_size("dp"))
    return [{"expert": flip(e, m)} for m in (1, 2, 4)] + [{"dp": across}]


class Several:
    def __init__(self, copies):
        self.copies = copies

    def wait_recv(self):
        for copy in self.copies:
            copy.wait_recv()


def exchange_plane(wire, partners, near, far, begin=None):
    core, side_x, side_y, across = partners

    def cut(ref, h):
        rows = ref.shape[0] // 2
        return ref.at[pl.ds(h * rows, rows)]

    def start(src, dst, to, h=None):
        if h is not None:
            src, dst = [[cut(ref, h) for ref in refs] for refs in (src, dst)]
        return Several([wire.start(x, y, to) for x, y in zip(src, dst)])

    z_low = start(near[0], far[0], across, 0)
    z_high = start(near[0], far[0], across, 1)
    near_x_low = start(near[0], near[2], side_x, 0)
    near_y_high = start(near[0], near[4], side_y, 1)
    near_x_high = start(near[0], near[2], side_x, 1)
    near_y_low = start(near[0], near[4], side_y, 0)
    last = [start(near[0], near[1], core)]
    cargo = begin() if begin else None
    near_x_low.wait_recv()
    near_diag_low = start(near[2], near[6], side_y, 0)
    near_y_high.wait_recv()
    near_diag_high = start(near[4], near[6], side_x, 1)
    near_x_high.wait_recv()
    last.append(start(near[2], near[3], core))
    near_y_low.wait_recv()
    last.append(start(near[4], near[5], core))
    z_low.wait_recv()
    far_x_low = start(far[0], far[2], side_x, 0)
    far_y_low = start(far[0], far[4], side_y, 0)
    near_diag_low.wait_recv()
    near_diag_high.wait_recv()
    last.append(start(near[6], near[7], core))
    z_high.wait_recv()
    far_x_high = start(far[0], far[2], side_x, 1)
    far_y_high = start(far[0], far[4], side_y, 1)
    last.append(start(far[0], far[1], core))
    far_x_low.wait_recv()
    far_diag_low = start(far[2], far[6], side_y, 0)
    far_y_low.wait_recv()
    far_y_high.wait_recv()
    far_diag_high = start(far[4], far[6], side_x, 1)
    last.append(start(far[4], far[5], core))
    far_x_high.wait_recv()
    last.append(start(far[2], far[3], core))
    far_diag_low.wait_recv()
    far_diag_high.wait_recv()
    last.append(start(far[6], far[7], core))
    for copy in last:
        copy.wait_recv()
    if cargo:
        cargo.finish()


def plane_gather_kernel(half, experts, count, *refs):
    inputs, refs = refs[:count], refs[count:]
    if experts:
        (w_gate_up, w_down), refs = refs[:2], refs[4:]
    outs, refs = refs[: 15 * count], refs[15 * count :]
    near = [list(inputs)] + [list(outs[j * count : (j + 1) * count]) for j in range(7)]
    far = [list(outs[j * count : (j + 1) * count]) for j in range(7, 15)]
    wire = Wire(*refs[-2:])
    partners = neighbours(half)
    begin = None
    if experts:
        greet(partners + [{"dp": plane_places()[1]}])
        begin = lambda: WeightsIn(wire, experts, w_gate_up, w_down, *refs[:5])
    else:
        greet(partners)
    exchange_plane(wire, partners, near, far, begin)
    wire.finish()


def plane_gather(inputs, half, number, name, experts=(), weights=(), filled=()):
    count, size = len(inputs), inputs[0].size
    blocks = [jax.ShapeDtypeStruct(x.shape, x.dtype) for x in inputs]
    scratch, aliases = [], {}
    if experts:
        (w_gate_up, w_down), (gate_up, down) = weights, filled
        scratch = weights_scratch(
            len(experts), w_gate_up.shape[1], gate_up.shape[2], w_down.shape[1], down.shape[2]
        )
        aliases = {count + 2: 15 * count, count + 3: 15 * count + 1}
    out = comm_call(
        functools.partial(plane_gather_kernel, half, experts, count),
        name,
        number,
        22 * count + 6 * len(experts),
        [ANYWHERE] * (count + len(weights) + len(filled)),
        [ANYWHERE] * (15 * count + len(filled)),
        blocks * 15 + [jax.ShapeDtypeStruct(x.shape, x.dtype) for x in filled],
        scratch,
        80 * size,
        aliases,
    )(*inputs, *weights, *filled)
    pairs = []
    for n, x in enumerate(inputs):
        own = out[n : 15 * count : count]
        pairs.append(([x] + list(own[:7]), list(own[7:])))
    return pairs, out[15 * count :]


def plane_scatter_kernel(half, *refs):
    parts = {"near": refs[:8], "far": refs[8:16]}
    out, core_in, sums, diag_in, last_in, z_out, z_in = refs[16:23]
    wire = Wire(*refs[23:])
    core, side_x, side_y, across = partners = neighbours(half)
    rows = out.shape[0] // 2
    cut = rows // 2
    low, high = pl.ds(0, cut), pl.ds(cut, cut)
    greet(partners)
    segments = [(kind, h) for kind in ("far", "near") for h in range(2)]
    from_core, from_diag, from_last, from_z = {}, {}, {}, {}

    def part(s, j):
        kind, h = segments[s]
        return parts[kind][j].at[pl.ds(h * rows, rows)]

    for s in range(4):
        for k in (3, 1, 2, 0):
            from_core[s, k] = wire.start(part(s, 2 * k + 1), core_in.at[s, k], core)

    def chip_sum(s, k):
        from_core[s, k].wait_recv()
        add_into(rows, sums.at[s, k], part(s, 2 * k), core_in.at[s, k])

    def enter(s):
        chip_sum(s, 3)
        from_diag[s, 0] = wire.start(sums.at[s, 3, low], diag_in.at[s, 0], side_x)
        from_diag[s, 1] = wire.start(sums.at[s, 3, high], diag_in.at[s, 1], side_y)
        chip_sum(s, 1)
        from_last[s, 0] = wire.start(sums.at[s, 1, low], last_in.at[s, 0, low], side_x)
        chip_sum(s, 2)
        from_last[s, 1] = wire.start(sums.at[s, 2, high], last_in.at[s, 1, high], side_y)

    def turn(s):
        from_diag[s, 1].wait_recv()
        add_into(cut, sums.at[s, 1, high], sums.at[s, 1, high], diag_in.at[s, 1])
        from_last[s, 2] = wire.start(sums.at[s, 1, high], last_in.at[s, 0, high], side_x)
        from_diag[s, 0].wait_recv()
        add_into(cut, sums.at[s, 2, low], sums.at[s, 2, low], diag_in.at[s, 0])
        from_last[s, 3] = wire.start(sums.at[s, 2, low], last_in.at[s, 1, low], side_y)

    def leave(s):
        kind, h = segments[s]
        from_core[s, 0].wait_recv()
        for i in range(4):
            from_last[s, i].wait_recv()
        target = z_out.at[h] if kind == "far" else out.at[pl.ds(h * rows, rows)]
        add_into(rows, target, part(s, 0), core_in.at[s, 0], last_in.at[s, 0], last_in.at[s, 1])
        if kind == "far":
            from_z[h] = wire.start(z_out.at[h], z_in.at[h], across)

    for step, s in (
        (enter, 0),
        (enter, 1),
        (turn, 0),
        (enter, 2),
        (turn, 1),
        (leave, 0),
        (enter, 3),
        (leave, 1),
        (turn, 2),
        (turn, 3),
        (leave, 2),
        (leave, 3),
    ):
        step(s)
    for h in range(2):
        from_z[h].wait_recv()
        target = out.at[pl.ds(h * rows, rows)]
        add_into(rows, target, target, z_in.at[h])
    wire.finish()


def plane_scatter(near, far, half, number, name):
    rows, width = near[0].shape
    specs = [ON_CHIP, ANYWHERE] * 8
    block = (rows // 2, width)
    return comm_call(
        functools.partial(plane_scatter_kernel, half),
        name,
        number,
        42,
        specs,
        ON_CHIP,
        jax.ShapeDtypeStruct((rows, width), f32),
        [
            pltpu.VMEM((4, 4) + block, bf16),
            pltpu.VMEM((4, 4) + block, bf16),
            pltpu.VMEM((4, 2, rows // 4, width), bf16),
            pltpu.VMEM((4, 2) + block, bf16),
            pltpu.VMEM((2,) + block, bf16),
            pltpu.VMEM((2,) + block, bf16),
        ],
        50 * rows * width,
    )(*near, *far)


def chip_partners():
    e = lax.axis_index("expert")
    return [{"expert": flip(e, m)} for m in (1, 2)]


def exchange_seq(wire, group, x_ref, out, between=None):
    head = lax.rem(lax.axis_index("expert"), group)
    core, side_x = chip_partners()
    rows = x_ref.shape[0]
    cut = rows // 2
    mine = pl.multiple_of(head * rows, rows)
    other = pl.multiple_of(flip(head, 2) * rows, rows)
    crossing = [
        wire.start(x_ref.at[pl.ds(h * cut, cut)], out.at[pl.ds(mine + h * cut, cut)], side_x)
        for h in range(2)
    ]
    last = [wire.start(x_ref, out.at[pl.ds(mine, rows)], core)]
    out[pl.ds(mine, rows), :] = x_ref[...]
    if between:
        between()
    for h in range(2):
        crossing[h].wait_recv()
        piece = out.at[pl.ds(other + h * cut, cut)]
        last.append(wire.start(piece, piece, core))
    for copy in last:
        copy.wait_recv()


def seq_gather_kernel(group, x_ref, out, send_sem, recv_sem):
    wire = Wire(send_sem, recv_sem)
    greet(chip_partners())
    exchange_seq(wire, group, x_ref, out)
    wire.finish()


def seq_gather(x, group, number, name):
    rows, width = x.shape
    return comm_call(
        functools.partial(seq_gather_kernel, group),
        name,
        number,
        5,
        [ON_CHIP],
        ON_CHIP,
        jax.ShapeDtypeStruct((group * rows, width), x.dtype),
        [],
        20 * x.size,
    )(x)


def sum_seq(wire, group, x_ref, out, core_in, sums, last_in):
    head = lax.rem(lax.axis_index("expert"), group)
    core, side_x = chip_partners()
    rows = out.shape[0]
    cut = rows // 2

    def part(block, h):
        return x_ref.at[pl.ds(pl.multiple_of(block * rows + h * cut, cut), cut)]

    crossing = [
        wire.start(part(flip(flip(head, 2), 1), h), core_in.at[1, h], core) for h in range(2)
    ]
    near = [wire.start(part(flip(head, 1), h), core_in.at[0, h], core) for h in range(2)]
    last = []
    for h in range(2):
        crossing[h].wait_recv()
        add_into(cut, sums.at[h], part(flip(head, 2), h), core_in.at[1, h])
        last.append(wire.start(sums.at[h], last_in.at[h], side_x))
    for h in range(2):
        near[h].wait_recv()
        last[h].wait_recv()
        add_into(
            cut, out.at[pl.ds(h * cut, cut)], part(head, h), core_in.at[0, h], last_in.at[h]
        )


def seq_scatter_kernel(group, x_ref, out, core_in, sums, last_in, send_sem, recv_sem):
    wire = Wire(send_sem, recv_sem)
    greet(chip_partners())
    sum_seq(wire, group, x_ref, out, core_in, sums, last_in)
    wire.finish()


def seq_scratch(rows, width):
    piece = (rows // 2, width)
    return [
        pltpu.VMEM((2, 2) + piece, bf16),
        pltpu.VMEM((2,) + piece, bf16),
        pltpu.VMEM((2,) + piece, bf16),
    ]


def seq_scatter(x, group, number, name):
    rows, width = x.shape[0] // group, x.shape[1]
    return comm_call(
        functools.partial(seq_scatter_kernel, group),
        name,
        number,
        6,
        [ON_CHIP],
        ON_CHIP,
        jax.ShapeDtypeStruct((rows, width), f32),
        seq_scratch(rows, width),
        20 * rows * width,
    )(x)


def entry_kernel(group, x_ref, qkv_in, out_in, seq, qkv, out_slice, send_sem, recv_sem):
    wire = Wire(send_sem, recv_sem)
    e, z = lax.axis_index("expert"), lax.axis_index("dp")
    head, row = lax.rem(e, group), lax.div(e, group)
    side_y = {"expert": flip(e, 4)}
    block = [lax.rem(z + k, 4) for k in range(4)]
    planes = [{"dp": b} for b in block]
    slab = qkv_in.shape[0]
    cut = slab // 2
    greet(chip_partners() + [side_y] + planes[1:])
    mine = pl.ds(pl.multiple_of(row * cut, cut), cut)

    def spot(plane):
        return qkv.at[pl.ds(pl.multiple_of(plane * slab + row * cut, cut), cut)]

    from_z = [wire.start(qkv_in.at[mine], spot(z), planes[k]) for k in (1, 2, 3)]
    owner = z == head

    def out_copy(n, to, at):
        return pltpu.make_async_remote_copy(
            src_ref=out_in.at[at] if n < 3 else out_slice.at[at],
            dst_ref=out_slice.at[at],
            send_sem=send_sem.at[12 + n],
            recv_sem=recv_sem.at[12 if n < 3 else 13],
            device_id=to,
            device_id_type=MESH,
        )

    spread = [out_copy(k - 1, planes[k], mine) for k in (1, 2, 3)]
    swap = out_copy(3, side_y, mine)

    @pl.when(owner)
    def _():
        for copy in spread:
            copy.start()
        out_slice[...] = out_in[...]

    qkv[pl.ds(pl.multiple_of(z * slab, slab), slab), :] = qkv_in[...]
    from_y = []

    def relay():
        for k in (1, 3, 2):
            from_z[k - 1].wait_recv()
            piece = spot(block[4 - k])
            from_y.append(wire.start(piece, piece, side_y))

    exchange_seq(wire, group, x_ref, seq, relay)
    for copy in from_y:
        copy.wait_recv()

    @pl.when(owner)
    def _():
        for copy in spread:
            copy.wait_send()

    @pl.when(jnp.logical_not(owner))
    def _():
        spread[0].wait_recv()
        swap.start()
        swap.wait()

    wire.finish()


def attention_entry(x, qkv_slice, w_out, group):
    rows, width = x.shape
    slab, columns = qkv_slice.shape
    return comm_call(
        functools.partial(entry_kernel, group),
        "attention_entry",
        8,
        16,
        [ON_CHIP] * 3,
        [ON_CHIP] * 3,
        [
            jax.ShapeDtypeStruct((group * rows, width), bf16),
            jax.ShapeDtypeStruct((4 * slab, columns), bf16),
            jax.ShapeDtypeStruct((slab, width), bf16),
        ],
        [],
        40 * x.size,
    )(x, qkv_slice, w_out)


def scatter_weights_kernel(group, experts, x_ref, w_gate_up, w_down, out, gate_up, down, *refs):
    wire = Wire(*refs[6:])
    _, beside, opposite, _, _ = plane_places()
    greet(chip_partners() + [{"dp": beside}, {"dp": opposite}])
    cargo = WeightsIn(wire, experts, w_gate_up, w_down, gate_up, down, *refs[3:6])
    sum_seq(wire, group, x_ref, out, *refs[:3])
    cargo.finish()
    wire.finish()


def seq_scatter_weights(x, group, experts, w_gate_up, w_down):
    rows, width = x.shape[0] // group, x.shape[1]
    count, slab, columns = w_gate_up.shape
    ff_rows = w_down.shape[1]
    return comm_call(
        functools.partial(scatter_weights_kernel, group, experts),
        "scatter_branch_weights",
        9,
        6 + 6 * len(experts),
        [ON_CHIP, ANYWHERE, ANYWHERE],
        [ON_CHIP, ANYWHERE, ANYWHERE],
        [
            jax.ShapeDtypeStruct((rows, width), f32),
            jax.ShapeDtypeStruct((count, 4 * slab, columns // 2), bf16),
            jax.ShapeDtypeStruct((count, 2 * ff_rows, width), bf16),
        ],
        seq_scratch(rows, width)
        + weights_scratch(len(experts), slab, columns // 2, ff_rows, width),
        40 * rows * width,
    )(x, w_gate_up, w_down)


def gather_grads_kernel(group, i, x_ref, grad_gate_up, grad_down, seq, out, out_down, *refs):
    wire = Wire(*refs[4:])
    _, beside, opposite, _, _ = plane_places()
    greet(chip_partners() + [{"dp": beside}, {"dp": opposite}])
    cargo = GradsOut(wire, i, grad_gate_up, grad_down, out, out_down, *refs[:4])
    exchange_seq(wire, group, x_ref, seq, cargo.cross)
    cargo.finish()
    wire.finish()


def seq_gather_grads(x, group, i, grad_gate_up, grad_down):
    rows, width = x.shape
    shapes, scratch = grads_shapes(grad_gate_up, grad_down)
    return comm_call(
        functools.partial(gather_grads_kernel, group, i),
        "gather_branch_grads",
        10,
        9,
        [ON_CHIP, ANYWHERE, ANYWHERE],
        [ON_CHIP] * 3,
        [jax.ShapeDtypeStruct((group * rows, width), x.dtype)] + shapes,
        scratch,
        40 * x.size,
    )(x, grad_gate_up, grad_down)


def scatter_grads_kernel(group, i, x_ref, grad_gate_up, grad_down, total, out, out_down, *refs):
    wire = Wire(*refs[7:])
    _, beside, opposite, _, _ = plane_places()
    greet(chip_partners() + [{"dp": beside}, {"dp": opposite}])
    cargo = GradsOut(wire, i, grad_gate_up, grad_down, out, out_down, *refs[3:7])
    sum_seq(wire, group, x_ref, total, *refs[:3])
    cargo.cross()
    cargo.finish()
    wire.finish()


def seq_scatter_grads(x, group, i, grad_gate_up, grad_down):
    rows, width = x.shape[0] // group, x.shape[1]
    shapes, scratch = grads_shapes(grad_gate_up, grad_down)
    return comm_call(
        functools.partial(scatter_grads_kernel, group, i),
        "scatter_normed_grads",
        11,
        10,
        [ON_CHIP, ANYWHERE, ANYWHERE],
        [ON_CHIP] * 3,
        [jax.ShapeDtypeStruct((rows, width), f32)] + shapes,
        seq_scratch(rows, width) + scratch,
        40 * rows * width,
    )(x, grad_gate_up, grad_down)


def start_kernel(replicas, small_ref, small_out, send_sem, recv_sem):
    wire = Wire(send_sem, recv_sem)
    z = lax.axis_index("dp")
    planes = [{"dp": lax.rem(z + k, replicas)} for k in range(1, replicas)]
    greet(planes)
    spread = [wire.start(small_ref, small_out.at[z], plane) for plane in planes]
    small_out[z] = small_ref[...]
    for copy in spread:
        copy.wait_recv()
    wire.finish()


def start_exchange(small, replicas):
    return comm_call(
        functools.partial(start_kernel, replicas),
        "start_exchange",
        1,
        replicas - 1,
        [ON_CHIP],
        ON_CHIP,
        jax.ShapeDtypeStruct((replicas,) + small.shape, small.dtype),
        [],
        10**6,
    )(small)


def dense_kernel(
    replicas, i, grads, small, grad_gate_up, grad_down, out, small_out, cargo_out, cargo_down, *refs
):
    y_in, z_out, z_in, small_in, small_sum, turn_in = refs[:6]
    wire = Wire(*refs[10:])
    e, z = lax.axis_index("expert"), lax.axis_index("dp")
    head, row = lax.rem(e, 4), lax.div(e, 4)
    partners = [{"expert": flip(e, m)} for m in (1, 2, 4)]
    core, side_x, side_y = partners
    slab, width = grads.shape[0] // replicas, grads.shape[1]
    cut = slab // 2
    quarter = cut // 2
    order = [2, 1, 3, 0]
    block = {k: lax.rem(z + k, replicas) for k in range(replicas)}
    plane = {k: {"dp": block[k]} for k in range(1, replicas)}
    greet(partners + list(plane.values()))

    def half_of(k, which):
        return grads.at[pl.ds(pl.multiple_of(block[k] * slab + which * cut, cut), cut)]

    small_copies = [wire.start(small.at[block[k]], small_in.at[k - 1], plane[k]) for k in plane]
    from_y = {k: wire.start(half_of(k, 1 - row), y_in.at[k], side_y) for k in order}
    cargo = GradsOut(wire, i, grad_gate_up, grad_down, cargo_out, cargo_down, *refs[6:10])
    for copy in small_copies:
        copy.wait_recv()
    small_sum[0] = small[z] + small_in[0] + small_in[1] + small_in[2]
    turn = wire.start(small_sum.at[0], turn_in.at[0], core)
    from_z = {}
    for step, k in enumerate(order):
        from_y[k].wait_recv()
        add_into(cut, z_out.at[k], half_of(k, row), y_in.at[k])
        if k:
            from_z[k] = wire.start(z_out.at[k], z_in.at[k - 1], plane[k])
        if step == 0:
            turn.wait_recv()
            small_sum[1] = small_sum[0] + turn_in[0]
            turn = wire.start(small_sum.at[1], turn_in.at[1], side_x)
        if step == 1:
            turn.wait_recv()
            small_sum[2] = small_sum[1] + turn_in[1]
            turn = wire.start(small_sum.at[2], turn_in.at[2], side_y)
    turn.wait_recv()
    small_out[...] = small_sum[2] + turn_in[2]
    cargo.cross()
    for k in from_z:
        from_z[k].wait_recv()

    def place(which_head, which_row, first=0, size=cut):
        start = pl.multiple_of(which_row * cut + first, quarter)
        columns = pl.ds(pl.multiple_of(which_head * width, 128), width)
        return out.at[pl.ds(start, size), columns]

    mine = place(head, row)
    add_into(cut, mine, z_out.at[0], z_in.at[0], z_in.at[1], z_in.at[2])
    other = flip(head, 2)
    pieces = [place(head, row, h * quarter, quarter) for h in range(2)]
    over_x = [wire.start(piece, piece, side_x) for piece in pieces]
    over_y = [wire.start(piece, piece, side_y) for piece in reversed(pieces)]
    last = [wire.start(mine, mine, core)]
    over_x[0].wait_recv()
    piece = place(other, row, 0, quarter)
    diag = [wire.start(piece, piece, side_y)]
    over_y[0].wait_recv()
    piece = place(head, 1 - row, quarter, quarter)
    diag.append(wire.start(piece, piece, side_x))
    over_x[1].wait_recv()
    last.append(wire.start(place(other, row), place(other, row), core))
    over_y[1].wait_recv()
    last.append(wire.start(place(head, 1 - row), place(head, 1 - row), core))
    for copy in diag:
        copy.wait_recv()
    last.append(wire.start(place(other, 1 - row), place(other, 1 - row), core))
    for copy in last:
        copy.wait_recv()
    cargo.finish()
    wire.finish()


def dense_reduce(grads, small, replicas, i, grad_gate_up, grad_down):
    slab, width = grads.shape[0] // replicas, grads.shape[1]
    piece = (slab // 2, width)
    lot = small.shape[1:]
    shapes, scratch = grads_shapes(grad_gate_up, grad_down)
    return comm_call(
        functools.partial(dense_kernel, replicas, i),
        "dense_reduce",
        2,
        27,
        [ON_CHIP] * 2 + [ANYWHERE] * 2,
        [ON_CHIP] * 4,
        [jax.ShapeDtypeStruct((slab, 4 * width), bf16), jax.ShapeDtypeStruct(lot, f32)] + shapes,
        [
            pltpu.VMEM((4,) + piece, bf16),
            pltpu.VMEM((4,) + piece, bf16),
            pltpu.VMEM((3,) + piece, bf16),
            pltpu.VMEM((3,) + lot, f32),
            pltpu.VMEM((3,) + lot, f32),
            pltpu.VMEM((3,) + lot, f32),
        ]
        + scratch,
        10**8,
    )(grads, small, grad_gate_up, grad_down)


def body(
    hidden_in,
    teacher,
    valid,
    routes,
    gain_attn,
    gain_moe,
    w_query,
    w_key,
    w_value,
    w_out,
    w_router,
    w_gate_up,
    w_down,
):
    tok, width = hidden_in.shape
    owners = lax.axis_size("expert")
    replicas = lax.axis_size("dp")
    me = lax.axis_index("expert")
    plane = lax.axis_index("dp")
    length = min(SEQ_MIN, owners * tok)
    group = length // tok
    head = me % group
    experts_all = EXP_DEV * owners
    slots = 8 * ((tok * TOP + experts_all * 7 - 1) // (experts_all * 7))
    half = replicas // 2
    side = plane // half
    ff_half = FF // 2
    slab = width // replicas
    q_cols = H * HD // group
    kv_cols = KVH * HD // group
    kv_dev = KVH // group
    per_kv = H // KVH

    def over_dp(x, axis):
        if replicas > group:
            return lax.all_gather(x, "dp", axis=axis, tiled=True)
        return place(
            [x] + [send(x, "dp", m) for m in range(1, replicas)],
            [plane ^ m for m in range(replicas)],
            axis,
            replicas,
        )

    routes_t = jnp.transpose(routes)
    count = jnp.full_like(routes_t, jnp.sum(valid))
    small = jnp.concatenate(
        [gain_attn[None], gain_moe[None], jnp.transpose(w_router), jnp.zeros((6, slab), bf16)]
    )
    names = jnp.concatenate([routes_t, count])
    small = start_exchange(small, replicas)
    small = jnp.transpose(small, (1, 0, 2)).reshape(small.shape[1], width)
    gain_one, gain_two, router_t = small[0], small[1], small[2 : 2 + experts_all]
    me_ref = jnp.reshape(me, (1,)).astype(jnp.int32)
    valid_float = valid.astype(f32)
    qkv_slice = jnp.concatenate(
        [
            pick(w_query, head, q_cols, 1),
            pick(w_key, head, kv_cols, 1),
            pick(w_value, head, kv_cols, 1),
        ],
        axis=1,
    )
    inputs = hidden_in.astype(f32)
    normed_f, norm_one_pull = jax.vjp(rms_norm, inputs, gain_one.astype(f32))
    normed = normed_f.astype(bf16)
    compact = replicas == group

    def on_grid(x, pairs):
        return lax.ppermute(x, ("dp", "expert"), pairs)

    if compact:
        seq, qkv, out_slice = attention_entry(normed, qkv_slice, w_out, group)
    else:
        seq = seq_gather(normed, group, 3, "gather_normed")
        qkv = over_dp(qkv_slice, 0)
        out_slice = pick(lax.all_gather(w_out, "dp", axis=0, tiled=True), head, q_cols, 0)

    lin = mm("td,dc->tc", seq, qkv)
    cosine, sine = rope_tables(jnp.arange(length, dtype=f32))
    queries = (
        rotary(lin[:, :q_cols].reshape(length, kv_dev * per_kv, HD), cosine, sine)
        .astype(bf16)
        .reshape(length, kv_dev, per_kv, HD)
    )
    keys = rotary(
        lin[:, q_cols : q_cols + kv_cols].reshape(length, kv_dev, HD), cosine, sine
    ).astype(bf16)
    values = lin[:, q_cols + kv_cols :].reshape(length, kv_dev, HD).astype(bf16)
    context, log_total = attend(queries, keys, values)
    context = context.reshape(length, q_cols)
    branch = mm("tc,cd->td", context, out_slice).astype(bf16)
    if compact:
        summed, gate_up_w, down_w = seq_scatter_weights(branch, group, (0,), w_gate_up, w_down)
    else:
        summed = seq_scatter(branch, group, 4, "scatter_branch")
        gate_up_all = lax.all_gather(w_gate_up, "dp", axis=1, tiled=True)
        gate_up_w = jnp.concatenate(
            [pick(gate_up_all, p * 2 + side, ff_half, 2) for p in range(2)], axis=2
        )
        down_w = pick(lax.all_gather(w_down, "dp", axis=1, tiled=True), side, ff_half, 1)
    mid = inputs + RESIDUAL * summed
    moe_f, norm_two_pull = jax.vjp(rms_norm, mid, gain_two.astype(f32))
    moe_input = moe_f.astype(bf16)

    if compact:
        blocks, (gate_up_w, down_w) = plane_gather(
            [moe_input, names],
            half,
            12,
            "gather_all",
            (1, 2),
            (w_gate_up, w_down),
            (gate_up_w, down_w),
        )
    else:
        blocks, _ = plane_gather([moe_input, names], half, 13, "gather_names")
    (near, far), (near_names, far_names) = blocks
    near_parts, near_kept, near_count = experts_forward(
        me_ref, near_names, router_t, near, gate_up_w, down_w
    )
    far_parts, far_kept, far_count = experts_forward(
        me_ref, far_names, router_t, far, gate_up_w, down_w
    )
    valid_count = near_count[0, :1] + far_count[0, :1]
    mask = 1
    while mask < half:
        valid_count = valid_count + send(valid_count, "dp", mask)
        mask *= 2
    valid_count = valid_count[0].astype(f32)
    final_state = mid + RESIDUAL * plane_scatter(near_parts, far_parts, half, 6, "scatter_outputs")
    activations = final_state.astype(bf16)
    mismatch = final_state - teacher.astype(f32)
    squares = jnp.sum(0.5 * valid_float[:, None] * mismatch * mismatch)
    tokens_all = tok * replicas * owners
    grad_final = tokens_all / valid_count * valid_float[:, None] * mismatch

    ((grad_near, grad_far),), _ = plane_gather([grad_final.astype(bf16)], half, 5, "gather_tokens")

    def back(kept, blocks):
        arrived, lin, weighted, slot, gate = kept
        parts, (grads, lin_grad) = experts_backward(
            me_ref, slot, gate, lin, blocks, gate_up_w, down_w
        )
        return parts, (arrived, lin_grad, weighted, grads)

    near_grads, near_chunk = back(near_kept, grad_near)
    far_grads, far_chunk = back(far_kept, grad_far)
    returned = plane_scatter(near_grads, far_grads, half, 7, "scatter_grads")
    after = jnp.reshape(never(returned[0, 0]), (1,))
    grad_gate_up, grad_down = expert_weights(after, [near_chunk, far_chunk])
    branch_scale = jnp.where(never(grad_down[0, 0, 0]) == 0, RESIDUAL, 0.0)

    grad_gates = returned[:, width : width + experts_all]
    own_routed = jnp.any(
        routes[:, :, None] == jnp.arange(experts_all, dtype=jnp.int32), axis=1
    )
    own_logits = jnp.where(own_routed, mm("td,ed->te", moe_input, router_t), NEG)
    own_gates = jnp.where(own_routed, jax.nn.softmax(own_logits, axis=-1), 0.0)
    grad_logits = (
        own_gates * (grad_gates - jnp.sum(own_gates * grad_gates, axis=-1, keepdims=True))
    ).astype(bf16)
    grad_router_t = mm("td,te->ed", moe_input, grad_logits)
    grad_moe_input = returned[:, :width] + mm("te,ed->td", grad_logits, router_t)
    grad_mid_norm, grad_gain_two = norm_two_pull(grad_moe_input)
    grad_mid = grad_final + grad_mid_norm
    grad_branch = (branch_scale * grad_mid).astype(bf16)

    done = []
    if compact:
        seq_grad, *part = seq_gather_grads(grad_branch, group, 0, grad_gate_up, grad_down)
        done.append(part)
    else:
        seq_grad = seq_gather(grad_branch, group, 3, "gather_normed")
    grad_out = mm("tc,td->cd", context, seq_grad).astype(bf16)
    if compact:
        out_sum = grad_out.astype(f32)
        for step in range(1, replicas):
            pairs = [
                (
                    ((i % group + step) % replicas) * owners + i,
                    (i % group) * owners + i,
                )
                for i in range(owners)
            ]
            out_sum = out_sum + on_grid(grad_out, pairs).astype(f32)
        entered = jnp.where(never(out_sum[0, 0]) == 0, 1.0, 0.0)
    grad_context = (
        mm("td,cd->tc", seq_grad, out_slice).astype(bf16).reshape(length, kv_dev, per_kv, HD)
    )
    grad_q, grad_k, grad_v = attend_back(queries, keys, values, log_total, grad_context)
    grad_lin = jnp.concatenate(
        [
            rotary(grad_q.reshape(length, kv_dev * per_kv, HD), cosine, -sine).reshape(
                length, q_cols
            ),
            rotary(grad_k, cosine, -sine).reshape(length, kv_cols),
            grad_v.reshape(length, kv_cols),
        ],
        axis=1,
    ).astype(bf16)
    grad_qkv = mm("td,tc->dc", seq, grad_lin).astype(bf16)
    normed_parts = mm("tc,dc->td", grad_lin, qkv)
    normed_parts = (entered * normed_parts if compact else normed_parts).astype(bf16)
    if compact:
        grad_normed, *part = seq_scatter_grads(normed_parts, group, 1, grad_gate_up, grad_down)
        done.append(part)
    else:
        grad_normed = seq_scatter(normed_parts, group, 4, "scatter_branch")
    grad_in_norm, grad_gain_one = norm_one_pull(grad_normed)
    grad_in = grad_mid + grad_in_norm

    def other_sequences(x):
        total = x.astype(f32)
        mask = group
        while mask < owners:
            total = total + send(total.astype(bf16), "expert", mask).astype(f32)
            mask *= 2
        return total

    lot = jnp.concatenate(
        [
            grad_router_t,
            grad_gain_one[None],
            grad_gain_two[None],
            jnp.full((6, width), squares),
        ]
    )
    if compact:
        out_sum = other_sequences(out_sum).astype(bf16)
        g_out = jnp.where(plane == head, out_sum, jnp.zeros((), bf16))
        for m in range(1, group):
            pairs = [
                ((i % group) * owners + i, (i % group) * owners + (i ^ m)) for i in range(owners)
            ]
            g_out = g_out + on_grid(out_sum, pairs)
        g_out = g_out.astype(f32)
        lot = jnp.where(never(out_sum[0, 0]) == 0, lot, 0.0)
        lot = jnp.transpose(lot.reshape(32, replicas, slab), (1, 0, 2))
        by_head, lot, *part = dense_reduce(
            grad_qkv, lot, replicas, 2, grad_gate_up, grad_down
        )
        done.append(part)
        gate_up_out, down_out = [jnp.stack(x).astype(f32) for x in zip(*done)]
    else:
        out_sum = other_sequences(lax.psum(grad_out, "dp")).astype(bf16)
        g_out = pick(
            place(
                gather_blocks(out_sum, group), [head ^ j for j in range(group)], 0, group
            ),
            plane,
            slab,
            0,
        ).astype(f32)
        lot = lax.psum_scatter(lot, "dp", scatter_dimension=1, tiled=True)
        lot = lax.psum(lot, "expert")
        qkv_sum = lax.psum_scatter(
            grad_qkv.astype(f32), "dp", scatter_dimension=0, tiled=True
        )
        qkv_sum = other_sequences(qkv_sum).astype(bf16)
        by_head = place(
            gather_blocks(qkv_sum, group), [head ^ j for j in range(group)], 1, group
        )
        spread = lambda x: lax.psum_scatter(
            x.astype(f32), "dp", scatter_dimension=1, tiled=True
        )
        blank = jnp.zeros_like(grad_down)
        down_out = spread(
            jnp.where(
                side == 0,
                jnp.concatenate([grad_down, blank], axis=1),
                jnp.concatenate([blank, grad_down], axis=1),
            )
        )
        first = spread(jnp.where(side == 0, grad_gate_up, jnp.zeros((), bf16)))
        last = spread(jnp.where(side == 1, grad_gate_up, jnp.zeros((), bf16)))
        gate_up_out = jnp.concatenate(
            [
                first[:, :, :ff_half],
                last[:, :, :ff_half],
                first[:, :, ff_half:],
                last[:, :, ff_half:],
            ],
            axis=2,
        )

    def of_heads(first, count):
        wide = q_cols + 2 * kv_cols
        return jnp.concatenate(
            [by_head[:, h * wide + first : h * wide + first + count] for h in range(group)], axis=1
        ).astype(f32)

    g_query = of_heads(0, q_cols)
    g_key = of_heads(q_cols, kv_cols)
    g_value = of_heads(q_cols + kv_cols, kv_cols)
    g_router, g_one, g_two = (
        jnp.transpose(lot[:experts_all]),
        lot[experts_all],
        lot[experts_all + 1],
    )
    loss_value = lot[experts_all + 2, 0] / (valid_count * width)

    return (
        activations,
        loss_value,
        grad_in,
        g_one,
        g_two,
        g_query,
        g_key,
        g_value,
        g_out,
        g_router,
        gate_up_out,
        down_out,
    )


def solution(mesh):
    placed = (
        P(("dp", "expert"), None),
        P(("dp", "expert"), None),
        P(("dp", "expert")),
        P(("dp", "expert"), None),
        P("dp"),
        P("dp"),
        P("dp", None),
        P("dp", None),
        P("dp", None),
        P("dp", None),
        P("dp", None),
        P("expert", "dp", None),
        P("expert", "dp", None),
    )
    return jax.shard_map(
        body,
        mesh=mesh,
        in_specs=placed,
        out_specs=(
            P(("dp", "expert"), None),
            P(),
            P(("dp", "expert"), None),
            P("dp"),
            P("dp"),
            P("dp", None),
            P("dp", None),
            P("dp", None),
            P("dp", None),
            P("dp", None),
            P("expert", "dp", None),
            P("expert", "dp", None),
        ),
        check_vma=False,
    )
```

```python
import functools

import jax
import jax.numpy as jnp
from jax import lax
from jax.experimental import pallas as pl
from jax.experimental.pallas import tpu as pltpu
from jax.sharding import PartitionSpec as P

H = 24
KVH = 8
HD = 64
FF = 512
TOP = 8
EXP_DEV = 3
SEQ_MIN = 1024

EPS = 1e-05
RESIDUAL = 0.22
SCORE_SCALE = 1.0 / 64.0
ROPE_BASE = 10000.0
NEG = -1000000000.0

f32 = jnp.float32
bf16 = jnp.bfloat16


def mm(spec, a, b):
    return jnp.einsum(spec, a, b, preferred_element_type=f32)


def rms_norm(states, gain):
    return states * lax.rsqrt(jnp.mean(states * states, axis=-1, keepdims=True) + EPS) * gain


def rope_tables(positions):
    half_dim = HD // 2
    frequencies = ROPE_BASE ** (-(2.0 * jnp.arange(half_dim, dtype=f32)) / HD)
    angles = frequencies[:, None] * positions[None, :]
    return jnp.cos(angles), jnp.sin(angles)


def send(x, axis, mask):
    count = lax.axis_size(axis)
    return lax.ppermute(x, axis, [(i, i ^ mask) for i in range(count)])


def gather_blocks(x, count):
    blocks = [x]
    for j in range(1, count):
        blocks.append(send(blocks[j - 1], "expert", 1) if j % 2 else send(x, "expert", j))
    return blocks


def scatter_sum(parts):
    total = None
    for j in range(0, len(parts), 2):
        chip = parts[j].astype(f32) + send(parts[j + 1], "expert", 1).astype(f32)
        if j:
            chip = send(chip.astype(bf16), "expert", j).astype(f32)
        total = chip if total is None else total + chip
    return total


def total_over(x, axis):
    mask = 1
    while mask < lax.axis_size(axis):
        x = x + send(x, axis, mask)
        mask *= 2
    return x


def place(blocks, starts, axis, size):
    width = blocks[0].shape[axis]
    shape = list(blocks[0].shape)
    shape[axis] = size * width
    out = jnp.zeros(shape, blocks[0].dtype)
    for block, start in zip(blocks, starts):
        out = lax.dynamic_update_slice_in_dim(out, block, start * width, axis)
    return out


def pick(x, index, width, axis):
    return lax.dynamic_slice_in_dim(x, index * width, width, axis)


def never(x):
    return (x != x).astype(jnp.int32)


CAP = 112
GATE_COLUMNS = 128
NT = (((1,), (1,)), ((), ()))
TN = (((0,), (0,)), ((), ()))
NN = (((1,), (0,)), ((), ()))


def dg(a, b, dims):
    return lax.dot_general(a, b, dims, preferred_element_type=f32)


def whole(shape):
    return pl.BlockSpec(shape, lambda *_: (0,) * len(shape))


def params(mib):
    return pltpu.CompilerParams(vmem_limit_bytes=mib << 20)


def select_rows(slot_row):
    row = lax.broadcasted_iota(jnp.int32, (CAP, slot_row.shape[1]), 0).astype(f32)
    return row == slot_row


def experts_kernel(me_ref, router_ref, gate_up_ref, down_ref, *refs):
    blocks, routes, refs = refs[:8], refs[8:16], refs[16:]
    parts, refs = refs[:8], refs[8:]
    arrived_ref, lin_ref, weighted_ref, slot_ref, gate_ref, count_ref, sel, made = refs
    step = pl.program_id(0)
    tok, width = blocks[0].shape

    @pl.when(step == 0)
    def _():
        first = me_ref[0] * EXP_DEV
        experts = router_ref.shape[0]
        which = lax.broadcasted_iota(jnp.int32, (experts, tok), 0)
        before = (
            lax.broadcasted_iota(jnp.int32, (tok, tok), 0)
            < lax.broadcasted_iota(jnp.int32, (tok, tok), 1)
        ).astype(bf16)
        count = jnp.zeros(count_ref.shape, jnp.int32)
        for s in range(8):
            logits = dg(router_ref[...], blocks[s][...], NT)
            names = routes[s][...]
            count = count + names[TOP:]
            routed = which == names[0:1, :]
            for k in range(1, TOP):
                routed = routed | (which == names[k : k + 1, :])
            logits = jnp.where(routed, logits, NEG)
            top = jnp.max(logits, axis=0, keepdims=True)
            grown = jnp.where(routed, jnp.exp(logits - top), 0.0)
            gates = grown / jnp.sum(grown, axis=0, keepdims=True)
            hots, picked = [], []
            for i in range(EXP_DEV):
                own = which == first + i
                hots.append(jnp.sum(jnp.where(own & routed, 1.0, 0.0), axis=0, keepdims=True))
                picked.append(jnp.sum(jnp.where(own, gates, 0.0), axis=0, keepdims=True))
            filler = jnp.zeros((8 - EXP_DEV, tok), f32)
            hot = jnp.concatenate(hots + [filler], axis=0)
            rank = dg(hot.astype(bf16), before, NN)
            slot = jnp.where(hot > 0.0, rank, -1.0)
            slot_ref[s] = slot
            gate_ref[s] = jnp.concatenate(picked + [filler], axis=0)
            for i in range(EXP_DEV):
                sel[s, i * CAP : (i + 1) * CAP, :] = select_rows(slot[i : i + 1, :]).astype(bf16)
        count_ref[...] = count

    at = pl.ds(pl.multiple_of(step * CAP, CAP), CAP)
    for s in range(8):
        arrived_ref[s, 0] = dg(sel[s, at, :], blocks[s][...], NN).astype(bf16)
    lin = dg(arrived_ref[:, 0].reshape(8 * CAP, width), gate_up_ref[0], NN)
    lin_ref[:, 0] = lin.reshape(8, CAP, lin.shape[1])
    half = lin.shape[1] // 2
    gate_part, up_part = lin[:, :half], lin[:, half:]
    hidden = gate_part * jax.nn.sigmoid(gate_part) * up_part
    for s in range(8):
        gate_row = gate_ref[s, pl.ds(step, 1), :]
        row_gate = jnp.sum(
            jnp.where(sel[s, at, :] > 0, gate_row, 0.0), axis=1, keepdims=True
        )
        weighted_ref[s, 0] = (row_gate * hidden[s * CAP : (s + 1) * CAP]).astype(bf16)
    out = dg(weighted_ref[:, 0].reshape(8 * CAP, half), down_ref[0], NN)
    made[:, at, :] = out.reshape(8, CAP, width).astype(bf16)

    @pl.when(step == EXP_DEV - 1)
    def _():
        for s in range(8):
            parts[s][...] = dg(sel[s], made[s], TN).astype(bf16)


def experts_forward(me, routes, router_t, blocks, gate_up_w, down_w):
    tok, width = blocks[0].shape
    cols, half = gate_up_w.shape[2], down_w.shape[1]
    by_expert = lambda w: pl.BlockSpec((8, 1, CAP, w), lambda e, *_: (0, e, 0, 0))
    rows = lambda w, t: jax.ShapeDtypeStruct((8, EXP_DEV, CAP, w), t)
    out = pl.pallas_call(
        experts_kernel,
        grid_spec=pltpu.PrefetchScalarGridSpec(
            num_scalar_prefetch=1,
            grid=(EXP_DEV,),
            in_specs=[
                whole(router_t.shape),
                pl.BlockSpec((1, width, cols), lambda e, *_: (e, 0, 0)),
                pl.BlockSpec((1, half, width), lambda e, *_: (e, 0, 0)),
            ]
            + [whole((tok, width))] * 8
            + [whole(routes[0].shape)] * 8,
            out_specs=[whole((tok, width))] * 8
            + [by_expert(width), by_expert(cols), by_expert(half)]
            + [whole((8, 8, tok))] * 2
            + [whole((8, tok))],
            scratch_shapes=[
                pltpu.VMEM((8, EXP_DEV * CAP, tok), bf16),
                pltpu.VMEM((8, EXP_DEV * CAP, width), bf16),
            ],
        ),
        out_shape=[jax.ShapeDtypeStruct((tok, width), bf16)] * 8
        + [rows(width, bf16), rows(cols, f32), rows(half, bf16)]
        + [jax.ShapeDtypeStruct((8, 8, tok), f32)] * 2
        + [jax.ShapeDtypeStruct((8, tok), jnp.int32)],
        compiler_params=params(60),
        cost_estimate=pl.CostEstimate(
            flops=11 * 10**9, bytes_accessed=40 * 10**6, transcendentals=10**6
        ),
        name="experts_forward",
    )(me, router_t, gate_up_w, down_w, *blocks, *routes)
    return list(out[:8]), out[8:13], out[13]


def experts_back_kernel(me_ref, slot_ref, gate_ref, lin_ref, gate_up_ref, down_ref, *refs):
    blocks, refs = refs[:8], refs[8:]
    parts, refs = refs[:8], refs[8:]
    arrived_ref, lin_grad_ref, sel, made = refs
    step = pl.program_id(0)
    tok, width = blocks[0].shape
    half = down_ref.shape[1]
    at = pl.ds(pl.multiple_of(step * CAP, CAP), CAP)

    for s in range(8):
        sel[s, at, :] = select_rows(slot_ref[s, pl.ds(step, 1), :]).astype(bf16)
        arrived_ref[s, 0] = dg(sel[s, at, :], blocks[s][...], NN).astype(bf16)
    pull = dg(arrived_ref[:, 0].reshape(8 * CAP, width), down_ref[0], NT)
    lin = lin_ref[:, 0].reshape(8 * CAP, 2 * half)
    gate_part, up_part = lin[:, :half], lin[:, half:]
    sig = jax.nn.sigmoid(gate_part)
    act = gate_part * sig
    row_gg = RESIDUAL * jnp.sum(act * up_part * pull, axis=1, keepdims=True)
    slope = sig * (1.0 + gate_part * (1.0 - sig))
    own = me_ref[0] * EXP_DEV + step
    column = lax.broadcasted_iota(jnp.int32, (CAP, made.shape[2] - width), 1)
    for s in range(8):
        mine = slice(s * CAP, (s + 1) * CAP)
        chosen = sel[s, at, :] > 0
        gate_row = gate_ref[s, pl.ds(step, 1), :]
        row_gate = jnp.sum(jnp.where(chosen, gate_row, 0.0), axis=1, keepdims=True)
        made[s, at, width:] = jnp.where(column == own, row_gg[mine], 0.0).astype(bf16)
        hidden_grad = RESIDUAL * row_gate * pull[mine]
        lin_grad_ref[s, 0, :, :half] = (hidden_grad * up_part[mine] * slope[mine]).astype(bf16)
        lin_grad_ref[s, 0, :, half:] = (hidden_grad * act[mine]).astype(bf16)
    out = dg(lin_grad_ref[:, 0].reshape(8 * CAP, 2 * half), gate_up_ref[0], NT)
    made[:, at, :width] = out.reshape(8, CAP, width).astype(bf16)

    @pl.when(step == EXP_DEV - 1)
    def _():
        for s in range(8):
            parts[s][...] = dg(sel[s], made[s], TN).astype(bf16)


def experts_backward(me, slot, gate, lin, blocks, gate_up_w, down_w):
    tok, width = blocks[0].shape
    cols, half = gate_up_w.shape[2], down_w.shape[1]
    wide = width + GATE_COLUMNS
    by_expert = lambda w: pl.BlockSpec((8, 1, CAP, w), lambda e, *_: (0, e, 0, 0))
    rows = lambda w: jax.ShapeDtypeStruct((8, EXP_DEV, CAP, w), bf16)
    out = pl.pallas_call(
        experts_back_kernel,
        grid_spec=pltpu.PrefetchScalarGridSpec(
            num_scalar_prefetch=1,
            grid=(EXP_DEV,),
            in_specs=[
                whole(slot.shape),
                whole(gate.shape),
                by_expert(cols),
                pl.BlockSpec((1, width, cols), lambda e, *_: (e, 0, 0)),
                pl.BlockSpec((1, half, width), lambda e, *_: (e, 0, 0)),
            ]
            + [whole((tok, width))] * 8,
            out_specs=[whole((tok, wide))] * 8 + [by_expert(width), by_expert(cols)],
            scratch_shapes=[
                pltpu.VMEM((8, EXP_DEV * CAP, tok), bf16),
                pltpu.VMEM((8, EXP_DEV * CAP, wide), bf16),
            ],
        ),
        out_shape=[jax.ShapeDtypeStruct((tok, wide), bf16)] * 8 + [rows(width), rows(cols)],
        compiler_params=params(60),
        cost_estimate=pl.CostEstimate(
            flops=11 * 10**9, bytes_accessed=40 * 10**6, transcendentals=10**6
        ),
        name="experts_backward",
    )(me, slot, gate, lin, gate_up_w, down_w, *blocks)
    return list(out[:8]), out[8:]


def expert_weights_kernel(after_ref, *refs):
    chunks = len(refs) // 4
    gate_up_ref, down_ref = refs[-2:]
    gate_up, down = None, None
    for c in range(chunks):
        states, lin_grad, weighted, grads = [
            r[:, 0].reshape(8 * CAP, r.shape[3]) for r in refs[4 * c : 4 * c + 4]
        ]
        one, two = dg(states, lin_grad, TN), dg(weighted, grads, TN)
        gate_up = one if gate_up is None else gate_up + one
        down = two if down is None else down + two
    gate_up_ref[0] = gate_up.astype(bf16)
    down_ref[0] = (RESIDUAL * down).astype(bf16)


def expert_weights(after, chunks):
    width, cols, half = [chunks[0][i].shape[3] for i in range(3)]
    by_expert = lambda w: pl.BlockSpec((8, 1, CAP, w), lambda e, *_: (0, e, 0, 0))
    flat = [x for chunk in chunks for x in chunk]
    return pl.pallas_call(
        expert_weights_kernel,
        grid_spec=pltpu.PrefetchScalarGridSpec(
            num_scalar_prefetch=1,
            grid=(EXP_DEV,),
            in_specs=[by_expert(x.shape[3]) for x in flat],
            out_specs=[
                pl.BlockSpec((1, width, cols), lambda e, *_: (e, 0, 0)),
                pl.BlockSpec((1, half, width), lambda e, *_: (e, 0, 0)),
            ],
        ),
        out_shape=[
            jax.ShapeDtypeStruct((EXP_DEV, width, cols), bf16),
            jax.ShapeDtypeStruct((EXP_DEV, half, width), bf16),
        ],
        compiler_params=params(60),
        cost_estimate=pl.CostEstimate(
            flops=14 * 10**9, bytes_accessed=40 * 10**6, transcendentals=0
        ),
        name="expert_weights",
    )(after, *flat)


MESH = pl.DeviceIdType.MESH


def flip(index, mask):
    return index + mask - 2 * mask * lax.rem(lax.div(index, mask), 2)


def greet(partners):
    barrier = pltpu.get_barrier_semaphore()
    for partner in partners:
        pl.semaphore_signal(barrier, inc=1, device_id=partner, device_id_type=MESH)
    pl.semaphore_wait(barrier, len(partners))


class Wire:
    def __init__(self, send_sem, recv_sem):
        self.send_sem, self.recv_sem, self.copies = send_sem, recv_sem, []

    def start(self, src, dst, partner):
        i = len(self.copies)
        copy = pltpu.make_async_remote_copy(
            src_ref=src,
            dst_ref=dst,
            send_sem=self.send_sem.at[i],
            recv_sem=self.recv_sem.at[i],
            device_id=partner,
            device_id_type=MESH,
        )
        copy.start()
        self.copies.append(copy)
        return copy

    def finish(self):
        for copy in self.copies:
            copy.wait_send()


def comm_call(
    kernel, name, number, copies, in_specs, out_specs, out_shape, scratch, cost, aliases={}
):
    return pl.pallas_call(
        kernel,
        in_specs=in_specs,
        out_specs=out_specs,
        out_shape=out_shape,
        scratch_shapes=list(scratch) + [pltpu.SemaphoreType.DMA((copies,))] * 2,
        compiler_params=pltpu.CompilerParams(
            vmem_limit_bytes=60 << 20, collective_id=number, has_side_effects=True
        ),
        cost_estimate=pl.CostEstimate(flops=cost, bytes_accessed=cost, transcendentals=0),
        input_output_aliases=aliases,
        name=name,
    )


ANYWHERE = pl.BlockSpec(memory_space=pl.ANY)
ON_CHIP = pl.BlockSpec(memory_space=pltpu.VMEM)


def add_into(rows, out, first, *others, step=32):
    @pl.loop(0, rows // step)
    def _(i):
        at = pl.ds(pl.multiple_of(i * step, step), step)
        total = first[at].astype(f32)
        for other in others:
            total = total + other[at].astype(f32)
        out[at] = total.astype(out.dtype)


def plane_places():
    z = lax.axis_index("dp")
    return z, flip(z, 1), lax.rem(z + 2, 4), lax.div(z, 2), lax.rem(z, 2)


def stripe(index, size):
    return pl.ds(pl.multiple_of(index * size, size), size)


class WeightsIn:
    def __init__(
        self,
        wire,
        experts,
        w_gate_up,
        w_down,
        gate_up,
        down,
        stage,
        stage_down,
        sems,
        direct=False,
    ):
        z, beside, opposite, side, low = plane_places()
        slab, part = w_gate_up.shape[1], gate_up.shape[2] // 2
        rows = w_down.shape[1]
        self.wire, self.gate_up, self.slab, self.opposite = wire, gate_up, slab, opposite
        self.beside = {"dp": beside}
        self.crossing, self.arriving, self.stores = [], [], []
        self.direct = direct

        def columns(i, which, p):
            return w_gate_up.at[i, :, stripe(2 * p + which, part)]

        def spot(i, p):
            return gate_up.at[i, stripe(z, slab), pl.ds(p * part, part)]

        self.loads = loads = []
        for n, i in enumerate(experts):
            for p in range(2):
                loads.append(
                    pltpu.make_async_copy(
                        columns(i, side, p),
                        stage.at[n, :, pl.ds(p * part, part)],
                        sems.at[n, p],
                    )
                )
            loads.append(pltpu.make_async_copy(w_down.at[i], stage_down.at[n], sems.at[n, 2]))
            for load in loads[-3:]:
                load.start()
            if direct:
                corner = {"dp": flip(opposite, 1)}
                for p in range(2):
                    self.arriving.append(wire.start(columns(i, 1 - side, p), spot(i, p), corner))
            self.crossing.append(
                (
                    i,
                    [
                        wire.start(columns(i, 1 - side, p), spot(i, p), {"dp": opposite})
                        for p in range(2)
                    ],
                )
            )
            for p in range(2):
                self.arriving.append(wire.start(columns(i, side, p), spot(i, p), self.beside))
            here = down.at[i, stripe(low, rows)]
            self.arriving.append(wire.start(w_down.at[i], here, self.beside))
            self.stores.append(
                pltpu.make_async_copy(
                    stage.at[n], gate_up.at[i, stripe(z, slab)], sems.at[n, 3]
                )
            )
            self.stores.append(pltpu.make_async_copy(stage_down.at[n], here, sems.at[n, 4]))

    def finish(self):
        for load in self.loads:
            load.wait()
        for store in self.stores:
            store.start()
        for i, copies in self.crossing:
            for copy in copies:
                copy.wait_recv()
            if self.direct:
                continue
            piece = self.gate_up.at[i, stripe(self.opposite, self.slab)]
            self.arriving.append(self.wire.start(piece, piece, self.beside))
        for copy in self.arriving:
            copy.wait_recv()
        for store in self.stores:
            store.wait()


def weights_scratch(count, slab, columns, rows, width):
    return [
        pltpu.VMEM((count, slab, columns), bf16),
        pltpu.VMEM((count, rows, width), bf16),
        pltpu.SemaphoreType.DMA((count, 5)),
    ]


class GradsOut:
    def __init__(self, wire, i, grad_gate_up, grad_down, out, out_down, got, own, downs, sems):
        z, beside, opposite, side, low = plane_places()
        slab, rows = out.shape[0], out_down.shape[0]
        self.wire, self.side, self.across = wire, side, {"dp": opposite}
        self.out, self.out_down, self.got, self.own, self.downs = out, out_down, got, own, downs

        def slab_of(plane):
            return grad_gate_up.at[i, stripe(plane, slab)]

        def rows_of(which):
            return grad_down.at[i, stripe(which, rows)]

        to = {"dp": beside}
        self.loads = [
            pltpu.make_async_copy(slab_of(opposite), own.at[0], sems.at[0]),
            pltpu.make_async_copy(slab_of(z), own.at[1], sems.at[1]),
            pltpu.make_async_copy(rows_of(low), downs.at[0], sems.at[2]),
        ]
        for load in self.loads:
            load.start()
        self.copies = [
            wire.start(slab_of(flip(opposite, 1)), got.at[0], to),
            wire.start(slab_of(beside), got.at[1], to),
            wire.start(rows_of(1 - low), downs.at[1], to),
        ]

    def cross(self):
        self.loads[0].wait()
        self.copies[0].wait_recv()
        slab = self.out.shape[0]
        add_into(slab, self.own.at[2], self.own.at[0], self.got.at[0])
        self.copies.append(self.wire.start(self.own.at[2], self.got.at[2], self.across))

    def finish(self):
        part = self.out.shape[1] // 4
        slab = self.out.shape[0]
        self.loads[1].wait()
        self.copies[1].wait_recv()
        self.copies[3].wait_recv()
        out, got, own, side = self.out, self.got, self.own, self.side

        @pl.loop(0, slab // 32)
        def _(r):
            at = pl.ds(pl.multiple_of(r * 32, 32), 32)
            for p in range(2):
                lanes = pl.ds(p * part, part)
                total = own[1, at, lanes].astype(f32) + got[1, at, lanes].astype(f32)
                out[at, stripe(2 * p + side, part)] = total.astype(bf16)
                out[at, stripe(2 * p + 1 - side, part)] = got[2, at, lanes]

        self.loads[2].wait()
        self.copies[2].wait_recv()
        add_into(self.out_down.shape[0], self.out_down, self.downs.at[0], self.downs.at[1])


def grads_scratch(slab, columns, rows, width):
    return [
        pltpu.VMEM((3, slab, columns), bf16),
        pltpu.VMEM((3, slab, columns), bf16),
        pltpu.VMEM((2, rows, width), bf16),
        pltpu.SemaphoreType.DMA((3,)),
    ]


def grads_shapes(grad_gate_up, grad_down):
    slab, columns = grad_gate_up.shape[1] // 4, grad_gate_up.shape[2]
    rows, width = grad_down.shape[1] // 2, grad_down.shape[2]
    return (
        [jax.ShapeDtypeStruct((slab, 2 * columns), bf16), jax.ShapeDtypeStruct((rows, width), bf16)],
        grads_scratch(slab, columns, rows, width),
    )


def neighbours(half):
    e, z = lax.axis_index("expert"), lax.axis_index("dp")
    across = lax.rem(z + half, lax.axis_size("dp"))
    return [{"expert": flip(e, m)} for m in (1, 2, 4)] + [{"dp": across}]


class Several:
    def __init__(self, copies):
        self.copies = copies

    def wait_recv(self):
        for copy in self.copies:
            copy.wait_recv()


def exchange_plane(wire, partners, near, far, begin=None):
    core, side_x, side_y, across = partners

    def cut(ref, h):
        rows = ref.shape[0] // 2
        return ref.at[pl.ds(h * rows, rows)]

    def start(src, dst, to, h=None):
        if h is not None:
            src, dst = [[cut(ref, h) for ref in refs] for refs in (src, dst)]
        return Several([wire.start(x, y, to) for x, y in zip(src, dst)])

    z_low = start(near[0], far[0], across, 0)
    z_high = start(near[0], far[0], across, 1)
    near_x_low = start(near[0], near[2], side_x, 0)
    near_y_high = start(near[0], near[4], side_y, 1)
    near_x_high = start(near[0], near[2], side_x, 1)
    near_y_low = start(near[0], near[4], side_y, 0)
    last = [start(near[0], near[1], core)]
    cargo = begin() if begin else None
    near_x_low.wait_recv()
    near_diag_low = start(near[2], near[6], side_y, 0)
    near_y_high.wait_recv()
    near_diag_high = start(near[4], near[6], side_x, 1)
    near_x_high.wait_recv()
    last.append(start(near[2], near[3], core))
    near_y_low.wait_recv()
    last.append(start(near[4], near[5], core))
    z_low.wait_recv()
    far_x_low = start(far[0], far[2], side_x, 0)
    far_y_low = start(far[0], far[4], side_y, 0)
    near_diag_low.wait_recv()
    near_diag_high.wait_recv()
    last.append(start(near[6], near[7], core))
    z_high.wait_recv()
    far_x_high = start(far[0], far[2], side_x, 1)
    far_y_high = start(far[0], far[4], side_y, 1)
    last.append(start(far[0], far[1], core))
    far_x_low.wait_recv()
    far_diag_low = start(far[2], far[6], side_y, 0)
    far_y_low.wait_recv()
    far_y_high.wait_recv()
    far_diag_high = start(far[4], far[6], side_x, 1)
    last.append(start(far[4], far[5], core))
    far_x_high.wait_recv()
    last.append(start(far[2], far[3], core))
    far_diag_low.wait_recv()
    far_diag_high.wait_recv()
    last.append(start(far[6], far[7], core))
    for copy in last:
        copy.wait_recv()
    if cargo:
        cargo.finish()


def plane_gather_kernel(half, experts, count, *refs):
    inputs, refs = refs[:count], refs[count:]
    if experts:
        (w_gate_up, w_down), refs = refs[:2], refs[4:]
    outs, refs = refs[: 15 * count], refs[15 * count :]
    near = [list(inputs)] + [list(outs[j * count : (j + 1) * count]) for j in range(7)]
    far = [list(outs[j * count : (j + 1) * count]) for j in range(7, 15)]
    wire = Wire(*refs[-2:])
    partners = neighbours(half)
    begin = None
    if experts:
        greet(partners + [{"dp": plane_places()[1]}])
        begin = lambda: WeightsIn(wire, experts, w_gate_up, w_down, *refs[:5])
    else:
        greet(partners)
    exchange_plane(wire, partners, near, far, begin)
    wire.finish()


def plane_gather(inputs, half, number, name, experts=(), weights=(), filled=()):
    count, size = len(inputs), inputs[0].size
    blocks = [jax.ShapeDtypeStruct(x.shape, x.dtype) for x in inputs]
    scratch, aliases = [], {}
    if experts:
        (w_gate_up, w_down), (gate_up, down) = weights, filled
        scratch = weights_scratch(
            len(experts), w_gate_up.shape[1], gate_up.shape[2], w_down.shape[1], down.shape[2]
        )
        aliases = {count + 2: 15 * count, count + 3: 15 * count + 1}
    out = comm_call(
        functools.partial(plane_gather_kernel, half, experts, count),
        name,
        number,
        22 * count + 6 * len(experts),
        [ANYWHERE] * (count + len(weights) + len(filled)),
        [ANYWHERE] * (15 * count + len(filled)),
        blocks * 15 + [jax.ShapeDtypeStruct(x.shape, x.dtype) for x in filled],
        scratch,
        80 * size,
        aliases,
    )(*inputs, *weights, *filled)
    pairs = []
    for n, x in enumerate(inputs):
        own = out[n : 15 * count : count]
        pairs.append(([x] + list(own[:7]), list(own[7:])))
    return pairs, out[15 * count :]


def plane_scatter_kernel(half, *refs):
    parts = {"near": refs[:8], "far": refs[8:16]}
    out, core_in, sums, diag_in, last_in, z_out, z_in = refs[16:23]
    wire = Wire(*refs[23:])
    core, side_x, side_y, across = partners = neighbours(half)
    rows = out.shape[0] // 2
    cut = rows // 2
    low, high = pl.ds(0, cut), pl.ds(cut, cut)
    greet(partners)
    segments = [(kind, h) for kind in ("far", "near") for h in range(2)]
    from_core, from_diag, from_last, from_z = {}, {}, {}, {}

    def part(s, j):
        kind, h = segments[s]
        return parts[kind][j].at[pl.ds(h * rows, rows)]

    for s in range(4):
        for k in (3, 1, 2, 0):
            from_core[s, k] = wire.start(part(s, 2 * k + 1), core_in.at[s, k], core)

    def chip_sum(s, k):
        from_core[s, k].wait_recv()
        add_into(rows, sums.at[s, k], part(s, 2 * k), core_in.at[s, k])

    def enter(s):
        chip_sum(s, 3)
        from_diag[s, 0] = wire.start(sums.at[s, 3, low], diag_in.at[s, 0], side_x)
        from_diag[s, 1] = wire.start(sums.at[s, 3, high], diag_in.at[s, 1], side_y)
        chip_sum(s, 1)
        from_last[s, 0] = wire.start(sums.at[s, 1, low], last_in.at[s, 0, low], side_x)
        chip_sum(s, 2)
        from_last[s, 1] = wire.start(sums.at[s, 2, high], last_in.at[s, 1, high], side_y)

    def turn(s):
        from_diag[s, 1].wait_recv()
        add_into(cut, sums.at[s, 1, high], sums.at[s, 1, high], diag_in.at[s, 1])
        from_last[s, 2] = wire.start(sums.at[s, 1, high], last_in.at[s, 0, high], side_x)
        from_diag[s, 0].wait_recv()
        add_into(cut, sums.at[s, 2, low], sums.at[s, 2, low], diag_in.at[s, 0])
        from_last[s, 3] = wire.start(sums.at[s, 2, low], last_in.at[s, 1, low], side_y)

    def leave(s):
        kind, h = segments[s]
        from_core[s, 0].wait_recv()
        for i in range(4):
            from_last[s, i].wait_recv()
        target = z_out.at[h] if kind == "far" else out.at[pl.ds(h * rows, rows)]
        add_into(rows, target, part(s, 0), core_in.at[s, 0], last_in.at[s, 0], last_in.at[s, 1])
        if kind == "far":
            from_z[h] = wire.start(z_out.at[h], z_in.at[h], across)

    for step, s in (
        (enter, 0),
        (enter, 1),
        (turn, 0),
        (enter, 2),
        (turn, 1),
        (leave, 0),
        (enter, 3),
        (leave, 1),
        (turn, 2),
        (turn, 3),
        (leave, 2),
        (leave, 3),
    ):
        step(s)
    for h in range(2):
        from_z[h].wait_recv()
        target = out.at[pl.ds(h * rows, rows)]
        add_into(rows, target, target, z_in.at[h])
    wire.finish()


def plane_scatter(near, far, half, number, name):
    rows, width = near[0].shape
    specs = [ON_CHIP, ANYWHERE] * 8
    block = (rows // 2, width)
    return comm_call(
        functools.partial(plane_scatter_kernel, half),
        name,
        number,
        42,
        specs,
        ON_CHIP,
        jax.ShapeDtypeStruct((rows, width), f32),
        [
            pltpu.VMEM((4, 4) + block, bf16),
            pltpu.VMEM((4, 4) + block, bf16),
            pltpu.VMEM((4, 2, rows // 4, width), bf16),
            pltpu.VMEM((4, 2) + block, bf16),
            pltpu.VMEM((2,) + block, bf16),
            pltpu.VMEM((2,) + block, bf16),
        ],
        50 * rows * width,
    )(*near, *far)


def chip_partners():
    e = lax.axis_index("expert")
    return [{"expert": flip(e, m)} for m in (1, 2)]


def exchange_seq(wire, group, x_ref, out, between=None, steps=()):
    head = lax.rem(lax.axis_index("expert"), group)
    core, side_x = chip_partners()
    rows = x_ref.shape[0]
    cut = rows // 2
    mine = pl.multiple_of(head * rows, rows)
    other = pl.multiple_of(flip(head, 2) * rows, rows)
    crossing = [
        wire.start(x_ref.at[pl.ds(h * cut, cut)], out.at[pl.ds(mine + h * cut, cut)], side_x)
        for h in range(2)
    ]
    last = [wire.start(x_ref, out.at[pl.ds(mine, rows)], core)]
    out[pl.ds(mine, rows), :] = x_ref[...]
    if between:
        between()
    for h in range(2):
        if steps:
            steps[h]()
        crossing[h].wait_recv()
        piece = out.at[pl.ds(other + h * cut, cut)]
        last.append(wire.start(piece, piece, core))
    if steps:
        steps[2]()
    for copy in last:
        copy.wait_recv()


def seq_gather_kernel(group, x_ref, out, send_sem, recv_sem):
    wire = Wire(send_sem, recv_sem)
    greet(chip_partners())
    exchange_seq(wire, group, x_ref, out)
    wire.finish()


def seq_gather(x, group, number, name):
    rows, width = x.shape
    return comm_call(
        functools.partial(seq_gather_kernel, group),
        name,
        number,
        5,
        [ON_CHIP],
        ON_CHIP,
        jax.ShapeDtypeStruct((group * rows, width), x.dtype),
        [],
        20 * x.size,
    )(x)


def sum_seq(wire, group, x_ref, out, core_in, sums, last_in, between=None):
    head = lax.rem(lax.axis_index("expert"), group)
    core, side_x = chip_partners()
    rows = out.shape[0]
    cut = rows // 2

    def part(block, h):
        return x_ref.at[pl.ds(pl.multiple_of(block * rows + h * cut, cut), cut)]

    crossing = [
        wire.start(part(flip(flip(head, 2), 1), h), core_in.at[1, h], core) for h in range(2)
    ]
    near = [wire.start(part(flip(head, 1), h), core_in.at[0, h], core) for h in range(2)]
    last = []
    for h in range(2):
        crossing[h].wait_recv()
        add_into(cut, sums.at[h], part(flip(head, 2), h), core_in.at[1, h])
        last.append(wire.start(sums.at[h], last_in.at[h], side_x))
    if between:
        between()
    for h in range(2):
        near[h].wait_recv()
        last[h].wait_recv()
        add_into(
            cut, out.at[pl.ds(h * cut, cut)], part(head, h), core_in.at[0, h], last_in.at[h]
        )


def seq_scatter_kernel(group, x_ref, out, core_in, sums, last_in, send_sem, recv_sem):
    wire = Wire(send_sem, recv_sem)
    greet(chip_partners())
    sum_seq(wire, group, x_ref, out, core_in, sums, last_in)
    wire.finish()


def seq_scratch(rows, width):
    piece = (rows // 2, width)
    return [
        pltpu.VMEM((2, 2) + piece, bf16),
        pltpu.VMEM((2,) + piece, bf16),
        pltpu.VMEM((2,) + piece, bf16),
    ]


def seq_scatter(x, group, number, name):
    rows, width = x.shape[0] // group, x.shape[1]
    return comm_call(
        functools.partial(seq_scatter_kernel, group),
        name,
        number,
        6,
        [ON_CHIP],
        ON_CHIP,
        jax.ShapeDtypeStruct((rows, width), f32),
        seq_scratch(rows, width),
        20 * rows * width,
    )(x)


def entry_kernel(group, x_ref, qkv_in, out_in, seq, qkv, out_slice, send_sem, recv_sem):
    wire = Wire(send_sem, recv_sem)
    e, z = lax.axis_index("expert"), lax.axis_index("dp")
    head, row = lax.rem(e, group), lax.div(e, group)
    side_y = {"expert": flip(e, 4)}
    top = 3
    slab = qkv_in.shape[0]
    cut = slab // 2
    greet(chip_partners() + [side_y] + [{"dp": lax.rem(z + k, 4)} for k in range(1, 4)])
    mine = pl.ds(pl.multiple_of(row * cut, cut), cut)

    def spot(plane):
        return qkv.at[pl.ds(pl.multiple_of(plane * slab + row * cut, cut), cut)]

    def copy(n, src, dst, to):
        return pltpu.make_async_remote_copy(
            src_ref=src,
            dst_ref=dst,
            send_sem=send_sem.at[n],
            recv_sem=recv_sem.at[n],
            device_id=to,
            device_id_type=MESH,
        )

    up, down = {"dp": lax.rem(z + 1, 4)}, {"dp": lax.rem(z + 3, 4)}
    hops = []
    for sign, to in ((1, up), (-1, down)):
        for d in (1, 2, 3):
            n = 5 + len(hops) * 2
            held, got = lax.rem(z - sign * (d - 1) + 8, 4), lax.rem(z - sign * d + 8, 4)
            source = qkv_in.at[mine] if d == 1 else spot(held)
            edge = z < top if sign > 0 else z > 0
            held_there = z >= d - 1 if sign > 0 else z <= top - (d - 1)
            arrives = z >= d if sign > 0 else z <= top - d
            hops.append(
                (
                    jnp.logical_and(edge, held_there),
                    arrives,
                    copy(n, source, spot(held), to),
                    copy(n + 1, spot(got), spot(got), side_y),
                )
            )
    for sends, _, hop, _ in (hops[0], hops[3]):
        pl.when(sends)(hop.start)

    owner = z == head
    out_up = copy(17, out_slice.at[mine], out_slice.at[mine], up)
    out_down = copy(18, out_slice.at[mine], out_slice.at[mine], down)
    own_up = copy(17, out_in.at[mine], out_slice.at[mine], up)
    own_down = copy(18, out_in.at[mine], out_slice.at[mine], down)
    swap = copy(19, out_slice.at[mine], out_slice.at[mine], side_y)
    pl.when(jnp.logical_and(owner, z < top))(own_up.start)
    pl.when(jnp.logical_and(owner, z > 0))(own_down.start)

    @pl.when(owner)
    def _():
        out_slice[...] = out_in[...]

    qkv[pl.ds(pl.multiple_of(z * slab, slab), slab), :] = qkv_in[...]

    def relay(d):
        for way in (0, 3):
            _, arrives, hop, across = hops[way + d]

            @pl.when(arrives)
            def _():
                hop.wait_recv()
                across.start()

            if d < 2:
                sends, _, following, _ = hops[way + d + 1]
                pl.when(sends)(following.start)

        @pl.when(z == head + d + 1)
        def _():
            out_up.wait_recv()
            pl.when(z < top)(out_up.start)
            swap.start()

        @pl.when(z == head - d - 1)
        def _():
            out_down.wait_recv()
            pl.when(z > 0)(out_down.start)
            swap.start()

    steps = [functools.partial(relay, d) for d in range(3)]
    exchange_seq(wire, group, x_ref, seq, steps=steps)
    for sends, arrives, hop, across in hops:
        pl.when(arrives)(across.wait)
        pl.when(sends)(hop.wait_send)
    pl.when(jnp.logical_not(owner))(swap.wait)
    pl.when(jnp.logical_and(z >= head, z < top))(out_up.wait_send)
    pl.when(jnp.logical_and(z <= head, z > 0))(out_down.wait_send)
    wire.finish()


def attention_entry(x, qkv_slice, w_out, group):
    rows, width = x.shape
    slab, columns = qkv_slice.shape
    return comm_call(
        functools.partial(entry_kernel, group),
        "attention_entry",
        8,
        20,
        [ON_CHIP] * 3,
        [ON_CHIP] * 3,
        [
            jax.ShapeDtypeStruct((group * rows, width), bf16),
            jax.ShapeDtypeStruct((4 * slab, columns), bf16),
            jax.ShapeDtypeStruct((slab, width), bf16),
        ],
        [],
        40 * x.size,
    )(x, qkv_slice, w_out)


def scatter_weights_kernel(group, experts, x_ref, w_gate_up, w_down, out, gate_up, down, *refs):
    wire = Wire(*refs[6:])
    _, beside, opposite, _, _ = plane_places()
    greet(chip_partners() + [{"dp": p} for p in (beside, opposite, flip(opposite, 1))])
    cargo = WeightsIn(wire, experts, w_gate_up, w_down, gate_up, down, *refs[3:6], direct=True)
    sum_seq(wire, group, x_ref, out, *refs[:3])
    cargo.finish()
    wire.finish()


def seq_scatter_weights(x, group, experts, w_gate_up, w_down):
    rows, width = x.shape[0] // group, x.shape[1]
    count, slab, columns = w_gate_up.shape
    ff_rows = w_down.shape[1]
    return comm_call(
        functools.partial(scatter_weights_kernel, group, experts),
        "scatter_branch_weights",
        9,
        6 + 7 * len(experts),
        [ON_CHIP, ANYWHERE, ANYWHERE],
        [ON_CHIP, ANYWHERE, ANYWHERE],
        [
            jax.ShapeDtypeStruct((rows, width), f32),
            jax.ShapeDtypeStruct((count, 4 * slab, columns // 2), bf16),
            jax.ShapeDtypeStruct((count, 2 * ff_rows, width), bf16),
        ],
        seq_scratch(rows, width)
        + weights_scratch(len(experts), slab, columns // 2, ff_rows, width),
        40 * rows * width,
    )(x, w_gate_up, w_down)


def gather_grads_kernel(group, i, x_ref, grad_gate_up, grad_down, seq, out, out_down, *refs):
    wire = Wire(*refs[4:])
    _, beside, opposite, _, _ = plane_places()
    greet(chip_partners() + [{"dp": beside}, {"dp": opposite}])
    cargo = GradsOut(wire, i, grad_gate_up, grad_down, out, out_down, *refs[:4])
    exchange_seq(wire, group, x_ref, seq, cargo.cross)
    cargo.finish()
    wire.finish()


def seq_gather_grads(x, group, i, grad_gate_up, grad_down):
    rows, width = x.shape
    shapes, scratch = grads_shapes(grad_gate_up, grad_down)
    return comm_call(
        functools.partial(gather_grads_kernel, group, i),
        "gather_branch_grads",
        10,
        9,
        [ON_CHIP, ANYWHERE, ANYWHERE],
        [ON_CHIP] * 3,
        [jax.ShapeDtypeStruct((group * rows, width), x.dtype)] + shapes,
        scratch,
        40 * x.size,
    )(x, grad_gate_up, grad_down)


def scatter_grads_kernel(group, i, x_ref, grad_gate_up, grad_down, total, out, out_down, *refs):
    wire = Wire(*refs[7:])
    _, beside, opposite, _, _ = plane_places()
    greet(chip_partners() + [{"dp": beside}, {"dp": opposite}])
    cargo = GradsOut(wire, i, grad_gate_up, grad_down, out, out_down, *refs[3:7])
    sum_seq(wire, group, x_ref, total, *refs[:3], cargo.cross)
    cargo.finish()
    wire.finish()


def seq_scatter_grads(x, group, i, grad_gate_up, grad_down):
    rows, width = x.shape[0] // group, x.shape[1]
    shapes, scratch = grads_shapes(grad_gate_up, grad_down)
    return comm_call(
        functools.partial(scatter_grads_kernel, group, i),
        "scatter_normed_grads",
        11,
        10,
        [ON_CHIP, ANYWHERE, ANYWHERE],
        [ON_CHIP] * 3,
        [jax.ShapeDtypeStruct((rows, width), f32)] + shapes,
        seq_scratch(rows, width) + scratch,
        40 * rows * width,
    )(x, grad_gate_up, grad_down)


def start_kernel(replicas, small_ref, small_out, send_sem, recv_sem):
    wire = Wire(send_sem, recv_sem)
    z = lax.axis_index("dp")
    planes = [{"dp": lax.rem(z + k, replicas)} for k in range(1, replicas)]
    greet(planes)
    spread = [wire.start(small_ref, small_out.at[z], plane) for plane in planes]
    small_out[z] = small_ref[...]
    for copy in spread:
        copy.wait_recv()
    wire.finish()


def start_exchange(small, replicas):
    return comm_call(
        functools.partial(start_kernel, replicas),
        "start_exchange",
        1,
        replicas - 1,
        [ON_CHIP],
        ON_CHIP,
        jax.ShapeDtypeStruct((replicas,) + small.shape, small.dtype),
        [],
        10**6,
    )(small)


def dense_kernel(
    replicas, i, grads, small, grad_gate_up, grad_down, out, small_out, cargo_out, cargo_down, *refs
):
    y_in, z_out, z_in, small_in, small_sum, turn_in = refs[:6]
    wire = Wire(*refs[10:])
    e, z = lax.axis_index("expert"), lax.axis_index("dp")
    head, row = lax.rem(e, 4), lax.div(e, 4)
    partners = [{"expert": flip(e, m)} for m in (1, 2, 4)]
    core, side_x, side_y = partners
    slab, width = grads.shape[0] // replicas, grads.shape[1]
    cut = slab // 2
    quarter = cut // 2
    order = [2, 1, 3, 0]
    block = {k: lax.rem(z + k, replicas) for k in range(replicas)}
    plane = {k: {"dp": block[k]} for k in range(1, replicas)}
    greet(partners + list(plane.values()))

    def half_of(k, which):
        return grads.at[pl.ds(pl.multiple_of(block[k] * slab + which * cut, cut), cut)]

    small_copies = [wire.start(small.at[block[k]], small_in.at[k - 1], plane[k]) for k in plane]
    from_y = {k: wire.start(half_of(k, 1 - row), y_in.at[k], side_y) for k in order}
    cargo = GradsOut(wire, i, grad_gate_up, grad_down, cargo_out, cargo_down, *refs[6:10])
    for copy in small_copies:
        copy.wait_recv()
    small_sum[0] = small[z] + small_in[0] + small_in[1] + small_in[2]
    turn = wire.start(small_sum.at[0], turn_in.at[0], core)
    from_z = {}
    for step, k in enumerate(order):
        from_y[k].wait_recv()
        add_into(cut, z_out.at[k], half_of(k, row), y_in.at[k])
        if k:
            from_z[k] = wire.start(z_out.at[k], z_in.at[k - 1], plane[k])
        if step == 0:
            turn.wait_recv()
            small_sum[1] = small_sum[0] + turn_in[0]
            turn = wire.start(small_sum.at[1], turn_in.at[1], side_x)
        if step == 1:
            turn.wait_recv()
            small_sum[2] = small_sum[1] + turn_in[1]
            turn = wire.start(small_sum.at[2], turn_in.at[2], side_y)
    turn.wait_recv()
    small_out[...] = small_sum[2] + turn_in[2]
    cargo.cross()
    for k in from_z:
        from_z[k].wait_recv()

    def place(which_head, which_row, first=0, size=cut):
        start = pl.multiple_of(which_row * cut + first, quarter)
        columns = pl.ds(pl.multiple_of(which_head * width, 128), width)
        return out.at[pl.ds(start, size), columns]

    mine = place(head, row)
    add_into(cut, mine, z_out.at[0], z_in.at[0], z_in.at[1], z_in.at[2])
    other = flip(head, 2)
    pieces = [place(head, row, h * quarter, quarter) for h in range(2)]
    over_x = [wire.start(piece, piece, side_x) for piece in pieces]
    over_y = [wire.start(piece, piece, side_y) for piece in reversed(pieces)]
    last = [wire.start(mine, mine, core)]
    over_x[0].wait_recv()
    piece = place(other, row, 0, quarter)
    diag = [wire.start(piece, piece, side_y)]
    over_y[0].wait_recv()
    piece = place(head, 1 - row, quarter, quarter)
    diag.append(wire.start(piece, piece, side_x))
    over_x[1].wait_recv()
    last.append(wire.start(place(other, row), place(other, row), core))
    over_y[1].wait_recv()
    last.append(wire.start(place(head, 1 - row), place(head, 1 - row), core))
    for copy in diag:
        copy.wait_recv()
    last.append(wire.start(place(other, 1 - row), place(other, 1 - row), core))
    for copy in last:
        copy.wait_recv()
    cargo.finish()
    wire.finish()


def dense_reduce(grads, small, replicas, i, grad_gate_up, grad_down):
    slab, width = grads.shape[0] // replicas, grads.shape[1]
    piece = (slab // 2, width)
    lot = small.shape[1:]
    shapes, scratch = grads_shapes(grad_gate_up, grad_down)
    return comm_call(
        functools.partial(dense_kernel, replicas, i),
        "dense_reduce",
        2,
        27,
        [ON_CHIP] * 2 + [ANYWHERE] * 2,
        [ON_CHIP] * 4,
        [jax.ShapeDtypeStruct((slab, 4 * width), bf16), jax.ShapeDtypeStruct(lot, f32)] + shapes,
        [
            pltpu.VMEM((4,) + piece, bf16),
            pltpu.VMEM((4,) + piece, bf16),
            pltpu.VMEM((3,) + piece, bf16),
            pltpu.VMEM((3,) + lot, f32),
            pltpu.VMEM((3,) + lot, f32),
            pltpu.VMEM((3,) + lot, f32),
        ]
        + scratch,
        10**8,
    )(grads, small, grad_gate_up, grad_down)


STRIP = 256


def strips(ref_rows):
    return [(b * STRIP, (b + 1) * STRIP) for b in range(ref_rows // STRIP)]


def head_rows(index):
    return pl.ds(pl.multiple_of(index * HD, HD), HD)


def scores_of(keys, queries, first):
    raw = dg(keys, queries, TN)
    key = lax.broadcasted_iota(jnp.int32, raw.shape, 0)
    query = lax.broadcasted_iota(jnp.int32, raw.shape, 1) + first
    raw = jnp.where(key <= query, raw, NEG)
    grown = jnp.exp(raw - jnp.max(raw, axis=0, keepdims=True))
    return grown * (1.0 / jnp.sum(grown, axis=0, keepdims=True))


def attend_kernel(q_ref, k_ref, v_ref, out_ref):
    group = q_ref.shape[0] // k_ref.shape[0]

    @pl.loop(0, q_ref.shape[0] // HD)
    def _(h):
        mine, shared = head_rows(h), head_rows(lax.div(h, group))
        for first, last in strips(q_ref.shape[1]):
            probs = scores_of(k_ref[shared, :last], q_ref[mine, first:last], first)
            out = dg(v_ref[shared, :last], probs.astype(bf16), NN)
            out_ref[mine, first:last] = out.astype(bf16)


def attend_back_kernel(q_ref, k_ref, v_ref, grad_ref, dq_ref, dk_ref, dv_ref):
    group = q_ref.shape[0] // k_ref.shape[0]
    dk_ref[...] = jnp.zeros_like(dk_ref)
    dv_ref[...] = jnp.zeros_like(dv_ref)

    @pl.loop(0, q_ref.shape[0] // HD)
    def _(h):
        mine, shared = head_rows(h), head_rows(lax.div(h, group))
        for first, last in strips(q_ref.shape[1]):
            queries, grad = q_ref[mine, first:last], grad_ref[mine, first:last]
            keys = k_ref[shared, :last]
            probs = scores_of(keys, queries, first)
            grad_probs = dg(v_ref[shared, :last], grad, TN)
            delta = jnp.sum(probs * grad_probs, axis=0, keepdims=True)
            grad_scores = (probs * (grad_probs - delta)).astype(bf16)
            dq_ref[mine, first:last] = dg(keys, grad_scores, NN) * SCORE_SCALE
            dk_ref[shared, :last] += dg(queries, grad_scores, NT)
            dv_ref[shared, :last] += dg(grad, probs.astype(bf16), NT)


def on_chip_call(kernel, name, inputs, shapes, flops):
    return pl.pallas_call(
        kernel,
        in_specs=[ON_CHIP] * len(inputs),
        out_specs=[ON_CHIP] * len(shapes),
        out_shape=shapes,
        compiler_params=params(60),
        cost_estimate=pl.CostEstimate(
            flops=flops, bytes_accessed=10**7, transcendentals=4 * 10**6
        ),
        name=name,
    )(*inputs)


def attend(queries, keys, values):
    shapes = [jax.ShapeDtypeStruct(queries.shape, bf16)]
    return on_chip_call(attend_kernel, "attend", (queries, keys, values), shapes, 10**10)[0]


def attend_back(queries, keys, values, grad_context):
    shapes = [jax.ShapeDtypeStruct(x.shape, f32) for x in (queries, keys, values)]
    inputs = (queries, keys, values, grad_context)
    return on_chip_call(attend_back_kernel, "attend_back", inputs, shapes, 3 * 10**10)


def turned(x, cosine, sine):
    x = x.reshape(-1, 2, HD // 2, x.shape[1])
    first, second = x[:, 0], x[:, 1]
    out = jnp.stack([first * cosine - second * sine, second * cosine + first * sine], axis=1)
    return out.reshape(-1, x.shape[3])


def body(
    hidden_in,
    teacher,
    valid,
    routes,
    gain_attn,
    gain_moe,
    w_query,
    w_key,
    w_value,
    w_out,
    w_router,
    w_gate_up,
    w_down,
):
    tok, width = hidden_in.shape
    owners = lax.axis_size("expert")
    replicas = lax.axis_size("dp")
    me = lax.axis_index("expert")
    plane = lax.axis_index("dp")
    length = min(SEQ_MIN, owners * tok)
    group = length // tok
    head = me % group
    experts_all = EXP_DEV * owners
    slots = 8 * ((tok * TOP + experts_all * 7 - 1) // (experts_all * 7))
    half = replicas // 2
    side = plane // half
    ff_half = FF // 2
    slab = width // replicas
    q_cols = H * HD // group
    kv_cols = KVH * HD // group

    def over_dp(x, axis):
        if replicas > group:
            return lax.all_gather(x, "dp", axis=axis, tiled=True)
        return place(
            [x] + [send(x, "dp", m) for m in range(1, replicas)],
            [plane ^ m for m in range(replicas)],
            axis,
            replicas,
        )

    routes_t = jnp.transpose(routes)
    count = jnp.full_like(routes_t, jnp.sum(valid))
    small = jnp.concatenate(
        [gain_attn[None], gain_moe[None], jnp.transpose(w_router), jnp.zeros((6, slab), bf16)]
    )
    names = jnp.concatenate([routes_t, count])
    small = start_exchange(small, replicas)
    small = jnp.transpose(small, (1, 0, 2)).reshape(small.shape[1], width)
    gain_one, gain_two, router_t = small[0], small[1], small[2 : 2 + experts_all]
    me_ref = jnp.reshape(me, (1,)).astype(jnp.int32)
    valid_float = valid.astype(f32)
    qkv_slice = jnp.concatenate(
        [
            pick(w_query, head, q_cols, 1),
            pick(w_key, head, kv_cols, 1),
            pick(w_value, head, kv_cols, 1),
        ],
        axis=1,
    )
    inputs = hidden_in.astype(f32)
    normed_f, norm_one_pull = jax.vjp(rms_norm, inputs, gain_one.astype(f32))
    normed = normed_f.astype(bf16)
    compact = replicas == group

    def on_grid(x, pairs):
        return lax.ppermute(x, ("dp", "expert"), pairs)

    if compact:
        seq, qkv, out_slice = attention_entry(normed, qkv_slice, w_out, group)
    else:
        seq = seq_gather(normed, group, 3, "gather_normed")
        qkv = over_dp(qkv_slice, 0)
        out_slice = pick(lax.all_gather(w_out, "dp", axis=0, tiled=True), head, q_cols, 0)

    lin = mm("td,dc->ct", seq, qkv)
    cosine, sine = rope_tables(jnp.arange(length, dtype=f32))
    queries = turned(lin[:q_cols], cosine, sine).astype(bf16) * jnp.asarray(SCORE_SCALE, bf16)
    keys = turned(lin[q_cols : q_cols + kv_cols], cosine, sine).astype(bf16)
    values = lin[q_cols + kv_cols :].astype(bf16)
    context = attend(queries, keys, values)
    branch = mm("ct,cd->td", context, out_slice).astype(bf16)
    if compact:
        summed, gate_up_w, down_w = seq_scatter_weights(branch, group, (0,), w_gate_up, w_down)
    else:
        summed = seq_scatter(branch, group, 4, "scatter_branch")
        gate_up_all = lax.all_gather(w_gate_up, "dp", axis=1, tiled=True)
        gate_up_w = jnp.concatenate(
            [pick(gate_up_all, p * 2 + side, ff_half, 2) for p in range(2)], axis=2
        )
        down_w = pick(lax.all_gather(w_down, "dp", axis=1, tiled=True), side, ff_half, 1)
    mid = inputs + RESIDUAL * summed
    moe_f, norm_two_pull = jax.vjp(rms_norm, mid, gain_two.astype(f32))
    moe_input = moe_f.astype(bf16)

    if compact:
        blocks, (gate_up_w, down_w) = plane_gather(
            [moe_input, names],
            half,
            12,
            "gather_all",
            (1, 2),
            (w_gate_up, w_down),
            (gate_up_w, down_w),
        )
    else:
        blocks, _ = plane_gather([moe_input, names], half, 13, "gather_names")
    (near, far), (near_names, far_names) = blocks
    near_parts, near_kept, near_count = experts_forward(
        me_ref, near_names, router_t, near, gate_up_w, down_w
    )
    far_parts, far_kept, far_count = experts_forward(
        me_ref, far_names, router_t, far, gate_up_w, down_w
    )
    valid_count = near_count[0, :1] + far_count[0, :1]
    mask = 1
    while mask < half:
        valid_count = valid_count + send(valid_count, "dp", mask)
        mask *= 2
    valid_count = valid_count[0].astype(f32)
    final_state = mid + RESIDUAL * plane_scatter(near_parts, far_parts, half, 6, "scatter_outputs")
    activations = final_state.astype(bf16)
    mismatch = final_state - teacher.astype(f32)
    squares = jnp.sum(0.5 * valid_float[:, None] * mismatch * mismatch)
    tokens_all = tok * replicas * owners
    grad_final = tokens_all / valid_count * valid_float[:, None] * mismatch

    ((grad_near, grad_far),), _ = plane_gather([grad_final.astype(bf16)], half, 5, "gather_tokens")

    def back(kept, blocks):
        arrived, lin, weighted, slot, gate = kept
        parts, (grads, lin_grad) = experts_backward(
            me_ref, slot, gate, lin, blocks, gate_up_w, down_w
        )
        return parts, (arrived, lin_grad, weighted, grads)

    near_grads, near_chunk = back(near_kept, grad_near)
    far_grads, far_chunk = back(far_kept, grad_far)
    returned = plane_scatter(near_grads, far_grads, half, 7, "scatter_grads")
    after = jnp.reshape(never(returned[0, 0]), (1,))
    grad_gate_up, grad_down = expert_weights(after, [near_chunk, far_chunk])
    branch_scale = jnp.where(never(grad_down[0, 0, 0]) == 0, RESIDUAL, 0.0)

    grad_gates = returned[:, width : width + experts_all]
    own_routed = jnp.any(
        routes[:, :, None] == jnp.arange(experts_all, dtype=jnp.int32), axis=1
    )
    own_logits = jnp.where(own_routed, mm("td,ed->te", moe_input, router_t), NEG)
    own_gates = jnp.where(own_routed, jax.nn.softmax(own_logits, axis=-1), 0.0)
    grad_logits = (
        own_gates * (grad_gates - jnp.sum(own_gates * grad_gates, axis=-1, keepdims=True))
    ).astype(bf16)
    grad_router_t = mm("td,te->ed", moe_input, grad_logits)
    grad_moe_input = returned[:, :width] + mm("te,ed->td", grad_logits, router_t)
    grad_mid_norm, grad_gain_two = norm_two_pull(grad_moe_input)
    grad_mid = grad_final + grad_mid_norm
    grad_branch = (branch_scale * grad_mid).astype(bf16)

    done = []
    if compact:
        seq_grad, *part = seq_gather_grads(grad_branch, group, 0, grad_gate_up, grad_down)
        done.append(part)
    else:
        seq_grad = seq_gather(grad_branch, group, 3, "gather_normed")
    grad_out = mm("ct,td->cd", context, seq_grad).astype(bf16)
    if compact:
        out_sum = grad_out.astype(f32)
        for step in range(1, replicas):
            pairs = [
                (
                    ((i % group + step) % replicas) * owners + i,
                    (i % group) * owners + i,
                )
                for i in range(owners)
            ]
            out_sum = out_sum + on_grid(grad_out, pairs).astype(f32)
        entered = jnp.where(never(out_sum[0, 0]) == 0, 1.0, 0.0)
    grad_context = mm("td,cd->ct", seq_grad, out_slice).astype(bf16)
    grad_q, grad_k, grad_v = attend_back(queries, keys, values, grad_context)
    grad_lin = jnp.concatenate(
        [turned(grad_q, cosine, -sine), turned(grad_k, cosine, -sine), grad_v]
    ).astype(bf16)
    grad_qkv = mm("td,ct->dc", seq, grad_lin).astype(bf16)
    normed_parts = mm("ct,dc->td", grad_lin, qkv)
    normed_parts = (entered * normed_parts if compact else normed_parts).astype(bf16)
    if compact:
        grad_normed, *part = seq_scatter_grads(normed_parts, group, 1, grad_gate_up, grad_down)
        done.append(part)
    else:
        grad_normed = seq_scatter(normed_parts, group, 4, "scatter_branch")
    grad_in_norm, grad_gain_one = norm_one_pull(grad_normed)
    grad_in = grad_mid + grad_in_norm

    def other_sequences(x):
        total = x.astype(f32)
        mask = group
        while mask < owners:
            total = total + send(total.astype(bf16), "expert", mask).astype(f32)
            mask *= 2
        return total

    lot = jnp.concatenate(
        [
            grad_router_t,
            grad_gain_one[None],
            grad_gain_two[None],
            jnp.full((6, width), squares),
        ]
    )
    if compact:
        out_sum = other_sequences(out_sum).astype(bf16)
        g_out = jnp.where(plane == head, out_sum, jnp.zeros((), bf16))
        for m in range(1, group):
            pairs = [
                ((i % group) * owners + i, (i % group) * owners + (i ^ m)) for i in range(owners)
            ]
            g_out = g_out + on_grid(out_sum, pairs)
        g_out = g_out.astype(f32)
        lot = jnp.where(never(out_sum[0, 0]) == 0, lot, 0.0)
        lot = jnp.transpose(lot.reshape(32, replicas, slab), (1, 0, 2))
        by_head, lot, *part = dense_reduce(
            grad_qkv, lot, replicas, 2, grad_gate_up, grad_down
        )
        done.append(part)
        gate_up_out, down_out = [jnp.stack(x).astype(f32) for x in zip(*done)]
    else:
        out_sum = other_sequences(lax.psum(grad_out, "dp")).astype(bf16)
        g_out = pick(
            place(
                gather_blocks(out_sum, group), [head ^ j for j in range(group)], 0, group
            ),
            plane,
            slab,
            0,
        ).astype(f32)
        lot = lax.psum_scatter(lot, "dp", scatter_dimension=1, tiled=True)
        lot = lax.psum(lot, "expert")
        qkv_sum = lax.psum_scatter(
            grad_qkv.astype(f32), "dp", scatter_dimension=0, tiled=True
        )
        qkv_sum = other_sequences(qkv_sum).astype(bf16)
        by_head = place(
            gather_blocks(qkv_sum, group), [head ^ j for j in range(group)], 1, group
        )
        spread = lambda x: lax.psum_scatter(
            x.astype(f32), "dp", scatter_dimension=1, tiled=True
        )
        blank = jnp.zeros_like(grad_down)
        down_out = spread(
            jnp.where(
                side == 0,
                jnp.concatenate([grad_down, blank], axis=1),
                jnp.concatenate([blank, grad_down], axis=1),
            )
        )
        first = spread(jnp.where(side == 0, grad_gate_up, jnp.zeros((), bf16)))
        last = spread(jnp.where(side == 1, grad_gate_up, jnp.zeros((), bf16)))
        gate_up_out = jnp.concatenate(
            [
                first[:, :, :ff_half],
                last[:, :, :ff_half],
                first[:, :, ff_half:],
                last[:, :, ff_half:],
            ],
            axis=2,
        )

    def of_heads(first, count):
        wide = q_cols + 2 * kv_cols
        return jnp.concatenate(
            [by_head[:, h * wide + first : h * wide + first + count] for h in range(group)], axis=1
        ).astype(f32)

    g_query = of_heads(0, q_cols)
    g_key = of_heads(q_cols, kv_cols)
    g_value = of_heads(q_cols + kv_cols, kv_cols)
    g_router, g_one, g_two = (
        jnp.transpose(lot[:experts_all]),
        lot[experts_all],
        lot[experts_all + 1],
    )
    loss_value = lot[experts_all + 2, 0] / (valid_count * width)

    return (
        activations,
        loss_value,
        grad_in,
        g_one,
        g_two,
        g_query,
        g_key,
        g_value,
        g_out,
        g_router,
        gate_up_out,
        down_out,
    )


def solution(mesh):
    placed = (
        P(("dp", "expert"), None),
        P(("dp", "expert"), None),
        P(("dp", "expert")),
        P(("dp", "expert"), None),
        P("dp"),
        P("dp"),
        P("dp", None),
        P("dp", None),
        P("dp", None),
        P("dp", None),
        P("dp", None),
        P("expert", "dp", None),
        P("expert", "dp", None),
    )
    return jax.shard_map(
        body,
        mesh=mesh,
        in_specs=placed,
        out_specs=(
            P(("dp", "expert"), None),
            P(),
            P(("dp", "expert"), None),
            P("dp"),
            P("dp"),
            P("dp", None),
            P("dp", None),
            P("dp", None),
            P("dp", None),
            P("dp", None),
            P("expert", "dp", None),
            P("expert", "dp", None),
        ),
        check_vma=False,
    )
```

```python
import functools

import jax
import jax.numpy as jnp
from jax import lax
from jax.experimental import pallas as pl
from jax.experimental.pallas import tpu as pltpu
from jax.sharding import PartitionSpec as P

H = 24
KVH = 8
HD = 64
FF = 512
TOP = 8
EXP_DEV = 3
SEQ_MIN = 1024

EPS = 1e-05
RESIDUAL = 0.22
SCORE_SCALE = 1.0 / 64.0
ROPE_BASE = 10000.0
NEG = -1000000000.0

f32 = jnp.float32
bf16 = jnp.bfloat16


def mm(spec, a, b):
    return jnp.einsum(spec, a, b, preferred_element_type=f32)


def rms_norm(states, gain):
    return states * lax.rsqrt(jnp.mean(states * states, axis=-1, keepdims=True) + EPS) * gain


def rope_tables(positions):
    half_dim = HD // 2
    frequencies = ROPE_BASE ** (-(2.0 * jnp.arange(half_dim, dtype=f32)) / HD)
    angles = frequencies[:, None] * positions[None, :]
    return jnp.cos(angles), jnp.sin(angles)


def send(x, axis, mask):
    count = lax.axis_size(axis)
    return lax.ppermute(x, axis, [(i, i ^ mask) for i in range(count)])


def gather_blocks(x, count):
    blocks = [x]
    for j in range(1, count):
        blocks.append(send(blocks[j - 1], "expert", 1) if j % 2 else send(x, "expert", j))
    return blocks


def scatter_sum(parts):
    total = None
    for j in range(0, len(parts), 2):
        chip = parts[j].astype(f32) + send(parts[j + 1], "expert", 1).astype(f32)
        if j:
            chip = send(chip.astype(bf16), "expert", j).astype(f32)
        total = chip if total is None else total + chip
    return total


def total_over(x, axis):
    mask = 1
    while mask < lax.axis_size(axis):
        x = x + send(x, axis, mask)
        mask *= 2
    return x


def place(blocks, starts, axis, size):
    width = blocks[0].shape[axis]
    shape = list(blocks[0].shape)
    shape[axis] = size * width
    out = jnp.zeros(shape, blocks[0].dtype)
    for block, start in zip(blocks, starts):
        out = lax.dynamic_update_slice_in_dim(out, block, start * width, axis)
    return out


def pick(x, index, width, axis):
    return lax.dynamic_slice_in_dim(x, index * width, width, axis)


def never(x):
    return (x != x).astype(jnp.int32)


CAP = 112
GATE_COLUMNS = 128
NT = (((1,), (1,)), ((), ()))
TN = (((0,), (0,)), ((), ()))
NN = (((1,), (0,)), ((), ()))


def dg(a, b, dims):
    return lax.dot_general(a, b, dims, preferred_element_type=f32)


def whole(shape):
    return pl.BlockSpec(shape, lambda *_: (0,) * len(shape))


def params(mib):
    return pltpu.CompilerParams(vmem_limit_bytes=mib << 20)


def select_rows(slot_row):
    row = lax.broadcasted_iota(jnp.int32, (CAP, slot_row.shape[1]), 0).astype(f32)
    return row == slot_row


def experts_kernel(me_ref, router_ref, gate_up_ref, down_ref, *refs):
    blocks, routes, refs = refs[:8], refs[8:16], refs[16:]
    parts, refs = refs[:8], refs[8:]
    arrived_ref, lin_ref, weighted_ref, slot_ref, gate_ref, count_ref, sel, made = refs
    step = pl.program_id(0)
    tok, width = blocks[0].shape

    @pl.when(step == 0)
    def _():
        first = me_ref[0] * EXP_DEV
        experts = router_ref.shape[0]
        which = lax.broadcasted_iota(jnp.int32, (experts, tok), 0)
        before = (
            lax.broadcasted_iota(jnp.int32, (tok, tok), 0)
            < lax.broadcasted_iota(jnp.int32, (tok, tok), 1)
        ).astype(bf16)
        count = jnp.zeros(count_ref.shape, jnp.int32)
        for s in range(8):
            logits = dg(router_ref[...], blocks[s][...], NT)
            names = routes[s][...]
            count = count + names[TOP:]
            routed = which == names[0:1, :]
            for k in range(1, TOP):
                routed = routed | (which == names[k : k + 1, :])
            logits = jnp.where(routed, logits, NEG)
            top = jnp.max(logits, axis=0, keepdims=True)
            grown = jnp.where(routed, jnp.exp(logits - top), 0.0)
            gates = grown / jnp.sum(grown, axis=0, keepdims=True)
            hots, picked = [], []
            for i in range(EXP_DEV):
                own = which == first + i
                hots.append(jnp.sum(jnp.where(own & routed, 1.0, 0.0), axis=0, keepdims=True))
                picked.append(jnp.sum(jnp.where(own, gates, 0.0), axis=0, keepdims=True))
            filler = jnp.zeros((8 - EXP_DEV, tok), f32)
            hot = jnp.concatenate(hots + [filler], axis=0)
            rank = dg(hot.astype(bf16), before, NN)
            slot = jnp.where(hot > 0.0, rank, -1.0)
            slot_ref[s] = slot
            gate_ref[s] = jnp.concatenate(picked + [filler], axis=0)
            for i in range(EXP_DEV):
                sel[s, i * CAP : (i + 1) * CAP, :] = select_rows(slot[i : i + 1, :]).astype(bf16)
        count_ref[...] = count

    at = pl.ds(pl.multiple_of(step * CAP, CAP), CAP)
    for s in range(8):
        arrived_ref[s, 0] = dg(sel[s, at, :], blocks[s][...], NN).astype(bf16)
    lin = dg(arrived_ref[:, 0].reshape(8 * CAP, width), gate_up_ref[0], NN)
    lin_ref[:, 0] = lin.reshape(8, CAP, lin.shape[1])
    half = lin.shape[1] // 2
    gate_part, up_part = lin[:, :half], lin[:, half:]
    hidden = gate_part * jax.nn.sigmoid(gate_part) * up_part
    for s in range(8):
        gate_row = gate_ref[s, pl.ds(step, 1), :]
        row_gate = jnp.sum(
            jnp.where(sel[s, at, :] > 0, gate_row, 0.0), axis=1, keepdims=True
        )
        weighted_ref[s, 0] = (row_gate * hidden[s * CAP : (s + 1) * CAP]).astype(bf16)
    out = dg(weighted_ref[:, 0].reshape(8 * CAP, half), down_ref[0], NN)
    made[:, at, :] = out.reshape(8, CAP, width).astype(bf16)

    @pl.when(step == EXP_DEV - 1)
    def _():
        for s in range(8):
            parts[s][...] = dg(sel[s], made[s], TN).astype(bf16)


def experts_forward(me, routes, router_t, blocks, gate_up_w, down_w):
    tok, width = blocks[0].shape
    cols, half = gate_up_w.shape[2], down_w.shape[1]
    by_expert = lambda w: pl.BlockSpec((8, 1, CAP, w), lambda e, *_: (0, e, 0, 0))
    rows = lambda w, t: jax.ShapeDtypeStruct((8, EXP_DEV, CAP, w), t)
    out = pl.pallas_call(
        experts_kernel,
        grid_spec=pltpu.PrefetchScalarGridSpec(
            num_scalar_prefetch=1,
            grid=(EXP_DEV,),
            in_specs=[
                whole(router_t.shape),
                pl.BlockSpec((1, width, cols), lambda e, *_: (e, 0, 0)),
                pl.BlockSpec((1, half, width), lambda e, *_: (e, 0, 0)),
            ]
            + [whole((tok, width))] * 8
            + [whole(routes[0].shape)] * 8,
            out_specs=[whole((tok, width))] * 8
            + [by_expert(width), by_expert(cols), by_expert(half)]
            + [whole((8, 8, tok))] * 2
            + [whole((8, tok))],
            scratch_shapes=[
                pltpu.VMEM((8, EXP_DEV * CAP, tok), bf16),
                pltpu.VMEM((8, EXP_DEV * CAP, width), bf16),
            ],
        ),
        out_shape=[jax.ShapeDtypeStruct((tok, width), bf16)] * 8
        + [rows(width, bf16), rows(cols, f32), rows(half, bf16)]
        + [jax.ShapeDtypeStruct((8, 8, tok), f32)] * 2
        + [jax.ShapeDtypeStruct((8, tok), jnp.int32)],
        compiler_params=params(60),
        cost_estimate=pl.CostEstimate(
            flops=11 * 10**9, bytes_accessed=40 * 10**6, transcendentals=10**6
        ),
        name="experts_forward",
    )(me, router_t, gate_up_w, down_w, *blocks, *routes)
    return list(out[:8]), out[8:13], out[13]


def experts_back_kernel(me_ref, slot_ref, gate_ref, lin_ref, gate_up_ref, down_ref, *refs):
    blocks, refs = refs[:8], refs[8:]
    parts, refs = refs[:8], refs[8:]
    arrived_ref, lin_grad_ref, sel, made = refs
    step = pl.program_id(0)
    tok, width = blocks[0].shape
    half = down_ref.shape[1]
    at = pl.ds(pl.multiple_of(step * CAP, CAP), CAP)

    for s in range(8):
        sel[s, at, :] = select_rows(slot_ref[s, pl.ds(step, 1), :]).astype(bf16)
        arrived_ref[s, 0] = dg(sel[s, at, :], blocks[s][...], NN).astype(bf16)
    pull = dg(arrived_ref[:, 0].reshape(8 * CAP, width), down_ref[0], NT)
    lin = lin_ref[:, 0].reshape(8 * CAP, 2 * half)
    gate_part, up_part = lin[:, :half], lin[:, half:]
    sig = jax.nn.sigmoid(gate_part)
    act = gate_part * sig
    row_gg = RESIDUAL * jnp.sum(act * up_part * pull, axis=1, keepdims=True)
    slope = sig * (1.0 + gate_part * (1.0 - sig))
    own = me_ref[0] * EXP_DEV + step
    column = lax.broadcasted_iota(jnp.int32, (CAP, made.shape[2] - width), 1)
    for s in range(8):
        mine = slice(s * CAP, (s + 1) * CAP)
        chosen = sel[s, at, :] > 0
        gate_row = gate_ref[s, pl.ds(step, 1), :]
        row_gate = jnp.sum(jnp.where(chosen, gate_row, 0.0), axis=1, keepdims=True)
        made[s, at, width:] = jnp.where(column == own, row_gg[mine], 0.0).astype(bf16)
        hidden_grad = RESIDUAL * row_gate * pull[mine]
        lin_grad_ref[s, 0, :, :half] = (hidden_grad * up_part[mine] * slope[mine]).astype(bf16)
        lin_grad_ref[s, 0, :, half:] = (hidden_grad * act[mine]).astype(bf16)
    out = dg(lin_grad_ref[:, 0].reshape(8 * CAP, 2 * half), gate_up_ref[0], NT)
    made[:, at, :width] = out.reshape(8, CAP, width).astype(bf16)

    @pl.when(step == EXP_DEV - 1)
    def _():
        for s in range(8):
            parts[s][...] = dg(sel[s], made[s], TN).astype(bf16)


def experts_backward(me, slot, gate, lin, blocks, gate_up_w, down_w):
    tok, width = blocks[0].shape
    cols, half = gate_up_w.shape[2], down_w.shape[1]
    wide = width + GATE_COLUMNS
    by_expert = lambda w: pl.BlockSpec((8, 1, CAP, w), lambda e, *_: (0, e, 0, 0))
    rows = lambda w: jax.ShapeDtypeStruct((8, EXP_DEV, CAP, w), bf16)
    out = pl.pallas_call(
        experts_back_kernel,
        grid_spec=pltpu.PrefetchScalarGridSpec(
            num_scalar_prefetch=1,
            grid=(EXP_DEV,),
            in_specs=[
                whole(slot.shape),
                whole(gate.shape),
                by_expert(cols),
                pl.BlockSpec((1, width, cols), lambda e, *_: (e, 0, 0)),
                pl.BlockSpec((1, half, width), lambda e, *_: (e, 0, 0)),
            ]
            + [whole((tok, width))] * 8,
            out_specs=[whole((tok, wide))] * 8 + [by_expert(width), by_expert(cols)],
            scratch_shapes=[
                pltpu.VMEM((8, EXP_DEV * CAP, tok), bf16),
                pltpu.VMEM((8, EXP_DEV * CAP, wide), bf16),
            ],
        ),
        out_shape=[jax.ShapeDtypeStruct((tok, wide), bf16)] * 8 + [rows(width), rows(cols)],
        compiler_params=params(60),
        cost_estimate=pl.CostEstimate(
            flops=11 * 10**9, bytes_accessed=40 * 10**6, transcendentals=10**6
        ),
        name="experts_backward",
    )(me, slot, gate, lin, gate_up_w, down_w, *blocks)
    return list(out[:8]), out[8:]


def expert_weights_kernel(after_ref, *refs):
    chunks = len(refs) // 4
    gate_up_ref, down_ref = refs[-2:]
    gate_up, down = None, None
    for c in range(chunks):
        states, lin_grad, weighted, grads = [
            r[:, 0].reshape(8 * CAP, r.shape[3]) for r in refs[4 * c : 4 * c + 4]
        ]
        one, two = dg(states, lin_grad, TN), dg(weighted, grads, TN)
        gate_up = one if gate_up is None else gate_up + one
        down = two if down is None else down + two
    gate_up_ref[0] = gate_up.astype(bf16)
    down_ref[0] = (RESIDUAL * down).astype(bf16)


def expert_weights(after, chunks):
    width, cols, half = [chunks[0][i].shape[3] for i in range(3)]
    by_expert = lambda w: pl.BlockSpec((8, 1, CAP, w), lambda e, *_: (0, e, 0, 0))
    flat = [x for chunk in chunks for x in chunk]
    return pl.pallas_call(
        expert_weights_kernel,
        grid_spec=pltpu.PrefetchScalarGridSpec(
            num_scalar_prefetch=1,
            grid=(EXP_DEV,),
            in_specs=[by_expert(x.shape[3]) for x in flat],
            out_specs=[
                pl.BlockSpec((1, width, cols), lambda e, *_: (e, 0, 0)),
                pl.BlockSpec((1, half, width), lambda e, *_: (e, 0, 0)),
            ],
        ),
        out_shape=[
            jax.ShapeDtypeStruct((EXP_DEV, width, cols), bf16),
            jax.ShapeDtypeStruct((EXP_DEV, half, width), bf16),
        ],
        compiler_params=params(60),
        cost_estimate=pl.CostEstimate(
            flops=14 * 10**9, bytes_accessed=40 * 10**6, transcendentals=0
        ),
        name="expert_weights",
    )(after, *flat)


MESH = pl.DeviceIdType.MESH


def flip(index, mask):
    return index + mask - 2 * mask * lax.rem(lax.div(index, mask), 2)


def greet(partners):
    barrier = pltpu.get_barrier_semaphore()
    for partner in partners:
        pl.semaphore_signal(barrier, inc=1, device_id=partner, device_id_type=MESH)
    pl.semaphore_wait(barrier, len(partners))


class Wire:
    def __init__(self, send_sem, recv_sem):
        self.send_sem, self.recv_sem, self.copies = send_sem, recv_sem, []

    def start(self, src, dst, partner):
        i = len(self.copies)
        copy = pltpu.make_async_remote_copy(
            src_ref=src,
            dst_ref=dst,
            send_sem=self.send_sem.at[i],
            recv_sem=self.recv_sem.at[i],
            device_id=partner,
            device_id_type=MESH,
        )
        copy.start()
        self.copies.append(copy)
        return copy

    def finish(self):
        for copy in self.copies:
            copy.wait_send()


def comm_call(
    kernel, name, number, copies, in_specs, out_specs, out_shape, scratch, cost, aliases={}
):
    return pl.pallas_call(
        kernel,
        in_specs=in_specs,
        out_specs=out_specs,
        out_shape=out_shape,
        scratch_shapes=list(scratch) + [pltpu.SemaphoreType.DMA((copies,))] * 2,
        compiler_params=pltpu.CompilerParams(
            vmem_limit_bytes=60 << 20, collective_id=number, has_side_effects=True
        ),
        cost_estimate=pl.CostEstimate(flops=cost, bytes_accessed=cost, transcendentals=0),
        input_output_aliases=aliases,
        name=name,
    )


ANYWHERE = pl.BlockSpec(memory_space=pl.ANY)
ON_CHIP = pl.BlockSpec(memory_space=pltpu.VMEM)


def add_into(rows, out, first, *others, step=32):
    @pl.loop(0, rows // step)
    def _(i):
        at = pl.ds(pl.multiple_of(i * step, step), step)
        total = first[at].astype(f32)
        for other in others:
            total = total + other[at].astype(f32)
        out[at] = total.astype(out.dtype)


def plane_places():
    z = lax.axis_index("dp")
    return z, flip(z, 1), lax.rem(z + 2, 4), lax.div(z, 2), lax.rem(z, 2)


def stripe(index, size):
    return pl.ds(pl.multiple_of(index * size, size), size)


class WeightsIn:
    def __init__(
        self,
        wire,
        experts,
        w_gate_up,
        w_down,
        gate_up,
        down,
        stage,
        stage_down,
        sems,
        direct=False,
    ):
        z, beside, opposite, side, low = plane_places()
        slab, part = w_gate_up.shape[1], gate_up.shape[2] // 2
        rows = w_down.shape[1]
        self.wire, self.gate_up, self.slab, self.opposite = wire, gate_up, slab, opposite
        self.beside = {"dp": beside}
        self.crossing, self.arriving, self.stores = [], [], []
        self.direct = direct

        def columns(i, which, p):
            return w_gate_up.at[i, :, stripe(2 * p + which, part)]

        def spot(i, p):
            return gate_up.at[i, stripe(z, slab), pl.ds(p * part, part)]

        self.loads = loads = []
        for n, i in enumerate(experts):
            for p in range(2):
                loads.append(
                    pltpu.make_async_copy(
                        columns(i, side, p),
                        stage.at[n, :, pl.ds(p * part, part)],
                        sems.at[n, p],
                    )
                )
            loads.append(pltpu.make_async_copy(w_down.at[i], stage_down.at[n], sems.at[n, 2]))
            for load in loads[-3:]:
                load.start()
            if direct:
                corner = {"dp": flip(opposite, 1)}
                for p in range(2):
                    self.arriving.append(wire.start(columns(i, 1 - side, p), spot(i, p), corner))
            self.crossing.append(
                (
                    i,
                    [
                        wire.start(columns(i, 1 - side, p), spot(i, p), {"dp": opposite})
                        for p in range(2)
                    ],
                )
            )
            for p in range(2):
                self.arriving.append(wire.start(columns(i, side, p), spot(i, p), self.beside))
            here = down.at[i, stripe(low, rows)]
            self.arriving.append(wire.start(w_down.at[i], here, self.beside))
            self.stores.append(
                pltpu.make_async_copy(
                    stage.at[n], gate_up.at[i, stripe(z, slab)], sems.at[n, 3]
                )
            )
            self.stores.append(pltpu.make_async_copy(stage_down.at[n], here, sems.at[n, 4]))

    def finish(self):
        for load in self.loads:
            load.wait()
        for store in self.stores:
            store.start()
        for i, copies in self.crossing:
            for copy in copies:
                copy.wait_recv()
            if self.direct:
                continue
            piece = self.gate_up.at[i, stripe(self.opposite, self.slab)]
            self.arriving.append(self.wire.start(piece, piece, self.beside))
        for copy in self.arriving:
            copy.wait_recv()
        for store in self.stores:
            store.wait()


def weights_scratch(count, slab, columns, rows, width):
    return [
        pltpu.VMEM((count, slab, columns), bf16),
        pltpu.VMEM((count, rows, width), bf16),
        pltpu.SemaphoreType.DMA((count, 5)),
    ]


class GradsOut:
    def __init__(self, wire, i, grad_gate_up, grad_down, out, out_down, got, own, downs, sems):
        z, beside, opposite, side, low = plane_places()
        slab, rows = out.shape[0], out_down.shape[0]
        self.wire, self.side, self.across = wire, side, {"dp": opposite}
        self.out, self.out_down, self.got, self.own, self.downs = out, out_down, got, own, downs

        def slab_of(plane):
            return grad_gate_up.at[i, stripe(plane, slab)]

        def rows_of(which):
            return grad_down.at[i, stripe(which, rows)]

        to = {"dp": beside}
        self.loads = [
            pltpu.make_async_copy(slab_of(opposite), own.at[0], sems.at[0]),
            pltpu.make_async_copy(slab_of(z), own.at[1], sems.at[1]),
            pltpu.make_async_copy(rows_of(low), downs.at[0], sems.at[2]),
        ]
        for load in self.loads:
            load.start()
        self.copies = [
            wire.start(slab_of(flip(opposite, 1)), got.at[0], to),
            wire.start(slab_of(beside), got.at[1], to),
            wire.start(rows_of(1 - low), downs.at[1], to),
        ]

    def cross(self):
        self.loads[0].wait()
        self.copies[0].wait_recv()
        slab = self.out.shape[0]
        add_into(slab, self.own.at[2], self.own.at[0], self.got.at[0])
        self.copies.append(self.wire.start(self.own.at[2], self.got.at[2], self.across))

    def finish(self):
        part = self.out.shape[1] // 4
        slab = self.out.shape[0]
        self.loads[1].wait()
        self.copies[1].wait_recv()
        self.copies[3].wait_recv()
        out, got, own, side = self.out, self.got, self.own, self.side

        @pl.loop(0, slab // 32)
        def _(r):
            at = pl.ds(pl.multiple_of(r * 32, 32), 32)
            for p in range(2):
                lanes = pl.ds(p * part, part)
                total = own[1, at, lanes].astype(f32) + got[1, at, lanes].astype(f32)
                out[at, stripe(2 * p + side, part)] = total.astype(bf16)
                out[at, stripe(2 * p + 1 - side, part)] = got[2, at, lanes]

        self.loads[2].wait()
        self.copies[2].wait_recv()
        add_into(self.out_down.shape[0], self.out_down, self.downs.at[0], self.downs.at[1])


def grads_scratch(slab, columns, rows, width):
    return [
        pltpu.VMEM((3, slab, columns), bf16),
        pltpu.VMEM((3, slab, columns), bf16),
        pltpu.VMEM((2, rows, width), bf16),
        pltpu.SemaphoreType.DMA((3,)),
    ]


def grads_shapes(grad_gate_up, grad_down):
    slab, columns = grad_gate_up.shape[1] // 4, grad_gate_up.shape[2]
    rows, width = grad_down.shape[1] // 2, grad_down.shape[2]
    return (
        [jax.ShapeDtypeStruct((slab, 2 * columns), bf16), jax.ShapeDtypeStruct((rows, width), bf16)],
        grads_scratch(slab, columns, rows, width),
    )


def neighbours(half):
    e, z = lax.axis_index("expert"), lax.axis_index("dp")
    across = lax.rem(z + half, lax.axis_size("dp"))
    return [{"expert": flip(e, m)} for m in (1, 2, 4)] + [{"dp": across}]


class Several:
    def __init__(self, copies):
        self.copies = copies

    def wait_recv(self):
        for copy in self.copies:
            copy.wait_recv()


def exchange_plane(wire, partners, near, far, begin=None):
    core, side_x, side_y, across = partners

    def cut(ref, h):
        rows = ref.shape[0] // 2
        return ref.at[pl.ds(h * rows, rows)]

    def start(src, dst, to, h=None):
        if h is not None:
            src, dst = [[cut(ref, h) for ref in refs] for refs in (src, dst)]
        return Several([wire.start(x, y, to) for x, y in zip(src, dst)])

    z_low = start(near[0], far[0], across, 0)
    z_high = start(near[0], far[0], across, 1)
    near_x_low = start(near[0], near[2], side_x, 0)
    near_y_high = start(near[0], near[4], side_y, 1)
    near_x_high = start(near[0], near[2], side_x, 1)
    near_y_low = start(near[0], near[4], side_y, 0)
    last = [start(near[0], near[1], core)]
    cargo = begin() if begin else None
    near_x_low.wait_recv()
    near_diag_low = start(near[2], near[6], side_y, 0)
    near_y_high.wait_recv()
    near_diag_high = start(near[4], near[6], side_x, 1)
    near_x_high.wait_recv()
    last.append(start(near[2], near[3], core))
    near_y_low.wait_recv()
    last.append(start(near[4], near[5], core))
    z_low.wait_recv()
    far_x_low = start(far[0], far[2], side_x, 0)
    far_y_low = start(far[0], far[4], side_y, 0)
    near_diag_low.wait_recv()
    near_diag_high.wait_recv()
    last.append(start(near[6], near[7], core))
    z_high.wait_recv()
    far_x_high = start(far[0], far[2], side_x, 1)
    far_y_high = start(far[0], far[4], side_y, 1)
    last.append(start(far[0], far[1], core))
    far_x_low.wait_recv()
    far_diag_low = start(far[2], far[6], side_y, 0)
    far_y_low.wait_recv()
    far_y_high.wait_recv()
    far_diag_high = start(far[4], far[6], side_x, 1)
    last.append(start(far[4], far[5], core))
    far_x_high.wait_recv()
    last.append(start(far[2], far[3], core))
    far_diag_low.wait_recv()
    far_diag_high.wait_recv()
    last.append(start(far[6], far[7], core))
    for copy in last:
        copy.wait_recv()
    if cargo:
        cargo.finish()


def plane_gather_kernel(half, experts, count, *refs):
    inputs, refs = refs[:count], refs[count:]
    if experts:
        (w_gate_up, w_down), refs = refs[:2], refs[4:]
    outs, refs = refs[: 15 * count], refs[15 * count :]
    near = [list(inputs)] + [list(outs[j * count : (j + 1) * count]) for j in range(7)]
    far = [list(outs[j * count : (j + 1) * count]) for j in range(7, 15)]
    wire = Wire(*refs[-2:])
    partners = neighbours(half)
    begin = None
    if experts:
        greet(partners + [{"dp": plane_places()[1]}])
        begin = lambda: WeightsIn(wire, experts, w_gate_up, w_down, *refs[:5])
    else:
        greet(partners)
    exchange_plane(wire, partners, near, far, begin)
    wire.finish()


def plane_gather(inputs, half, number, name, experts=(), weights=(), filled=()):
    count, size = len(inputs), inputs[0].size
    blocks = [jax.ShapeDtypeStruct(x.shape, x.dtype) for x in inputs]
    scratch, aliases = [], {}
    if experts:
        (w_gate_up, w_down), (gate_up, down) = weights, filled
        scratch = weights_scratch(
            len(experts), w_gate_up.shape[1], gate_up.shape[2], w_down.shape[1], down.shape[2]
        )
        aliases = {count + 2: 15 * count, count + 3: 15 * count + 1}
    out = comm_call(
        functools.partial(plane_gather_kernel, half, experts, count),
        name,
        number,
        22 * count + 6 * len(experts),
        [ANYWHERE] * (count + len(weights) + len(filled)),
        [ANYWHERE] * (15 * count + len(filled)),
        blocks * 15 + [jax.ShapeDtypeStruct(x.shape, x.dtype) for x in filled],
        scratch,
        80 * size,
        aliases,
    )(*inputs, *weights, *filled)
    pairs = []
    for n, x in enumerate(inputs):
        own = out[n : 15 * count : count]
        pairs.append(([x] + list(own[:7]), list(own[7:])))
    return pairs, out[15 * count :]


def plane_scatter_kernel(half, i, *refs):
    parts = {"near": refs[:8], "far": refs[8:16]}
    refs = refs[16:]
    carried = ()
    if i is not None:
        carried, refs = refs[:2] + refs[3:5] + refs[11:15], refs[2:3] + refs[5:11] + refs[15:]
    out, core_in, sums, diag_in, last_in, z_out, z_in = refs[:7]
    wire = Wire(*refs[7:])
    core, side_x, side_y, across = partners = neighbours(half)
    rows = out.shape[0] // 2
    cut = rows // 2
    low, high = pl.ds(0, cut), pl.ds(cut, cut)
    if carried:
        greet(partners + [{"dp": plane_places()[1]}])
        cargo = GradsOut(wire, i, *carried)
    else:
        greet(partners)
    segments = [(kind, h) for kind in ("far", "near") for h in range(2)]
    from_core, from_diag, from_last, from_z = {}, {}, {}, {}

    def part(s, j):
        kind, h = segments[s]
        return parts[kind][j].at[pl.ds(h * rows, rows)]

    for s in range(4):
        for k in (3, 1, 2, 0):
            from_core[s, k] = wire.start(part(s, 2 * k + 1), core_in.at[s, k], core)

    def chip_sum(s, k):
        from_core[s, k].wait_recv()
        add_into(rows, sums.at[s, k], part(s, 2 * k), core_in.at[s, k])

    def enter(s):
        chip_sum(s, 3)
        from_diag[s, 0] = wire.start(sums.at[s, 3, low], diag_in.at[s, 0], side_x)
        from_diag[s, 1] = wire.start(sums.at[s, 3, high], diag_in.at[s, 1], side_y)
        chip_sum(s, 1)
        from_last[s, 0] = wire.start(sums.at[s, 1, low], last_in.at[s, 0, low], side_x)
        chip_sum(s, 2)
        from_last[s, 1] = wire.start(sums.at[s, 2, high], last_in.at[s, 1, high], side_y)

    def turn(s):
        from_diag[s, 1].wait_recv()
        add_into(cut, sums.at[s, 1, high], sums.at[s, 1, high], diag_in.at[s, 1])
        from_last[s, 2] = wire.start(sums.at[s, 1, high], last_in.at[s, 0, high], side_x)
        from_diag[s, 0].wait_recv()
        add_into(cut, sums.at[s, 2, low], sums.at[s, 2, low], diag_in.at[s, 0])
        from_last[s, 3] = wire.start(sums.at[s, 2, low], last_in.at[s, 1, low], side_y)

    def leave(s):
        kind, h = segments[s]
        from_core[s, 0].wait_recv()
        for i in range(4):
            from_last[s, i].wait_recv()
        target = z_out.at[h] if kind == "far" else out.at[pl.ds(h * rows, rows)]
        add_into(rows, target, part(s, 0), core_in.at[s, 0], last_in.at[s, 0], last_in.at[s, 1])
        if kind == "far":
            from_z[h] = wire.start(z_out.at[h], z_in.at[h], across)

    for step, s in (
        (enter, 0),
        (enter, 1),
        (turn, 0),
        (enter, 2),
        (turn, 1),
        (leave, 0),
        (enter, 3),
        (leave, 1),
        (turn, 2),
        (turn, 3),
        (leave, 2),
        (leave, 3),
    ):
        step(s)
        if carried and (step, s) == (leave, 1):
            cargo.cross()
    for h in range(2):
        from_z[h].wait_recv()
        target = out.at[pl.ds(h * rows, rows)]
        add_into(rows, target, target, z_in.at[h])
    if carried:
        cargo.finish()
    wire.finish()


def plane_scatter(near, far, half, number, name, i=None, grads=()):
    rows, width = near[0].shape
    specs = [ON_CHIP, ANYWHERE] * 8
    block = (rows // 2, width)
    shapes, scratch = grads_shapes(*grads) if grads else ([], [])
    return comm_call(
        functools.partial(plane_scatter_kernel, half, i),
        name,
        number,
        42 + 2 * len(grads),
        specs + [ANYWHERE] * len(grads),
        [ON_CHIP] * (1 + len(shapes)),
        [jax.ShapeDtypeStruct((rows, width), f32)] + shapes,
        [
            pltpu.VMEM((4, 4) + block, bf16),
            pltpu.VMEM((4, 4) + block, bf16),
            pltpu.VMEM((4, 2, rows // 4, width), bf16),
            pltpu.VMEM((4, 2) + block, bf16),
            pltpu.VMEM((2,) + block, bf16),
            pltpu.VMEM((2,) + block, bf16),
        ]
        + scratch,
        50 * rows * width,
    )(*near, *far, *grads)


def chip_partners():
    e = lax.axis_index("expert")
    return [{"expert": flip(e, m)} for m in (1, 2)]


def exchange_seq(wire, group, x_ref, out, between=None, steps=()):
    head = lax.rem(lax.axis_index("expert"), group)
    core, side_x = chip_partners()
    rows = x_ref.shape[0]
    cut = rows // 2
    mine = pl.multiple_of(head * rows, rows)
    other = pl.multiple_of(flip(head, 2) * rows, rows)
    crossing = [
        wire.start(x_ref.at[pl.ds(h * cut, cut)], out.at[pl.ds(mine + h * cut, cut)], side_x)
        for h in range(2)
    ]
    last = [wire.start(x_ref, out.at[pl.ds(mine, rows)], core)]
    out[pl.ds(mine, rows), :] = x_ref[...]
    if between:
        between()
    for h in range(2):
        if steps:
            steps[h]()
        crossing[h].wait_recv()
        piece = out.at[pl.ds(other + h * cut, cut)]
        last.append(wire.start(piece, piece, core))
    if steps:
        steps[2]()
    for copy in last:
        copy.wait_recv()


def seq_gather_kernel(group, x_ref, out, send_sem, recv_sem):
    wire = Wire(send_sem, recv_sem)
    greet(chip_partners())
    exchange_seq(wire, group, x_ref, out)
    wire.finish()


def seq_gather(x, group, number, name):
    rows, width = x.shape
    return comm_call(
        functools.partial(seq_gather_kernel, group),
        name,
        number,
        5,
        [ON_CHIP],
        ON_CHIP,
        jax.ShapeDtypeStruct((group * rows, width), x.dtype),
        [],
        20 * x.size,
    )(x)


def sum_seq(wire, group, x_ref, out, core_in, sums, last_in, between=None):
    head = lax.rem(lax.axis_index("expert"), group)
    core, side_x = chip_partners()
    rows = out.shape[0]
    cut = rows // 2

    def part(block, h):
        return x_ref.at[pl.ds(pl.multiple_of(block * rows + h * cut, cut), cut)]

    crossing = [
        wire.start(part(flip(flip(head, 2), 1), h), core_in.at[1, h], core) for h in range(2)
    ]
    near = [wire.start(part(flip(head, 1), h), core_in.at[0, h], core) for h in range(2)]
    last = []
    for h in range(2):
        crossing[h].wait_recv()
        add_into(cut, sums.at[h], part(flip(head, 2), h), core_in.at[1, h])
        last.append(wire.start(sums.at[h], last_in.at[h], side_x))
    if between:
        between()
    for h in range(2):
        near[h].wait_recv()
        last[h].wait_recv()
        add_into(
            cut, out.at[pl.ds(h * cut, cut)], part(head, h), core_in.at[0, h], last_in.at[h]
        )


def seq_scatter_kernel(group, x_ref, out, core_in, sums, last_in, send_sem, recv_sem):
    wire = Wire(send_sem, recv_sem)
    greet(chip_partners())
    sum_seq(wire, group, x_ref, out, core_in, sums, last_in)
    wire.finish()


def seq_scratch(rows, width):
    piece = (rows // 2, width)
    return [
        pltpu.VMEM((2, 2) + piece, bf16),
        pltpu.VMEM((2,) + piece, bf16),
        pltpu.VMEM((2,) + piece, bf16),
    ]


def seq_scatter(x, group, number, name):
    rows, width = x.shape[0] // group, x.shape[1]
    return comm_call(
        functools.partial(seq_scatter_kernel, group),
        name,
        number,
        6,
        [ON_CHIP],
        ON_CHIP,
        jax.ShapeDtypeStruct((rows, width), f32),
        seq_scratch(rows, width),
        20 * rows * width,
    )(x)


def entry_kernel(group, x_ref, qkv_in, out_in, seq, qkv, out_slice, send_sem, recv_sem):
    wire = Wire(send_sem, recv_sem)
    e, z = lax.axis_index("expert"), lax.axis_index("dp")
    head, row = lax.rem(e, group), lax.div(e, group)
    side_y = {"expert": flip(e, 4)}
    top = 3
    slab = qkv_in.shape[0]
    cut = slab // 2
    greet(chip_partners() + [side_y] + [{"dp": lax.rem(z + k, 4)} for k in range(1, 4)])
    mine = pl.ds(pl.multiple_of(row * cut, cut), cut)

    def spot(plane):
        return qkv.at[pl.ds(pl.multiple_of(plane * slab + row * cut, cut), cut)]

    def copy(n, src, dst, to):
        return pltpu.make_async_remote_copy(
            src_ref=src,
            dst_ref=dst,
            send_sem=send_sem.at[n],
            recv_sem=recv_sem.at[n],
            device_id=to,
            device_id_type=MESH,
        )

    up, down = {"dp": lax.rem(z + 1, 4)}, {"dp": lax.rem(z + 3, 4)}
    hops = []
    for sign, to in ((1, up), (-1, down)):
        for d in (1, 2, 3):
            n = 5 + len(hops) * 2
            held, got = lax.rem(z - sign * (d - 1) + 8, 4), lax.rem(z - sign * d + 8, 4)
            source = qkv_in.at[mine] if d == 1 else spot(held)
            edge = z < top if sign > 0 else z > 0
            held_there = z >= d - 1 if sign > 0 else z <= top - (d - 1)
            arrives = z >= d if sign > 0 else z <= top - d
            hops.append(
                (
                    jnp.logical_and(edge, held_there),
                    arrives,
                    copy(n, source, spot(held), to),
                    copy(n + 1, spot(got), spot(got), side_y),
                )
            )
    for sends, _, hop, _ in (hops[0], hops[3]):
        pl.when(sends)(hop.start)

    owner = z == head
    out_up = copy(17, out_slice.at[mine], out_slice.at[mine], up)
    out_down = copy(18, out_slice.at[mine], out_slice.at[mine], down)
    own_up = copy(17, out_in.at[mine], out_slice.at[mine], up)
    own_down = copy(18, out_in.at[mine], out_slice.at[mine], down)
    swap = copy(19, out_slice.at[mine], out_slice.at[mine], side_y)
    pl.when(jnp.logical_and(owner, z < top))(own_up.start)
    pl.when(jnp.logical_and(owner, z > 0))(own_down.start)

    @pl.when(owner)
    def _():
        out_slice[...] = out_in[...]

    qkv[pl.ds(pl.multiple_of(z * slab, slab), slab), :] = qkv_in[...]

    def relay(d):
        for way in (0, 3):
            _, arrives, hop, across = hops[way + d]

            @pl.when(arrives)
            def _():
                hop.wait_recv()
                across.start()

            if d < 2:
                sends, _, following, _ = hops[way + d + 1]
                pl.when(sends)(following.start)

        @pl.when(z == head + d + 1)
        def _():
            out_up.wait_recv()
            pl.when(z < top)(out_up.start)
            swap.start()

        @pl.when(z == head - d - 1)
        def _():
            out_down.wait_recv()
            pl.when(z > 0)(out_down.start)
            swap.start()

    steps = [functools.partial(relay, d) for d in range(3)]
    exchange_seq(wire, group, x_ref, seq, steps=steps)
    for sends, arrives, hop, across in hops:
        pl.when(arrives)(across.wait)
        pl.when(sends)(hop.wait_send)
    pl.when(jnp.logical_not(owner))(swap.wait)
    pl.when(jnp.logical_and(z >= head, z < top))(out_up.wait_send)
    pl.when(jnp.logical_and(z <= head, z > 0))(out_down.wait_send)
    wire.finish()


def attention_entry(x, qkv_slice, w_out, group):
    rows, width = x.shape
    slab, columns = qkv_slice.shape
    return comm_call(
        functools.partial(entry_kernel, group),
        "attention_entry",
        8,
        20,
        [ON_CHIP] * 3,
        [ON_CHIP] * 3,
        [
            jax.ShapeDtypeStruct((group * rows, width), bf16),
            jax.ShapeDtypeStruct((4 * slab, columns), bf16),
            jax.ShapeDtypeStruct((slab, width), bf16),
        ],
        [],
        40 * x.size,
    )(x, qkv_slice, w_out)


def scatter_weights_kernel(group, experts, x_ref, w_gate_up, w_down, out, gate_up, down, *refs):
    wire = Wire(*refs[6:])
    _, beside, opposite, _, _ = plane_places()
    greet(chip_partners() + [{"dp": p} for p in (beside, opposite, flip(opposite, 1))])
    cargo = WeightsIn(wire, experts, w_gate_up, w_down, gate_up, down, *refs[3:6], direct=True)
    sum_seq(wire, group, x_ref, out, *refs[:3])
    cargo.finish()
    wire.finish()


def seq_scatter_weights(x, group, experts, w_gate_up, w_down):
    rows, width = x.shape[0] // group, x.shape[1]
    count, slab, columns = w_gate_up.shape
    ff_rows = w_down.shape[1]
    return comm_call(
        functools.partial(scatter_weights_kernel, group, experts),
        "scatter_branch_weights",
        9,
        6 + 7 * len(experts),
        [ON_CHIP, ANYWHERE, ANYWHERE],
        [ON_CHIP, ANYWHERE, ANYWHERE],
        [
            jax.ShapeDtypeStruct((rows, width), f32),
            jax.ShapeDtypeStruct((count, 4 * slab, columns // 2), bf16),
            jax.ShapeDtypeStruct((count, 2 * ff_rows, width), bf16),
        ],
        seq_scratch(rows, width)
        + weights_scratch(len(experts), slab, columns // 2, ff_rows, width),
        40 * rows * width,
    )(x, w_gate_up, w_down)


def gather_grads_kernel(group, i, x_ref, grad_gate_up, grad_down, seq, out, out_down, *refs):
    wire = Wire(*refs[4:])
    _, beside, opposite, _, _ = plane_places()
    greet(chip_partners() + [{"dp": beside}, {"dp": opposite}])
    cargo = GradsOut(wire, i, grad_gate_up, grad_down, out, out_down, *refs[:4])
    exchange_seq(wire, group, x_ref, seq, cargo.cross)
    cargo.finish()
    wire.finish()


def seq_gather_grads(x, group, i, grad_gate_up, grad_down):
    rows, width = x.shape
    shapes, scratch = grads_shapes(grad_gate_up, grad_down)
    return comm_call(
        functools.partial(gather_grads_kernel, group, i),
        "gather_branch_grads",
        10,
        9,
        [ON_CHIP, ANYWHERE, ANYWHERE],
        [ON_CHIP] * 3,
        [jax.ShapeDtypeStruct((group * rows, width), x.dtype)] + shapes,
        scratch,
        40 * x.size,
    )(x, grad_gate_up, grad_down)


def scatter_grads_kernel(group, i, x_ref, grad_gate_up, grad_down, total, out, out_down, *refs):
    wire = Wire(*refs[7:])
    _, beside, opposite, _, _ = plane_places()
    greet(chip_partners() + [{"dp": beside}, {"dp": opposite}])
    cargo = GradsOut(wire, i, grad_gate_up, grad_down, out, out_down, *refs[3:7])
    sum_seq(wire, group, x_ref, total, *refs[:3], cargo.cross)
    cargo.finish()
    wire.finish()


def seq_scatter_grads(x, group, i, grad_gate_up, grad_down):
    rows, width = x.shape[0] // group, x.shape[1]
    shapes, scratch = grads_shapes(grad_gate_up, grad_down)
    return comm_call(
        functools.partial(scatter_grads_kernel, group, i),
        "scatter_normed_grads",
        11,
        10,
        [ON_CHIP, ANYWHERE, ANYWHERE],
        [ON_CHIP] * 3,
        [jax.ShapeDtypeStruct((rows, width), f32)] + shapes,
        seq_scratch(rows, width) + scratch,
        40 * rows * width,
    )(x, grad_gate_up, grad_down)


def start_kernel(replicas, small_ref, small_out, send_sem, recv_sem):
    wire = Wire(send_sem, recv_sem)
    z = lax.axis_index("dp")
    planes = [{"dp": lax.rem(z + k, replicas)} for k in range(1, replicas)]
    greet(planes)
    spread = [wire.start(small_ref, small_out.at[z], plane) for plane in planes]
    small_out[z] = small_ref[...]
    for copy in spread:
        copy.wait_recv()
    wire.finish()


def start_exchange(small, replicas):
    return comm_call(
        functools.partial(start_kernel, replicas),
        "start_exchange",
        1,
        replicas - 1,
        [ON_CHIP],
        ON_CHIP,
        jax.ShapeDtypeStruct((replicas,) + small.shape, small.dtype),
        [],
        10**6,
    )(small)


def dense_kernel(replicas, grads, small, out, small_out, *refs):
    y_in, z_out, z_in, small_in, small_sum, turn_in = refs[:6]
    wire = Wire(*refs[6:])
    e, z = lax.axis_index("expert"), lax.axis_index("dp")
    head, row = lax.rem(e, 4), lax.div(e, 4)
    partners = [{"expert": flip(e, m)} for m in (1, 2, 4)]
    core, side_x, side_y = partners
    slab, width = grads.shape[0] // replicas, grads.shape[1]
    cut = slab // 2
    quarter = cut // 2
    order = [2, 1, 3, 0]
    block = {k: lax.rem(z + k, replicas) for k in range(replicas)}
    plane = {k: {"dp": block[k]} for k in range(1, replicas)}
    greet(partners + list(plane.values()))

    def half_of(k, which):
        return grads.at[pl.ds(pl.multiple_of(block[k] * slab + which * cut, cut), cut)]

    small_copies = [wire.start(small.at[block[k]], small_in.at[k - 1], plane[k]) for k in plane]
    from_y = {k: wire.start(half_of(k, 1 - row), y_in.at[k], side_y) for k in order}
    for copy in small_copies:
        copy.wait_recv()
    small_sum[0] = small[z] + small_in[0] + small_in[1] + small_in[2]
    turn = wire.start(small_sum.at[0], turn_in.at[0], core)
    from_z = {}
    for step, k in enumerate(order):
        from_y[k].wait_recv()
        add_into(cut, z_out.at[k], half_of(k, row), y_in.at[k])
        if k:
            from_z[k] = wire.start(z_out.at[k], z_in.at[k - 1], plane[k])
        if step == 0:
            turn.wait_recv()
            small_sum[1] = small_sum[0] + turn_in[0]
            turn = wire.start(small_sum.at[1], turn_in.at[1], side_x)
        if step == 1:
            turn.wait_recv()
            small_sum[2] = small_sum[1] + turn_in[1]
            turn = wire.start(small_sum.at[2], turn_in.at[2], side_y)
    turn.wait_recv()
    small_out[...] = small_sum[2] + turn_in[2]
    for k in from_z:
        from_z[k].wait_recv()

    def place(which_head, which_row, first=0, size=cut):
        start = pl.multiple_of(which_row * cut + first, quarter)
        columns = pl.ds(pl.multiple_of(which_head * width, 128), width)
        return out.at[pl.ds(start, size), columns]

    mine = place(head, row)
    add_into(cut, mine, z_out.at[0], z_in.at[0], z_in.at[1], z_in.at[2])
    other = flip(head, 2)
    pieces = [place(head, row, h * quarter, quarter) for h in range(2)]
    over_x = [wire.start(piece, piece, side_x) for piece in pieces]
    over_y = [wire.start(piece, piece, side_y) for piece in reversed(pieces)]
    last = [wire.start(mine, mine, core)]
    over_x[0].wait_recv()
    piece = place(other, row, 0, quarter)
    diag = [wire.start(piece, piece, side_y)]
    over_y[0].wait_recv()
    piece = place(head, 1 - row, quarter, quarter)
    diag.append(wire.start(piece, piece, side_x))
    over_x[1].wait_recv()
    last.append(wire.start(place(other, row), place(other, row), core))
    over_y[1].wait_recv()
    last.append(wire.start(place(head, 1 - row), place(head, 1 - row), core))
    for copy in diag:
        copy.wait_recv()
    last.append(wire.start(place(other, 1 - row), place(other, 1 - row), core))
    for copy in last:
        copy.wait_recv()
    wire.finish()


def dense_reduce(grads, small, replicas):
    slab, width = grads.shape[0] // replicas, grads.shape[1]
    piece = (slab // 2, width)
    lot = small.shape[1:]
    return comm_call(
        functools.partial(dense_kernel, replicas),
        "dense_reduce",
        2,
        23,
        [ON_CHIP] * 2,
        [ON_CHIP] * 2,
        [jax.ShapeDtypeStruct((slab, 4 * width), bf16), jax.ShapeDtypeStruct(lot, f32)],
        [
            pltpu.VMEM((4,) + piece, bf16),
            pltpu.VMEM((4,) + piece, bf16),
            pltpu.VMEM((3,) + piece, bf16),
            pltpu.VMEM((3,) + lot, f32),
            pltpu.VMEM((3,) + lot, f32),
            pltpu.VMEM((3,) + lot, f32),
        ],
        10**8,
    )(grads, small)


STRIP = 256


def strips(ref_rows):
    return [(b * STRIP, (b + 1) * STRIP) for b in range(ref_rows // STRIP)]


def head_rows(index):
    return pl.ds(pl.multiple_of(index * HD, HD), HD)


def scores_of(keys, queries, first):
    raw = dg(keys, queries, TN)
    key = lax.broadcasted_iota(jnp.int32, raw.shape, 0)
    query = lax.broadcasted_iota(jnp.int32, raw.shape, 1) + first
    raw = jnp.where(key <= query, raw, NEG)
    grown = jnp.exp(raw - jnp.max(raw, axis=0, keepdims=True))
    return grown * (1.0 / jnp.sum(grown, axis=0, keepdims=True))


def attend_kernel(q_ref, k_ref, v_ref, out_ref):
    group = q_ref.shape[0] // k_ref.shape[0]

    @pl.loop(0, q_ref.shape[0] // HD)
    def _(h):
        mine, shared = head_rows(h), head_rows(lax.div(h, group))
        for first, last in strips(q_ref.shape[1]):
            probs = scores_of(k_ref[shared, :last], q_ref[mine, first:last], first)
            out = dg(v_ref[shared, :last], probs.astype(bf16), NN)
            out_ref[mine, first:last] = out.astype(bf16)


def attend_back_kernel(q_ref, k_ref, v_ref, grad_ref, dq_ref, dk_ref, dv_ref):
    group = q_ref.shape[0] // k_ref.shape[0]
    dk_ref[...] = jnp.zeros_like(dk_ref)
    dv_ref[...] = jnp.zeros_like(dv_ref)

    @pl.loop(0, q_ref.shape[0] // HD)
    def _(h):
        mine, shared = head_rows(h), head_rows(lax.div(h, group))
        for first, last in strips(q_ref.shape[1]):
            queries, grad = q_ref[mine, first:last], grad_ref[mine, first:last]
            keys = k_ref[shared, :last]
            probs = scores_of(keys, queries, first)
            grad_probs = dg(v_ref[shared, :last], grad, TN)
            delta = jnp.sum(probs * grad_probs, axis=0, keepdims=True)
            grad_scores = (probs * (grad_probs - delta)).astype(bf16)
            dq_ref[mine, first:last] = dg(keys, grad_scores, NN) * SCORE_SCALE
            dk_ref[shared, :last] += dg(queries, grad_scores, NT)
            dv_ref[shared, :last] += dg(grad, probs.astype(bf16), NT)


def on_chip_call(kernel, name, inputs, shapes, flops):
    return pl.pallas_call(
        kernel,
        in_specs=[ON_CHIP] * len(inputs),
        out_specs=[ON_CHIP] * len(shapes),
        out_shape=shapes,
        compiler_params=params(60),
        cost_estimate=pl.CostEstimate(
            flops=flops, bytes_accessed=10**7, transcendentals=4 * 10**6
        ),
        name=name,
    )(*inputs)


def attend(queries, keys, values):
    shapes = [jax.ShapeDtypeStruct(queries.shape, bf16)]
    return on_chip_call(attend_kernel, "attend", (queries, keys, values), shapes, 10**10)[0]


def attend_back(queries, keys, values, grad_context):
    shapes = [jax.ShapeDtypeStruct(x.shape, f32) for x in (queries, keys, values)]
    inputs = (queries, keys, values, grad_context)
    return on_chip_call(attend_back_kernel, "attend_back", inputs, shapes, 3 * 10**10)


def turned(x, cosine, sine):
    x = x.reshape(-1, 2, HD // 2, x.shape[1])
    first, second = x[:, 0], x[:, 1]
    out = jnp.stack([first * cosine - second * sine, second * cosine + first * sine], axis=1)
    return out.reshape(-1, x.shape[3])


def body(
    hidden_in,
    teacher,
    valid,
    routes,
    gain_attn,
    gain_moe,
    w_query,
    w_key,
    w_value,
    w_out,
    w_router,
    w_gate_up,
    w_down,
):
    tok, width = hidden_in.shape
    owners = lax.axis_size("expert")
    replicas = lax.axis_size("dp")
    me = lax.axis_index("expert")
    plane = lax.axis_index("dp")
    length = min(SEQ_MIN, owners * tok)
    group = length // tok
    head = me % group
    experts_all = EXP_DEV * owners
    slots = 8 * ((tok * TOP + experts_all * 7 - 1) // (experts_all * 7))
    half = replicas // 2
    side = plane // half
    ff_half = FF // 2
    slab = width // replicas
    q_cols = H * HD // group
    kv_cols = KVH * HD // group

    def over_dp(x, axis):
        if replicas > group:
            return lax.all_gather(x, "dp", axis=axis, tiled=True)
        return place(
            [x] + [send(x, "dp", m) for m in range(1, replicas)],
            [plane ^ m for m in range(replicas)],
            axis,
            replicas,
        )

    routes_t = jnp.transpose(routes)
    count = jnp.full_like(routes_t, jnp.sum(valid))
    small = jnp.concatenate(
        [gain_attn[None], gain_moe[None], jnp.transpose(w_router), jnp.zeros((6, slab), bf16)]
    )
    names = jnp.concatenate([routes_t, count])
    small = start_exchange(small, replicas)
    small = jnp.transpose(small, (1, 0, 2)).reshape(small.shape[1], width)
    gain_one, gain_two, router_t = small[0], small[1], small[2 : 2 + experts_all]
    me_ref = jnp.reshape(me, (1,)).astype(jnp.int32)
    valid_float = valid.astype(f32)
    qkv_slice = jnp.concatenate(
        [
            pick(w_query, head, q_cols, 1),
            pick(w_key, head, kv_cols, 1),
            pick(w_value, head, kv_cols, 1),
        ],
        axis=1,
    )
    inputs = hidden_in.astype(f32)
    normed_f, norm_one_pull = jax.vjp(rms_norm, inputs, gain_one.astype(f32))
    normed = normed_f.astype(bf16)
    compact = replicas == group

    def on_grid(x, pairs):
        return lax.ppermute(x, ("dp", "expert"), pairs)

    if compact:
        seq, qkv, out_slice = attention_entry(normed, qkv_slice, w_out, group)
    else:
        seq = seq_gather(normed, group, 3, "gather_normed")
        qkv = over_dp(qkv_slice, 0)
        out_slice = pick(lax.all_gather(w_out, "dp", axis=0, tiled=True), head, q_cols, 0)

    lin = mm("td,dc->ct", seq, qkv)
    cosine, sine = rope_tables(jnp.arange(length, dtype=f32))
    queries = turned(lin[:q_cols], cosine, sine).astype(bf16) * jnp.asarray(SCORE_SCALE, bf16)
    keys = turned(lin[q_cols : q_cols + kv_cols], cosine, sine).astype(bf16)
    values = lin[q_cols + kv_cols :].astype(bf16)
    context = attend(queries, keys, values)
    branch = mm("ct,cd->td", context, out_slice).astype(bf16)
    if compact:
        summed, gate_up_w, down_w = seq_scatter_weights(branch, group, (0,), w_gate_up, w_down)
    else:
        summed = seq_scatter(branch, group, 4, "scatter_branch")
        gate_up_all = lax.all_gather(w_gate_up, "dp", axis=1, tiled=True)
        gate_up_w = jnp.concatenate(
            [pick(gate_up_all, p * 2 + side, ff_half, 2) for p in range(2)], axis=2
        )
        down_w = pick(lax.all_gather(w_down, "dp", axis=1, tiled=True), side, ff_half, 1)
    mid = inputs + RESIDUAL * summed
    moe_f, norm_two_pull = jax.vjp(rms_norm, mid, gain_two.astype(f32))
    moe_input = moe_f.astype(bf16)

    if compact:
        blocks, (gate_up_w, down_w) = plane_gather(
            [moe_input, names],
            half,
            12,
            "gather_all",
            (1, 2),
            (w_gate_up, w_down),
            (gate_up_w, down_w),
        )
    else:
        blocks, _ = plane_gather([moe_input, names], half, 13, "gather_names")
    (near, far), (near_names, far_names) = blocks
    near_parts, near_kept, near_count = experts_forward(
        me_ref, near_names, router_t, near, gate_up_w, down_w
    )
    far_parts, far_kept, far_count = experts_forward(
        me_ref, far_names, router_t, far, gate_up_w, down_w
    )
    valid_count = near_count[0, :1] + far_count[0, :1]
    mask = 1
    while mask < half:
        valid_count = valid_count + send(valid_count, "dp", mask)
        mask *= 2
    valid_count = valid_count[0].astype(f32)
    final_state = mid + RESIDUAL * plane_scatter(near_parts, far_parts, half, 6, "scatter_outputs")[0]
    activations = final_state.astype(bf16)
    mismatch = final_state - teacher.astype(f32)
    squares = jnp.sum(0.5 * valid_float[:, None] * mismatch * mismatch)
    tokens_all = tok * replicas * owners
    grad_final = tokens_all / valid_count * valid_float[:, None] * mismatch

    ((grad_near, grad_far),), _ = plane_gather([grad_final.astype(bf16)], half, 5, "gather_tokens")

    def back(kept, blocks):
        arrived, lin, weighted, slot, gate = kept
        parts, (grads, lin_grad) = experts_backward(
            me_ref, slot, gate, lin, blocks, gate_up_w, down_w
        )
        return parts, (arrived, lin_grad, weighted, grads)

    near_grads, near_chunk = back(near_kept, grad_near)
    far_grads, far_chunk = back(far_kept, grad_far)
    grad_gate_up, grad_down = expert_weights(me_ref, [near_chunk, far_chunk])
    done = []
    if compact:
        returned, *part = plane_scatter(
            near_grads, far_grads, half, 7, "scatter_grads", 0, (grad_gate_up, grad_down)
        )
        done.append(part)
    else:
        (returned,) = plane_scatter(near_grads, far_grads, half, 14, "scatter_rows")

    grad_gates = returned[:, width : width + experts_all]
    own_routed = jnp.any(
        routes[:, :, None] == jnp.arange(experts_all, dtype=jnp.int32), axis=1
    )
    own_logits = jnp.where(own_routed, mm("td,ed->te", moe_input, router_t), NEG)
    own_gates = jnp.where(own_routed, jax.nn.softmax(own_logits, axis=-1), 0.0)
    grad_logits = (
        own_gates * (grad_gates - jnp.sum(own_gates * grad_gates, axis=-1, keepdims=True))
    ).astype(bf16)
    grad_router_t = mm("td,te->ed", moe_input, grad_logits)
    grad_moe_input = returned[:, :width] + mm("te,ed->td", grad_logits, router_t)
    grad_mid_norm, grad_gain_two = norm_two_pull(grad_moe_input)
    grad_mid = grad_final + grad_mid_norm
    grad_branch = (RESIDUAL * grad_mid).astype(bf16)

    if compact:
        seq_grad, *part = seq_gather_grads(grad_branch, group, 1, grad_gate_up, grad_down)
        done.append(part)
    else:
        seq_grad = seq_gather(grad_branch, group, 3, "gather_normed")
    grad_out = mm("ct,td->cd", context, seq_grad).astype(bf16)
    if compact:
        out_sum = grad_out.astype(f32)
        for step in range(1, replicas):
            pairs = [
                (
                    ((i % group + step) % replicas) * owners + i,
                    (i % group) * owners + i,
                )
                for i in range(owners)
            ]
            out_sum = out_sum + on_grid(grad_out, pairs).astype(f32)
        entered = jnp.where(never(out_sum[0, 0]) == 0, 1.0, 0.0)
    grad_context = mm("td,cd->ct", seq_grad, out_slice).astype(bf16)
    grad_q, grad_k, grad_v = attend_back(queries, keys, values, grad_context)
    grad_lin = jnp.concatenate(
        [turned(grad_q, cosine, -sine), turned(grad_k, cosine, -sine), grad_v]
    ).astype(bf16)
    grad_qkv = mm("td,ct->dc", seq, grad_lin).astype(bf16)
    normed_parts = mm("ct,dc->td", grad_lin, qkv)
    normed_parts = (entered * normed_parts if compact else normed_parts).astype(bf16)
    if compact:
        grad_normed, *part = seq_scatter_grads(normed_parts, group, 2, grad_gate_up, grad_down)
        done.append(part)
    else:
        grad_normed = seq_scatter(normed_parts, group, 4, "scatter_branch")
    grad_in_norm, grad_gain_one = norm_one_pull(grad_normed)
    grad_in = grad_mid + grad_in_norm

    def other_sequences(x):
        total = x.astype(f32)
        mask = group
        while mask < owners:
            total = total + send(total.astype(bf16), "expert", mask).astype(f32)
            mask *= 2
        return total

    lot = jnp.concatenate(
        [
            grad_router_t,
            grad_gain_one[None],
            grad_gain_two[None],
            jnp.full((6, width), squares),
        ]
    )
    if compact:
        out_sum = other_sequences(out_sum).astype(bf16)
        g_out = jnp.where(plane == head, out_sum, jnp.zeros((), bf16))
        for m in range(1, group):
            pairs = [
                ((i % group) * owners + i, (i % group) * owners + (i ^ m)) for i in range(owners)
            ]
            g_out = g_out + on_grid(out_sum, pairs)
        g_out = g_out.astype(f32)
        lot = jnp.where(never(out_sum[0, 0]) == 0, lot, 0.0)
        lot = jnp.transpose(lot.reshape(32, replicas, slab), (1, 0, 2))
        by_head, lot = dense_reduce(grad_qkv, lot, replicas)
        gate_up_out, down_out = [jnp.stack(x).astype(f32) for x in zip(*done)]
    else:
        out_sum = other_sequences(lax.psum(grad_out, "dp")).astype(bf16)
        g_out = pick(
            place(
                gather_blocks(out_sum, group), [head ^ j for j in range(group)], 0, group
            ),
            plane,
            slab,
            0,
        ).astype(f32)
        lot = lax.psum_scatter(lot, "dp", scatter_dimension=1, tiled=True)
        lot = lax.psum(lot, "expert")
        qkv_sum = lax.psum_scatter(
            grad_qkv.astype(f32), "dp", scatter_dimension=0, tiled=True
        )
        qkv_sum = other_sequences(qkv_sum).astype(bf16)
        by_head = place(
            gather_blocks(qkv_sum, group), [head ^ j for j in range(group)], 1, group
        )
        spread = lambda x: lax.psum_scatter(
            x.astype(f32), "dp", scatter_dimension=1, tiled=True
        )
        blank = jnp.zeros_like(grad_down)
        down_out = spread(
            jnp.where(
                side == 0,
                jnp.concatenate([grad_down, blank], axis=1),
                jnp.concatenate([blank, grad_down], axis=1),
            )
        )
        first = spread(jnp.where(side == 0, grad_gate_up, jnp.zeros((), bf16)))
        last = spread(jnp.where(side == 1, grad_gate_up, jnp.zeros((), bf16)))
        gate_up_out = jnp.concatenate(
            [
                first[:, :, :ff_half],
                last[:, :, :ff_half],
                first[:, :, ff_half:],
                last[:, :, ff_half:],
            ],
            axis=2,
        )

    def of_heads(first, count):
        wide = q_cols + 2 * kv_cols
        return jnp.concatenate(
            [by_head[:, h * wide + first : h * wide + first + count] for h in range(group)], axis=1
        ).astype(f32)

    g_query = of_heads(0, q_cols)
    g_key = of_heads(q_cols, kv_cols)
    g_value = of_heads(q_cols + kv_cols, kv_cols)
    g_router, g_one, g_two = (
        jnp.transpose(lot[:experts_all]),
        lot[experts_all],
        lot[experts_all + 1],
    )
    loss_value = lot[experts_all + 2, 0] / (valid_count * width)

    return (
        activations,
        loss_value,
        grad_in,
        g_one,
        g_two,
        g_query,
        g_key,
        g_value,
        g_out,
        g_router,
        gate_up_out,
        down_out,
    )


def solution(mesh):
    placed = (
        P(("dp", "expert"), None),
        P(("dp", "expert"), None),
        P(("dp", "expert")),
        P(("dp", "expert"), None),
        P("dp"),
        P("dp"),
        P("dp", None),
        P("dp", None),
        P("dp", None),
        P("dp", None),
        P("dp", None),
        P("expert", "dp", None),
        P("expert", "dp", None),
    )
    return jax.shard_map(
        body,
        mesh=mesh,
        in_specs=placed,
        out_specs=(
            P(("dp", "expert"), None),
            P(),
            P(("dp", "expert"), None),
            P("dp"),
            P("dp"),
            P("dp", None),
            P("dp", None),
            P("dp", None),
            P("dp", None),
            P("dp", None),
            P("expert", "dp", None),
            P("expert", "dp", None),
        ),
        check_vma=False,
    )
```

```python
import functools

import jax
import jax.numpy as jnp
from jax import lax
from jax.experimental import pallas as pl
from jax.experimental.pallas import tpu as pltpu
from jax.sharding import PartitionSpec as P

H = 24
KVH = 8
HD = 64
FF = 512
TOP = 8
EXP_DEV = 3
SEQ_MIN = 1024

EPS = 1e-05
RESIDUAL = 0.22
SCORE_SCALE = 1.0 / 64.0
ROPE_BASE = 10000.0
NEG = -1000000000.0

f32 = jnp.float32
bf16 = jnp.bfloat16


def mm(spec, a, b):
    return jnp.einsum(spec, a, b, preferred_element_type=f32)


def rms_norm(states, gain):
    return states * lax.rsqrt(jnp.mean(states * states, axis=-1, keepdims=True) + EPS) * gain


def rope_tables(positions):
    half_dim = HD // 2
    frequencies = ROPE_BASE ** (-(2.0 * jnp.arange(half_dim, dtype=f32)) / HD)
    angles = frequencies[:, None] * positions[None, :]
    return jnp.cos(angles), jnp.sin(angles)


def send(x, axis, mask):
    count = lax.axis_size(axis)
    return lax.ppermute(x, axis, [(i, i ^ mask) for i in range(count)])


def gather_blocks(x, count):
    blocks = [x]
    for j in range(1, count):
        blocks.append(send(blocks[j - 1], "expert", 1) if j % 2 else send(x, "expert", j))
    return blocks


def scatter_sum(parts):
    total = None
    for j in range(0, len(parts), 2):
        chip = parts[j].astype(f32) + send(parts[j + 1], "expert", 1).astype(f32)
        if j:
            chip = send(chip.astype(bf16), "expert", j).astype(f32)
        total = chip if total is None else total + chip
    return total


def total_over(x, axis):
    mask = 1
    while mask < lax.axis_size(axis):
        x = x + send(x, axis, mask)
        mask *= 2
    return x


def place(blocks, starts, axis, size):
    width = blocks[0].shape[axis]
    shape = list(blocks[0].shape)
    shape[axis] = size * width
    out = jnp.zeros(shape, blocks[0].dtype)
    for block, start in zip(blocks, starts):
        out = lax.dynamic_update_slice_in_dim(out, block, start * width, axis)
    return out


def pick(x, index, width, axis):
    return lax.dynamic_slice_in_dim(x, index * width, width, axis)


def never(x):
    return (x != x).astype(jnp.int32)


CAP = 112
GATE_COLUMNS = 128
NT = (((1,), (1,)), ((), ()))
TN = (((0,), (0,)), ((), ()))
NN = (((1,), (0,)), ((), ()))


def dg(a, b, dims):
    return lax.dot_general(a, b, dims, preferred_element_type=f32)


def whole(shape):
    return pl.BlockSpec(shape, lambda *_: (0,) * len(shape))


def params(mib):
    return pltpu.CompilerParams(vmem_limit_bytes=mib << 20)


def select_rows(slot_row):
    row = lax.broadcasted_iota(jnp.int32, (CAP, slot_row.shape[1]), 0).astype(f32)
    return row == slot_row


def experts_kernel(me_ref, router_ref, gate_up_ref, down_ref, *refs):
    blocks, routes, refs = refs[:8], refs[8:16], refs[16:]
    parts, refs = refs[:8], refs[8:]
    arrived_ref, lin_ref, weighted_ref, slot_ref, gate_ref, count_ref, sel, made = refs
    step = pl.program_id(0)
    tok, width = blocks[0].shape

    @pl.when(step == 0)
    def _():
        first = me_ref[0] * EXP_DEV
        experts = router_ref.shape[0]
        which = lax.broadcasted_iota(jnp.int32, (experts, tok), 0)
        before = (
            lax.broadcasted_iota(jnp.int32, (tok, tok), 0)
            < lax.broadcasted_iota(jnp.int32, (tok, tok), 1)
        ).astype(bf16)
        count = jnp.zeros(count_ref.shape, jnp.int32)
        for s in range(8):
            logits = dg(router_ref[...], blocks[s][...], NT)
            names = routes[s][...]
            count = count + names[TOP:]
            routed = which == names[0:1, :]
            for k in range(1, TOP):
                routed = routed | (which == names[k : k + 1, :])
            logits = jnp.where(routed, logits, NEG)
            top = jnp.max(logits, axis=0, keepdims=True)
            grown = jnp.where(routed, jnp.exp(logits - top), 0.0)
            gates = grown / jnp.sum(grown, axis=0, keepdims=True)
            hots, picked = [], []
            for i in range(EXP_DEV):
                own = which == first + i
                hots.append(jnp.sum(jnp.where(own & routed, 1.0, 0.0), axis=0, keepdims=True))
                picked.append(jnp.sum(jnp.where(own, gates, 0.0), axis=0, keepdims=True))
            filler = jnp.zeros((8 - EXP_DEV, tok), f32)
            hot = jnp.concatenate(hots + [filler], axis=0)
            rank = dg(hot.astype(bf16), before, NN)
            slot = jnp.where(hot > 0.0, rank, -1.0)
            slot_ref[s] = slot
            gate_ref[s] = jnp.concatenate(picked + [filler], axis=0)
            for i in range(EXP_DEV):
                sel[s, i * CAP : (i + 1) * CAP, :] = select_rows(slot[i : i + 1, :]).astype(bf16)
        count_ref[...] = count

    at = pl.ds(pl.multiple_of(step * CAP, CAP), CAP)
    for s in range(8):
        arrived_ref[s, 0] = dg(sel[s, at, :], blocks[s][...], NN).astype(bf16)
    lin = dg(arrived_ref[:, 0].reshape(8 * CAP, width), gate_up_ref[0], NN)
    lin_ref[:, 0] = lin.reshape(8, CAP, lin.shape[1])
    half = lin.shape[1] // 2
    gate_part, up_part = lin[:, :half], lin[:, half:]
    hidden = gate_part * jax.nn.sigmoid(gate_part) * up_part
    for s in range(8):
        gate_row = gate_ref[s, pl.ds(step, 1), :]
        row_gate = jnp.sum(
            jnp.where(sel[s, at, :] > 0, gate_row, 0.0), axis=1, keepdims=True
        )
        weighted_ref[s, 0] = (row_gate * hidden[s * CAP : (s + 1) * CAP]).astype(bf16)
    out = dg(weighted_ref[:, 0].reshape(8 * CAP, half), down_ref[0], NN)
    made[:, at, :] = out.reshape(8, CAP, width).astype(bf16)

    @pl.when(step == EXP_DEV - 1)
    def _():
        for s in range(8):
            parts[s][...] = dg(sel[s], made[s], TN).astype(bf16)


def experts_forward(me, routes, router_t, blocks, gate_up_w, down_w):
    tok, width = blocks[0].shape
    cols, half = gate_up_w.shape[2], down_w.shape[1]
    by_expert = lambda w: pl.BlockSpec((8, 1, CAP, w), lambda e, *_: (0, e, 0, 0))
    rows = lambda w, t: jax.ShapeDtypeStruct((8, EXP_DEV, CAP, w), t)
    out = pl.pallas_call(
        experts_kernel,
        grid_spec=pltpu.PrefetchScalarGridSpec(
            num_scalar_prefetch=1,
            grid=(EXP_DEV,),
            in_specs=[
                whole(router_t.shape),
                pl.BlockSpec((1, width, cols), lambda e, *_: (e, 0, 0)),
                pl.BlockSpec((1, half, width), lambda e, *_: (e, 0, 0)),
            ]
            + [whole((tok, width))] * 8
            + [whole(routes[0].shape)] * 8,
            out_specs=[whole((tok, width))] * 8
            + [by_expert(width), by_expert(cols), by_expert(half)]
            + [whole((8, 8, tok))] * 2
            + [whole((8, tok))],
            scratch_shapes=[
                pltpu.VMEM((8, EXP_DEV * CAP, tok), bf16),
                pltpu.VMEM((8, EXP_DEV * CAP, width), bf16),
            ],
        ),
        out_shape=[jax.ShapeDtypeStruct((tok, width), bf16)] * 8
        + [rows(width, bf16), rows(cols, f32), rows(half, bf16)]
        + [jax.ShapeDtypeStruct((8, 8, tok), f32)] * 2
        + [jax.ShapeDtypeStruct((8, tok), jnp.int32)],
        compiler_params=params(60),
        cost_estimate=pl.CostEstimate(
            flops=11 * 10**9, bytes_accessed=40 * 10**6, transcendentals=10**6
        ),
        name="experts_forward",
    )(me, router_t, gate_up_w, down_w, *blocks, *routes)
    return list(out[:8]), out[8:13], out[13]


def experts_back_kernel(me_ref, slot_ref, gate_ref, lin_ref, gate_up_ref, down_ref, *refs):
    blocks, refs = refs[:8], refs[8:]
    parts, refs = refs[:8], refs[8:]
    arrived_ref, lin_grad_ref, sel, made = refs
    step = pl.program_id(0)
    tok, width = blocks[0].shape
    half = down_ref.shape[1]
    at = pl.ds(pl.multiple_of(step * CAP, CAP), CAP)

    for s in range(8):
        sel[s, at, :] = select_rows(slot_ref[s, pl.ds(step, 1), :]).astype(bf16)
        arrived_ref[s, 0] = dg(sel[s, at, :], blocks[s][...], NN).astype(bf16)
    pull = dg(arrived_ref[:, 0].reshape(8 * CAP, width), down_ref[0], NT)
    lin = lin_ref[:, 0].reshape(8 * CAP, 2 * half)
    gate_part, up_part = lin[:, :half], lin[:, half:]
    sig = jax.nn.sigmoid(gate_part)
    act = gate_part * sig
    row_gg = RESIDUAL * jnp.sum(act * up_part * pull, axis=1, keepdims=True)
    slope = sig * (1.0 + gate_part * (1.0 - sig))
    own = me_ref[0] * EXP_DEV + step
    column = lax.broadcasted_iota(jnp.int32, (CAP, made.shape[2] - width), 1)
    for s in range(8):
        mine = slice(s * CAP, (s + 1) * CAP)
        chosen = sel[s, at, :] > 0
        gate_row = gate_ref[s, pl.ds(step, 1), :]
        row_gate = jnp.sum(jnp.where(chosen, gate_row, 0.0), axis=1, keepdims=True)
        made[s, at, width:] = jnp.where(column == own, row_gg[mine], 0.0).astype(bf16)
        hidden_grad = RESIDUAL * row_gate * pull[mine]
        lin_grad_ref[s, 0, :, :half] = (hidden_grad * up_part[mine] * slope[mine]).astype(bf16)
        lin_grad_ref[s, 0, :, half:] = (hidden_grad * act[mine]).astype(bf16)
    out = dg(lin_grad_ref[:, 0].reshape(8 * CAP, 2 * half), gate_up_ref[0], NT)
    made[:, at, :width] = out.reshape(8, CAP, width).astype(bf16)

    @pl.when(step == EXP_DEV - 1)
    def _():
        for s in range(8):
            parts[s][...] = dg(sel[s], made[s], TN).astype(bf16)


def experts_backward(me, slot, gate, lin, blocks, gate_up_w, down_w):
    tok, width = blocks[0].shape
    cols, half = gate_up_w.shape[2], down_w.shape[1]
    wide = width + GATE_COLUMNS
    by_expert = lambda w: pl.BlockSpec((8, 1, CAP, w), lambda e, *_: (0, e, 0, 0))
    rows = lambda w: jax.ShapeDtypeStruct((8, EXP_DEV, CAP, w), bf16)
    out = pl.pallas_call(
        experts_back_kernel,
        grid_spec=pltpu.PrefetchScalarGridSpec(
            num_scalar_prefetch=1,
            grid=(EXP_DEV,),
            in_specs=[
                whole(slot.shape),
                whole(gate.shape),
                by_expert(cols),
                pl.BlockSpec((1, width, cols), lambda e, *_: (e, 0, 0)),
                pl.BlockSpec((1, half, width), lambda e, *_: (e, 0, 0)),
            ]
            + [whole((tok, width))] * 8,
            out_specs=[whole((tok, wide))] * 8 + [by_expert(width), by_expert(cols)],
            scratch_shapes=[
                pltpu.VMEM((8, EXP_DEV * CAP, tok), bf16),
                pltpu.VMEM((8, EXP_DEV * CAP, wide), bf16),
            ],
        ),
        out_shape=[jax.ShapeDtypeStruct((tok, wide), bf16)] * 8 + [rows(width), rows(cols)],
        compiler_params=params(60),
        cost_estimate=pl.CostEstimate(
            flops=11 * 10**9, bytes_accessed=40 * 10**6, transcendentals=10**6
        ),
        name="experts_backward",
    )(me, slot, gate, lin, gate_up_w, down_w, *blocks)
    return list(out[:8]), out[8:]


def expert_weights_kernel(after_ref, *refs):
    chunks = len(refs) // 4
    gate_up_ref, down_ref = refs[-2:]
    gate_up, down = None, None
    for c in range(chunks):
        states, lin_grad, weighted, grads = [
            r[:, 0].reshape(8 * CAP, r.shape[3]) for r in refs[4 * c : 4 * c + 4]
        ]
        one, two = dg(states, lin_grad, TN), dg(weighted, grads, TN)
        gate_up = one if gate_up is None else gate_up + one
        down = two if down is None else down + two
    gate_up_ref[0] = gate_up.astype(bf16)
    down_ref[0] = (RESIDUAL * down).astype(bf16)


def expert_weights(after, chunks):
    width, cols, half = [chunks[0][i].shape[3] for i in range(3)]
    by_expert = lambda w: pl.BlockSpec((8, 1, CAP, w), lambda e, *_: (0, e, 0, 0))
    flat = [x for chunk in chunks for x in chunk]
    return pl.pallas_call(
        expert_weights_kernel,
        grid_spec=pltpu.PrefetchScalarGridSpec(
            num_scalar_prefetch=1,
            grid=(EXP_DEV,),
            in_specs=[by_expert(x.shape[3]) for x in flat],
            out_specs=[
                pl.BlockSpec((1, width, cols), lambda e, *_: (e, 0, 0)),
                pl.BlockSpec((1, half, width), lambda e, *_: (e, 0, 0)),
            ],
        ),
        out_shape=[
            jax.ShapeDtypeStruct((EXP_DEV, width, cols), bf16),
            jax.ShapeDtypeStruct((EXP_DEV, half, width), bf16),
        ],
        compiler_params=params(60),
        cost_estimate=pl.CostEstimate(
            flops=14 * 10**9, bytes_accessed=40 * 10**6, transcendentals=0
        ),
        name="expert_weights",
    )(after, *flat)


MESH = pl.DeviceIdType.MESH


def flip(index, mask):
    return index + mask - 2 * mask * lax.rem(lax.div(index, mask), 2)


def greet(partners):
    barrier = pltpu.get_barrier_semaphore()
    for partner in partners:
        pl.semaphore_signal(barrier, inc=1, device_id=partner, device_id_type=MESH)
    pl.semaphore_wait(barrier, len(partners))


class Wire:
    def __init__(self, send_sem, recv_sem):
        self.send_sem, self.recv_sem, self.copies = send_sem, recv_sem, []

    def start(self, src, dst, partner):
        i = len(self.copies)
        copy = pltpu.make_async_remote_copy(
            src_ref=src,
            dst_ref=dst,
            send_sem=self.send_sem.at[i],
            recv_sem=self.recv_sem.at[i],
            device_id=partner,
            device_id_type=MESH,
        )
        copy.start()
        self.copies.append(copy)
        return copy

    def finish(self):
        for copy in self.copies:
            copy.wait_send()


def comm_call(
    kernel, name, number, copies, in_specs, out_specs, out_shape, scratch, cost, aliases={}
):
    return pl.pallas_call(
        kernel,
        in_specs=in_specs,
        out_specs=out_specs,
        out_shape=out_shape,
        scratch_shapes=list(scratch) + [pltpu.SemaphoreType.DMA((copies,))] * 2,
        compiler_params=pltpu.CompilerParams(
            vmem_limit_bytes=60 << 20, collective_id=number, has_side_effects=True
        ),
        cost_estimate=pl.CostEstimate(flops=cost, bytes_accessed=cost, transcendentals=0),
        input_output_aliases=aliases,
        name=name,
    )


ANYWHERE = pl.BlockSpec(memory_space=pl.ANY)
ON_CHIP = pl.BlockSpec(memory_space=pltpu.VMEM)


def add_into(rows, out, first, *others, step=32):
    @pl.loop(0, rows // step)
    def _(i):
        at = pl.ds(pl.multiple_of(i * step, step), step)
        total = first[at].astype(f32)
        for other in others:
            total = total + other[at].astype(f32)
        out[at] = total.astype(out.dtype)


def plane_places():
    z = lax.axis_index("dp")
    return z, flip(z, 1), lax.rem(z + 2, 4), lax.div(z, 2), lax.rem(z, 2)


def stripe(index, size):
    return pl.ds(pl.multiple_of(index * size, size), size)


class WeightsIn:
    def __init__(
        self,
        wire,
        experts,
        w_gate_up,
        w_down,
        gate_up,
        down,
        stage,
        stage_down,
        sems,
        direct=False,
    ):
        z, beside, opposite, side, low = plane_places()
        slab, part = w_gate_up.shape[1], gate_up.shape[2] // 2
        rows = w_down.shape[1]
        self.wire, self.gate_up, self.slab, self.opposite = wire, gate_up, slab, opposite
        self.beside = {"dp": beside}
        self.crossing, self.arriving, self.stores = [], [], []
        self.direct = direct

        def columns(i, which, p):
            return w_gate_up.at[i, :, stripe(2 * p + which, part)]

        def spot(i, p):
            return gate_up.at[i, stripe(z, slab), pl.ds(p * part, part)]

        self.loads = loads = []
        for n, i in enumerate(experts):
            for p in range(2):
                loads.append(
                    pltpu.make_async_copy(
                        columns(i, side, p),
                        stage.at[n, :, pl.ds(p * part, part)],
                        sems.at[n, p],
                    )
                )
            loads.append(pltpu.make_async_copy(w_down.at[i], stage_down.at[n], sems.at[n, 2]))
            for load in loads[-3:]:
                load.start()
            if direct:
                corner = {"dp": flip(opposite, 1)}
                for p in range(2):
                    self.arriving.append(wire.start(columns(i, 1 - side, p), spot(i, p), corner))
            self.crossing.append(
                (
                    i,
                    [
                        wire.start(columns(i, 1 - side, p), spot(i, p), {"dp": opposite})
                        for p in range(2)
                    ],
                )
            )
            for p in range(2):
                self.arriving.append(wire.start(columns(i, side, p), spot(i, p), self.beside))
            here = down.at[i, stripe(low, rows)]
            self.arriving.append(wire.start(w_down.at[i], here, self.beside))
            self.stores.append(
                pltpu.make_async_copy(
                    stage.at[n], gate_up.at[i, stripe(z, slab)], sems.at[n, 3]
                )
            )
            self.stores.append(pltpu.make_async_copy(stage_down.at[n], here, sems.at[n, 4]))

    def finish(self):
        for load in self.loads:
            load.wait()
        for store in self.stores:
            store.start()
        for i, copies in self.crossing:
            for copy in copies:
                copy.wait_recv()
            if self.direct:
                continue
            piece = self.gate_up.at[i, stripe(self.opposite, self.slab)]
            self.arriving.append(self.wire.start(piece, piece, self.beside))
        for copy in self.arriving:
            copy.wait_recv()
        for store in self.stores:
            store.wait()


def weights_scratch(count, slab, columns, rows, width):
    return [
        pltpu.VMEM((count, slab, columns), bf16),
        pltpu.VMEM((count, rows, width), bf16),
        pltpu.SemaphoreType.DMA((count, 5)),
    ]


class GradsOut:
    def __init__(self, wire, i, grad_gate_up, grad_down, out, out_down, got, own, downs, sems):
        z, beside, opposite, side, low = plane_places()
        slab, rows = out.shape[0], out_down.shape[0]
        self.wire, self.side, self.across = wire, side, {"dp": opposite}
        self.out, self.out_down, self.got, self.own, self.downs = out, out_down, got, own, downs

        def slab_of(plane):
            return grad_gate_up.at[i, stripe(plane, slab)]

        def rows_of(which):
            return grad_down.at[i, stripe(which, rows)]

        to = {"dp": beside}
        self.loads = [
            pltpu.make_async_copy(slab_of(opposite), own.at[0], sems.at[0]),
            pltpu.make_async_copy(slab_of(z), own.at[1], sems.at[1]),
            pltpu.make_async_copy(rows_of(low), downs.at[0], sems.at[2]),
        ]
        for load in self.loads:
            load.start()
        self.copies = [
            wire.start(slab_of(flip(opposite, 1)), got.at[0], to),
            wire.start(slab_of(beside), got.at[1], to),
            wire.start(rows_of(1 - low), downs.at[1], to),
        ]

    def cross(self):
        self.loads[0].wait()
        self.copies[0].wait_recv()
        slab = self.out.shape[0]
        add_into(slab, self.own.at[2], self.own.at[0], self.got.at[0])
        self.copies.append(self.wire.start(self.own.at[2], self.got.at[2], self.across))

    def finish(self):
        part = self.out.shape[1] // 4
        slab = self.out.shape[0]
        self.loads[1].wait()
        self.copies[1].wait_recv()
        self.copies[3].wait_recv()
        out, got, own, side = self.out, self.got, self.own, self.side

        @pl.loop(0, slab // 32)
        def _(r):
            at = pl.ds(pl.multiple_of(r * 32, 32), 32)
            for p in range(2):
                lanes = pl.ds(p * part, part)
                total = own[1, at, lanes].astype(f32) + got[1, at, lanes].astype(f32)
                out[at, stripe(2 * p + side, part)] = total.astype(bf16)
                out[at, stripe(2 * p + 1 - side, part)] = got[2, at, lanes]

        self.loads[2].wait()
        self.copies[2].wait_recv()
        add_into(self.out_down.shape[0], self.out_down, self.downs.at[0], self.downs.at[1])


def grads_scratch(slab, columns, rows, width):
    return [
        pltpu.VMEM((3, slab, columns), bf16),
        pltpu.VMEM((3, slab, columns), bf16),
        pltpu.VMEM((2, rows, width), bf16),
        pltpu.SemaphoreType.DMA((3,)),
    ]


def grads_shapes(grad_gate_up, grad_down):
    slab, columns = grad_gate_up.shape[1] // 4, grad_gate_up.shape[2]
    rows, width = grad_down.shape[1] // 2, grad_down.shape[2]
    return (
        [jax.ShapeDtypeStruct((slab, 2 * columns), bf16), jax.ShapeDtypeStruct((rows, width), bf16)],
        grads_scratch(slab, columns, rows, width),
    )


def neighbours(half):
    e, z = lax.axis_index("expert"), lax.axis_index("dp")
    across = lax.rem(z + half, lax.axis_size("dp"))
    return [{"expert": flip(e, m)} for m in (1, 2, 4)] + [{"dp": across}]


class Several:
    def __init__(self, copies):
        self.copies = copies

    def wait_recv(self):
        for copy in self.copies:
            copy.wait_recv()


def exchange_plane(wire, partners, near, far, begin=None):
    core, side_x, side_y, across = partners

    def cut(ref, h):
        rows = ref.shape[0] // 2
        return ref.at[pl.ds(h * rows, rows)]

    def start(src, dst, to, h=None):
        if h is not None:
            src, dst = [[cut(ref, h) for ref in refs] for refs in (src, dst)]
        return Several([wire.start(x, y, to) for x, y in zip(src, dst)])

    z_low = start(near[0], far[0], across, 0)
    z_high = start(near[0], far[0], across, 1)
    near_x_low = start(near[0], near[2], side_x, 0)
    near_y_high = start(near[0], near[4], side_y, 1)
    near_x_high = start(near[0], near[2], side_x, 1)
    near_y_low = start(near[0], near[4], side_y, 0)
    last = [start(near[0], near[1], core)]
    cargo = begin() if begin else None
    near_x_low.wait_recv()
    near_diag_low = start(near[2], near[6], side_y, 0)
    near_y_high.wait_recv()
    near_diag_high = start(near[4], near[6], side_x, 1)
    near_x_high.wait_recv()
    last.append(start(near[2], near[3], core))
    near_y_low.wait_recv()
    last.append(start(near[4], near[5], core))
    z_low.wait_recv()
    far_x_low = start(far[0], far[2], side_x, 0)
    far_y_low = start(far[0], far[4], side_y, 0)
    near_diag_low.wait_recv()
    near_diag_high.wait_recv()
    last.append(start(near[6], near[7], core))
    z_high.wait_recv()
    far_x_high = start(far[0], far[2], side_x, 1)
    far_y_high = start(far[0], far[4], side_y, 1)
    last.append(start(far[0], far[1], core))
    far_x_low.wait_recv()
    far_diag_low = start(far[2], far[6], side_y, 0)
    far_y_low.wait_recv()
    far_y_high.wait_recv()
    far_diag_high = start(far[4], far[6], side_x, 1)
    last.append(start(far[4], far[5], core))
    far_x_high.wait_recv()
    last.append(start(far[2], far[3], core))
    far_diag_low.wait_recv()
    far_diag_high.wait_recv()
    last.append(start(far[6], far[7], core))
    for copy in last:
        copy.wait_recv()
    if cargo:
        cargo.finish()


def plane_gather_kernel(half, experts, count, *refs):
    inputs, refs = refs[:count], refs[count:]
    if experts:
        (w_gate_up, w_down), refs = refs[:2], refs[4:]
    outs, refs = refs[: 15 * count], refs[15 * count :]
    near = [list(inputs)] + [list(outs[j * count : (j + 1) * count]) for j in range(7)]
    far = [list(outs[j * count : (j + 1) * count]) for j in range(7, 15)]
    wire = Wire(*refs[-2:])
    partners = neighbours(half)
    begin = None
    if experts:
        greet(partners + [{"dp": plane_places()[1]}])
        begin = lambda: WeightsIn(wire, experts, w_gate_up, w_down, *refs[:5])
    else:
        greet(partners)
    exchange_plane(wire, partners, near, far, begin)
    wire.finish()


def plane_gather(inputs, half, number, name, experts=(), weights=(), filled=()):
    count, size = len(inputs), inputs[0].size
    blocks = [jax.ShapeDtypeStruct(x.shape, x.dtype) for x in inputs]
    scratch, aliases = [], {}
    if experts:
        (w_gate_up, w_down), (gate_up, down) = weights, filled
        scratch = weights_scratch(
            len(experts), w_gate_up.shape[1], gate_up.shape[2], w_down.shape[1], down.shape[2]
        )
        aliases = {count + 2: 15 * count, count + 3: 15 * count + 1}
    out = comm_call(
        functools.partial(plane_gather_kernel, half, experts, count),
        name,
        number,
        22 * count + 6 * len(experts),
        [ANYWHERE] * (count + len(weights) + len(filled)),
        [ANYWHERE] * (15 * count + len(filled)),
        blocks * 15 + [jax.ShapeDtypeStruct(x.shape, x.dtype) for x in filled],
        scratch,
        80 * size,
        aliases,
    )(*inputs, *weights, *filled)
    pairs = []
    for n, x in enumerate(inputs):
        own = out[n : 15 * count : count]
        pairs.append(([x] + list(own[:7]), list(own[7:])))
    return pairs, out[15 * count :]


def plane_scatter_kernel(half, i, *refs):
    parts = {"near": refs[:8], "far": refs[8:16]}
    refs = refs[16:]
    carried = ()
    if i is not None:
        carried, refs = refs[:2] + refs[3:5] + refs[11:15], refs[2:3] + refs[5:11] + refs[15:]
    out, core_in, sums, diag_in, last_in, z_out, z_in = refs[:7]
    wire = Wire(*refs[7:])
    core, side_x, side_y, across = partners = neighbours(half)
    rows = out.shape[0] // 2
    cut = rows // 2
    low, high = pl.ds(0, cut), pl.ds(cut, cut)
    if carried:
        greet(partners + [{"dp": plane_places()[1]}])
        cargo = GradsOut(wire, i, *carried)
    else:
        greet(partners)
    segments = [(kind, h) for kind in ("far", "near") for h in range(2)]
    from_core, from_diag, from_last, from_z = {}, {}, {}, {}

    def part(s, j):
        kind, h = segments[s]
        return parts[kind][j].at[pl.ds(h * rows, rows)]

    for s in range(4):
        for k in (3, 1, 2, 0):
            from_core[s, k] = wire.start(part(s, 2 * k + 1), core_in.at[s, k], core)

    def chip_sum(s, k):
        from_core[s, k].wait_recv()
        add_into(rows, sums.at[s, k], part(s, 2 * k), core_in.at[s, k])

    def enter(s):
        chip_sum(s, 3)
        from_diag[s, 0] = wire.start(sums.at[s, 3, low], diag_in.at[s, 0], side_x)
        from_diag[s, 1] = wire.start(sums.at[s, 3, high], diag_in.at[s, 1], side_y)
        chip_sum(s, 1)
        from_last[s, 0] = wire.start(sums.at[s, 1, low], last_in.at[s, 0, low], side_x)
        chip_sum(s, 2)
        from_last[s, 1] = wire.start(sums.at[s, 2, high], last_in.at[s, 1, high], side_y)

    def turn(s):
        from_diag[s, 1].wait_recv()
        add_into(cut, sums.at[s, 1, high], sums.at[s, 1, high], diag_in.at[s, 1])
        from_last[s, 2] = wire.start(sums.at[s, 1, high], last_in.at[s, 0, high], side_x)
        from_diag[s, 0].wait_recv()
        add_into(cut, sums.at[s, 2, low], sums.at[s, 2, low], diag_in.at[s, 0])
        from_last[s, 3] = wire.start(sums.at[s, 2, low], last_in.at[s, 1, low], side_y)

    def leave(s):
        kind, h = segments[s]
        from_core[s, 0].wait_recv()
        for i in range(4):
            from_last[s, i].wait_recv()
        target = z_out.at[h] if kind == "far" else out.at[pl.ds(h * rows, rows)]
        add_into(rows, target, part(s, 0), core_in.at[s, 0], last_in.at[s, 0], last_in.at[s, 1])
        if kind == "far":
            from_z[h] = wire.start(z_out.at[h], z_in.at[h], across)

    for step, s in (
        (enter, 0),
        (enter, 1),
        (turn, 0),
        (enter, 2),
        (turn, 1),
        (leave, 0),
        (enter, 3),
        (leave, 1),
        (turn, 2),
        (turn, 3),
        (leave, 2),
        (leave, 3),
    ):
        step(s)
        if carried and (step, s) == (leave, 1):
            cargo.cross()
    for h in range(2):
        from_z[h].wait_recv()
        target = out.at[pl.ds(h * rows, rows)]
        add_into(rows, target, target, z_in.at[h])
    if carried:
        cargo.finish()
    wire.finish()


def plane_scatter(near, far, half, number, name, i=None, grads=()):
    rows, width = near[0].shape
    specs = [ON_CHIP, ANYWHERE] * 8
    block = (rows // 2, width)
    shapes, scratch = grads_shapes(*grads) if grads else ([], [])
    return comm_call(
        functools.partial(plane_scatter_kernel, half, i),
        name,
        number,
        42 + 2 * len(grads),
        specs + [ANYWHERE] * len(grads),
        [ON_CHIP] * (1 + len(shapes)),
        [jax.ShapeDtypeStruct((rows, width), f32)] + shapes,
        [
            pltpu.VMEM((4, 4) + block, bf16),
            pltpu.VMEM((4, 4) + block, bf16),
            pltpu.VMEM((4, 2, rows // 4, width), bf16),
            pltpu.VMEM((4, 2) + block, bf16),
            pltpu.VMEM((2,) + block, bf16),
            pltpu.VMEM((2,) + block, bf16),
        ]
        + scratch,
        50 * rows * width,
    )(*near, *far, *grads)


def chip_partners():
    e = lax.axis_index("expert")
    return [{"expert": flip(e, m)} for m in (1, 2)]


def exchange_seq(wire, group, x_ref, out, between=None, steps=()):
    head = lax.rem(lax.axis_index("expert"), group)
    core, side_x = chip_partners()
    rows = x_ref.shape[0]
    cut = rows // 2
    mine = pl.multiple_of(head * rows, rows)
    other = pl.multiple_of(flip(head, 2) * rows, rows)
    crossing = [
        wire.start(x_ref.at[pl.ds(h * cut, cut)], out.at[pl.ds(mine + h * cut, cut)], side_x)
        for h in range(2)
    ]
    last = [wire.start(x_ref, out.at[pl.ds(mine, rows)], core)]
    out[pl.ds(mine, rows), :] = x_ref[...]
    if between:
        between()
    for h in range(2):
        if steps:
            steps[h]()
        crossing[h].wait_recv()
        piece = out.at[pl.ds(other + h * cut, cut)]
        last.append(wire.start(piece, piece, core))
    if steps:
        steps[2]()
    for copy in last:
        copy.wait_recv()


def seq_gather_kernel(group, x_ref, out, send_sem, recv_sem):
    wire = Wire(send_sem, recv_sem)
    greet(chip_partners())
    exchange_seq(wire, group, x_ref, out)
    wire.finish()


def seq_gather(x, group, number, name):
    rows, width = x.shape
    return comm_call(
        functools.partial(seq_gather_kernel, group),
        name,
        number,
        5,
        [ON_CHIP],
        ON_CHIP,
        jax.ShapeDtypeStruct((group * rows, width), x.dtype),
        [],
        20 * x.size,
    )(x)


def sum_seq(wire, group, x_ref, out, core_in, sums, last_in, between=None):
    head = lax.rem(lax.axis_index("expert"), group)
    core, side_x = chip_partners()
    rows = out.shape[0]
    cut = rows // 2

    def part(block, h):
        return x_ref.at[pl.ds(pl.multiple_of(block * rows + h * cut, cut), cut)]

    crossing = [
        wire.start(part(flip(flip(head, 2), 1), h), core_in.at[1, h], core) for h in range(2)
    ]
    near = [wire.start(part(flip(head, 1), h), core_in.at[0, h], core) for h in range(2)]
    last = []
    for h in range(2):
        crossing[h].wait_recv()
        add_into(cut, sums.at[h], part(flip(head, 2), h), core_in.at[1, h])
        last.append(wire.start(sums.at[h], last_in.at[h], side_x))
    if between:
        between()
    for h in range(2):
        near[h].wait_recv()
        last[h].wait_recv()
        add_into(
            cut, out.at[pl.ds(h * cut, cut)], part(head, h), core_in.at[0, h], last_in.at[h]
        )


def seq_scatter_kernel(group, x_ref, out, core_in, sums, last_in, send_sem, recv_sem):
    wire = Wire(send_sem, recv_sem)
    greet(chip_partners())
    sum_seq(wire, group, x_ref, out, core_in, sums, last_in)
    wire.finish()


def seq_scratch(rows, width):
    piece = (rows // 2, width)
    return [
        pltpu.VMEM((2, 2) + piece, bf16),
        pltpu.VMEM((2,) + piece, bf16),
        pltpu.VMEM((2,) + piece, bf16),
    ]


def seq_scatter(x, group, number, name):
    rows, width = x.shape[0] // group, x.shape[1]
    return comm_call(
        functools.partial(seq_scatter_kernel, group),
        name,
        number,
        6,
        [ON_CHIP],
        ON_CHIP,
        jax.ShapeDtypeStruct((rows, width), f32),
        seq_scratch(rows, width),
        20 * rows * width,
    )(x)


def entry_kernel(group, x_ref, qkv_in, out_in, seq, qkv, out_slice, send_sem, recv_sem):
    wire = Wire(send_sem, recv_sem)
    e, z = lax.axis_index("expert"), lax.axis_index("dp")
    head, row = lax.rem(e, group), lax.div(e, group)
    side_y = {"expert": flip(e, 4)}
    top = 3
    slab = qkv_in.shape[0]
    cut = slab // 2
    greet(chip_partners() + [side_y] + [{"dp": lax.rem(z + k, 4)} for k in range(1, 4)])
    mine = pl.ds(pl.multiple_of(row * cut, cut), cut)

    def spot(plane):
        return qkv.at[pl.ds(pl.multiple_of(plane * slab + row * cut, cut), cut)]

    def copy(n, src, dst, to):
        return pltpu.make_async_remote_copy(
            src_ref=src,
            dst_ref=dst,
            send_sem=send_sem.at[n],
            recv_sem=recv_sem.at[n],
            device_id=to,
            device_id_type=MESH,
        )

    up, down = {"dp": lax.rem(z + 1, 4)}, {"dp": lax.rem(z + 3, 4)}
    hops = []
    for sign, to in ((1, up), (-1, down)):
        for d in (1, 2, 3):
            n = 5 + len(hops) * 2
            held, got = lax.rem(z - sign * (d - 1) + 8, 4), lax.rem(z - sign * d + 8, 4)
            source = qkv_in.at[mine] if d == 1 else spot(held)
            edge = z < top if sign > 0 else z > 0
            held_there = z >= d - 1 if sign > 0 else z <= top - (d - 1)
            arrives = z >= d if sign > 0 else z <= top - d
            hops.append(
                (
                    jnp.logical_and(edge, held_there),
                    arrives,
                    copy(n, source, spot(held), to),
                    copy(n + 1, spot(got), spot(got), side_y),
                )
            )
    for sends, _, hop, _ in (hops[0], hops[3]):
        pl.when(sends)(hop.start)

    owner = z == head
    out_up = copy(17, out_slice.at[mine], out_slice.at[mine], up)
    out_down = copy(18, out_slice.at[mine], out_slice.at[mine], down)
    own_up = copy(17, out_in.at[mine], out_slice.at[mine], up)
    own_down = copy(18, out_in.at[mine], out_slice.at[mine], down)
    swap = copy(19, out_slice.at[mine], out_slice.at[mine], side_y)
    pl.when(jnp.logical_and(owner, z < top))(own_up.start)
    pl.when(jnp.logical_and(owner, z > 0))(own_down.start)

    @pl.when(owner)
    def _():
        out_slice[...] = out_in[...]

    qkv[pl.ds(pl.multiple_of(z * slab, slab), slab), :] = qkv_in[...]

    def relay(d):
        for way in (0, 3):
            _, arrives, hop, across = hops[way + d]

            @pl.when(arrives)
            def _():
                hop.wait_recv()
                across.start()

            if d < 2:
                sends, _, following, _ = hops[way + d + 1]
                pl.when(sends)(following.start)

        @pl.when(z == head + d + 1)
        def _():
            out_up.wait_recv()
            pl.when(z < top)(out_up.start)
            swap.start()

        @pl.when(z == head - d - 1)
        def _():
            out_down.wait_recv()
            pl.when(z > 0)(out_down.start)
            swap.start()

    steps = [functools.partial(relay, d) for d in range(3)]
    exchange_seq(wire, group, x_ref, seq, steps=steps)
    for sends, arrives, hop, across in hops:
        pl.when(arrives)(across.wait)
        pl.when(sends)(hop.wait_send)
    pl.when(jnp.logical_not(owner))(swap.wait)
    pl.when(jnp.logical_and(z >= head, z < top))(out_up.wait_send)
    pl.when(jnp.logical_and(z <= head, z > 0))(out_down.wait_send)
    wire.finish()


def attention_entry(x, qkv_slice, w_out, group):
    rows, width = x.shape
    slab, columns = qkv_slice.shape
    return comm_call(
        functools.partial(entry_kernel, group),
        "attention_entry",
        8,
        20,
        [ON_CHIP] * 3,
        [ON_CHIP] * 3,
        [
            jax.ShapeDtypeStruct((group * rows, width), bf16),
            jax.ShapeDtypeStruct((4 * slab, columns), bf16),
            jax.ShapeDtypeStruct((slab, width), bf16),
        ],
        [],
        40 * x.size,
    )(x, qkv_slice, w_out)


def scatter_weights_kernel(group, experts, x_ref, w_gate_up, w_down, out, gate_up, down, *refs):
    wire = Wire(*refs[6:])
    _, beside, opposite, _, _ = plane_places()
    greet(chip_partners() + [{"dp": p} for p in (beside, opposite, flip(opposite, 1))])
    cargo = WeightsIn(wire, experts, w_gate_up, w_down, gate_up, down, *refs[3:6], direct=True)
    sum_seq(wire, group, x_ref, out, *refs[:3])
    cargo.finish()
    wire.finish()


def seq_scatter_weights(x, group, experts, w_gate_up, w_down):
    rows, width = x.shape[0] // group, x.shape[1]
    count, slab, columns = w_gate_up.shape
    ff_rows = w_down.shape[1]
    return comm_call(
        functools.partial(scatter_weights_kernel, group, experts),
        "scatter_branch_weights",
        9,
        6 + 7 * len(experts),
        [ON_CHIP, ANYWHERE, ANYWHERE],
        [ON_CHIP, ANYWHERE, ANYWHERE],
        [
            jax.ShapeDtypeStruct((rows, width), f32),
            jax.ShapeDtypeStruct((count, 4 * slab, columns // 2), bf16),
            jax.ShapeDtypeStruct((count, 2 * ff_rows, width), bf16),
        ],
        seq_scratch(rows, width)
        + weights_scratch(len(experts), slab, columns // 2, ff_rows, width),
        40 * rows * width,
    )(x, w_gate_up, w_down)


def gather_grads_kernel(group, i, x_ref, grad_gate_up, grad_down, seq, out, out_down, *refs):
    wire = Wire(*refs[4:])
    _, beside, opposite, _, _ = plane_places()
    greet(chip_partners() + [{"dp": beside}, {"dp": opposite}])
    cargo = GradsOut(wire, i, grad_gate_up, grad_down, out, out_down, *refs[:4])
    exchange_seq(wire, group, x_ref, seq, cargo.cross)
    cargo.finish()
    wire.finish()


def seq_gather_grads(x, group, i, grad_gate_up, grad_down):
    rows, width = x.shape
    shapes, scratch = grads_shapes(grad_gate_up, grad_down)
    return comm_call(
        functools.partial(gather_grads_kernel, group, i),
        "gather_branch_grads",
        10,
        9,
        [ON_CHIP, ANYWHERE, ANYWHERE],
        [ON_CHIP] * 3,
        [jax.ShapeDtypeStruct((group * rows, width), x.dtype)] + shapes,
        scratch,
        40 * x.size,
    )(x, grad_gate_up, grad_down)


def scatter_grads_kernel(
    group, i, x_ref, grad_gate_up, grad_down, once, total, out, out_down, twice, *refs
):
    wire = Wire(*refs[8:])
    other = refs[7]
    side_y = {"expert": flip(lax.axis_index("expert"), group)}
    _, beside, opposite, _, _ = plane_places()
    greet(chip_partners() + [side_y, {"dp": beside}, {"dp": opposite}])
    swap = wire.start(once, other, side_y)
    cargo = GradsOut(wire, i, grad_gate_up, grad_down, out, out_down, *refs[3:7])
    sum_seq(wire, group, x_ref, total, *refs[:3], cargo.cross)
    cargo.finish()
    swap.wait_recv()
    add_into(once.shape[0], twice, once, other)
    wire.finish()


def seq_scatter_grads(x, group, i, grad_gate_up, grad_down, once):
    rows, width = x.shape[0] // group, x.shape[1]
    shapes, scratch = grads_shapes(grad_gate_up, grad_down)
    return comm_call(
        functools.partial(scatter_grads_kernel, group, i),
        "scatter_normed_grads",
        11,
        11,
        [ON_CHIP, ANYWHERE, ANYWHERE, ON_CHIP],
        [ON_CHIP] * 4,
        [jax.ShapeDtypeStruct((rows, width), f32)]
        + shapes
        + [jax.ShapeDtypeStruct(once.shape, bf16)],
        seq_scratch(rows, width) + scratch + [pltpu.VMEM(once.shape, bf16)],
        40 * rows * width,
    )(x, grad_gate_up, grad_down, once)


def start_kernel(replicas, small_ref, small_out, send_sem, recv_sem):
    wire = Wire(send_sem, recv_sem)
    z = lax.axis_index("dp")
    planes = [{"dp": lax.rem(z + k, replicas)} for k in range(1, replicas)]
    greet(planes)
    spread = [wire.start(small_ref, small_out.at[z], plane) for plane in planes]
    small_out[z] = small_ref[...]
    for copy in spread:
        copy.wait_recv()
    wire.finish()


def start_exchange(small, replicas):
    return comm_call(
        functools.partial(start_kernel, replicas),
        "start_exchange",
        1,
        replicas - 1,
        [ON_CHIP],
        ON_CHIP,
        jax.ShapeDtypeStruct((replicas,) + small.shape, small.dtype),
        [],
        10**6,
    )(small)


def dense_kernel(replicas, grads, small, once, out, small_out, g_out, *refs):
    y_in, z_out, z_in, small_in, small_sum, turn_in = refs[:6]
    wire = Wire(*refs[6:])
    e, z = lax.axis_index("expert"), lax.axis_index("dp")
    head, row = lax.rem(e, 4), lax.div(e, 4)
    partners = [{"expert": flip(e, m)} for m in (1, 2, 4)]
    core, side_x, side_y = partners
    slab, width = grads.shape[0] // replicas, grads.shape[1]
    cut = slab // 2
    quarter = cut // 2
    order = [2, 1, 3, 0]
    block = {k: lax.rem(z + k, replicas) for k in range(replicas)}
    plane = {k: {"dp": block[k]} for k in range(1, replicas)}
    greet(partners + list(plane.values()))

    def hand(n, src, to):
        return pltpu.make_async_remote_copy(
            src_ref=src,
            dst_ref=g_out,
            send_sem=wire.send_sem.at[n],
            recv_sem=wire.recv_sem.at[23],
            device_id=to,
            device_id_type=MESH,
        )

    owner, over = head == z, flip(head, 2) == z
    to_core, to_x, onward = hand(23, once, core), hand(24, once, side_x), hand(25, g_out, core)

    @pl.when(owner)
    def _():
        to_x.start()
        to_core.start()
        g_out[...] = once[...]

    def half_of(k, which):
        return grads.at[pl.ds(pl.multiple_of(block[k] * slab + which * cut, cut), cut)]

    small_copies = [wire.start(small.at[block[k]], small_in.at[k - 1], plane[k]) for k in plane]
    from_y = {k: wire.start(half_of(k, 1 - row), y_in.at[k], side_y) for k in order}
    for copy in small_copies:
        copy.wait_recv()
    small_sum[0] = small[z] + small_in[0] + small_in[1] + small_in[2]
    turn = wire.start(small_sum.at[0], turn_in.at[0], core)
    from_z = {}
    for step, k in enumerate(order):
        from_y[k].wait_recv()
        add_into(cut, z_out.at[k], half_of(k, row), y_in.at[k])
        if k:
            from_z[k] = wire.start(z_out.at[k], z_in.at[k - 1], plane[k])
        if step == 0:
            turn.wait_recv()
            small_sum[1] = small_sum[0] + turn_in[0]
            turn = wire.start(small_sum.at[1], turn_in.at[1], side_x)
        if step == 1:
            turn.wait_recv()
            small_sum[2] = small_sum[1] + turn_in[1]
            turn = wire.start(small_sum.at[2], turn_in.at[2], side_y)
    turn.wait_recv()
    small_out[...] = small_sum[2] + turn_in[2]
    for k in from_z:
        from_z[k].wait_recv()

    def place(which_head, which_row, first=0, size=cut):
        start = pl.multiple_of(which_row * cut + first, quarter)
        columns = pl.ds(pl.multiple_of(which_head * width, 128), width)
        return out.at[pl.ds(start, size), columns]

    @pl.when(over)
    def _():
        to_x.wait_recv()
        onward.start()

    mine = place(head, row)
    add_into(cut, mine, z_out.at[0], z_in.at[0], z_in.at[1], z_in.at[2])
    other = flip(head, 2)
    pieces = [place(head, row, h * quarter, quarter) for h in range(2)]
    over_x = [wire.start(piece, piece, side_x) for piece in pieces]
    over_y = [wire.start(piece, piece, side_y) for piece in reversed(pieces)]
    last = [wire.start(mine, mine, core)]
    over_x[0].wait_recv()
    piece = place(other, row, 0, quarter)
    diag = [wire.start(piece, piece, side_y)]
    over_y[0].wait_recv()
    piece = place(head, 1 - row, quarter, quarter)
    diag.append(wire.start(piece, piece, side_x))
    over_x[1].wait_recv()
    last.append(wire.start(place(other, row), place(other, row), core))
    over_y[1].wait_recv()
    last.append(wire.start(place(head, 1 - row), place(head, 1 - row), core))
    for copy in diag:
        copy.wait_recv()
    last.append(wire.start(place(other, 1 - row), place(other, 1 - row), core))
    for copy in last:
        copy.wait_recv()
    @pl.when(owner)
    def _():
        to_x.wait_send()
        to_core.wait_send()

    pl.when(over)(onward.wait_send)
    pl.when(jnp.logical_not(jnp.logical_or(owner, over)))(to_core.wait_recv)
    wire.finish()


def dense_reduce(grads, small, once, replicas):
    slab, width = grads.shape[0] // replicas, grads.shape[1]
    piece = (slab // 2, width)
    lot = small.shape[1:]
    return comm_call(
        functools.partial(dense_kernel, replicas),
        "dense_reduce",
        2,
        26,
        [ON_CHIP] * 3,
        [ON_CHIP] * 3,
        [jax.ShapeDtypeStruct((slab, 4 * width), bf16), jax.ShapeDtypeStruct(lot, f32)]
        + [jax.ShapeDtypeStruct(once.shape, bf16)],
        [
            pltpu.VMEM((4,) + piece, bf16),
            pltpu.VMEM((4,) + piece, bf16),
            pltpu.VMEM((3,) + piece, bf16),
            pltpu.VMEM((3,) + lot, f32),
            pltpu.VMEM((3,) + lot, f32),
            pltpu.VMEM((3,) + lot, f32),
        ],
        10**8,
    )(grads, small, once)


STRIP = 256


def strips(ref_rows):
    return [(b * STRIP, (b + 1) * STRIP) for b in range(ref_rows // STRIP)]


def head_rows(index):
    return pl.ds(pl.multiple_of(index * HD, HD), HD)


def scores_of(keys, queries, first):
    raw = dg(keys, queries, TN)
    key = lax.broadcasted_iota(jnp.int32, raw.shape, 0)
    query = lax.broadcasted_iota(jnp.int32, raw.shape, 1) + first
    raw = jnp.where(key <= query, raw, NEG)
    grown = jnp.exp(raw - jnp.max(raw, axis=0, keepdims=True))
    return grown * (1.0 / jnp.sum(grown, axis=0, keepdims=True))


def attend_kernel(q_ref, k_ref, v_ref, out_ref):
    group = q_ref.shape[0] // k_ref.shape[0]

    @pl.loop(0, q_ref.shape[0] // HD)
    def _(h):
        mine, shared = head_rows(h), head_rows(lax.div(h, group))
        for first, last in strips(q_ref.shape[1]):
            probs = scores_of(k_ref[shared, :last], q_ref[mine, first:last], first)
            out = dg(v_ref[shared, :last], probs.astype(bf16), NN)
            out_ref[mine, first:last] = out.astype(bf16)


def attend_back_kernel(q_ref, k_ref, v_ref, grad_ref, dq_ref, dk_ref, dv_ref):
    group = q_ref.shape[0] // k_ref.shape[0]
    dk_ref[...] = jnp.zeros_like(dk_ref)
    dv_ref[...] = jnp.zeros_like(dv_ref)

    @pl.loop(0, q_ref.shape[0] // HD)
    def _(h):
        mine, shared = head_rows(h), head_rows(lax.div(h, group))
        for first, last in strips(q_ref.shape[1]):
            queries, grad = q_ref[mine, first:last], grad_ref[mine, first:last]
            keys = k_ref[shared, :last]
            probs = scores_of(keys, queries, first)
            grad_probs = dg(v_ref[shared, :last], grad, TN)
            delta = jnp.sum(probs * grad_probs, axis=0, keepdims=True)
            grad_scores = (probs * (grad_probs - delta)).astype(bf16)
            dq_ref[mine, first:last] = dg(keys, grad_scores, NN) * SCORE_SCALE
            dk_ref[shared, :last] += dg(queries, grad_scores, NT)
            dv_ref[shared, :last] += dg(grad, probs.astype(bf16), NT)


def on_chip_call(kernel, name, inputs, shapes, flops):
    return pl.pallas_call(
        kernel,
        in_specs=[ON_CHIP] * len(inputs),
        out_specs=[ON_CHIP] * len(shapes),
        out_shape=shapes,
        compiler_params=params(60),
        cost_estimate=pl.CostEstimate(
            flops=flops, bytes_accessed=10**7, transcendentals=4 * 10**6
        ),
        name=name,
    )(*inputs)


def attend(queries, keys, values):
    shapes = [jax.ShapeDtypeStruct(queries.shape, bf16)]
    return on_chip_call(attend_kernel, "attend", (queries, keys, values), shapes, 10**10)[0]


def attend_back(queries, keys, values, grad_context):
    shapes = [jax.ShapeDtypeStruct(x.shape, f32) for x in (queries, keys, values)]
    inputs = (queries, keys, values, grad_context)
    return on_chip_call(attend_back_kernel, "attend_back", inputs, shapes, 3 * 10**10)


def turned(x, cosine, sine):
    x = x.reshape(-1, 2, HD // 2, x.shape[1])
    first, second = x[:, 0], x[:, 1]
    out = jnp.stack([first * cosine - second * sine, second * cosine + first * sine], axis=1)
    return out.reshape(-1, x.shape[3])


def body(
    hidden_in,
    teacher,
    valid,
    routes,
    gain_attn,
    gain_moe,
    w_query,
    w_key,
    w_value,
    w_out,
    w_router,
    w_gate_up,
    w_down,
):
    tok, width = hidden_in.shape
    owners = lax.axis_size("expert")
    replicas = lax.axis_size("dp")
    me = lax.axis_index("expert")
    plane = lax.axis_index("dp")
    length = min(SEQ_MIN, owners * tok)
    group = length // tok
    head = me % group
    experts_all = EXP_DEV * owners
    slots = 8 * ((tok * TOP + experts_all * 7 - 1) // (experts_all * 7))
    half = replicas // 2
    side = plane // half
    ff_half = FF // 2
    slab = width // replicas
    q_cols = H * HD // group
    kv_cols = KVH * HD // group

    def over_dp(x, axis):
        if replicas > group:
            return lax.all_gather(x, "dp", axis=axis, tiled=True)
        return place(
            [x] + [send(x, "dp", m) for m in range(1, replicas)],
            [plane ^ m for m in range(replicas)],
            axis,
            replicas,
        )

    routes_t = jnp.transpose(routes)
    count = jnp.full_like(routes_t, jnp.sum(valid))
    small = jnp.concatenate(
        [gain_attn[None], gain_moe[None], jnp.transpose(w_router), jnp.zeros((6, slab), bf16)]
    )
    names = jnp.concatenate([routes_t, count])
    small = start_exchange(small, replicas)
    small = jnp.transpose(small, (1, 0, 2)).reshape(small.shape[1], width)
    gain_one, gain_two, router_t = small[0], small[1], small[2 : 2 + experts_all]
    me_ref = jnp.reshape(me, (1,)).astype(jnp.int32)
    valid_float = valid.astype(f32)
    qkv_slice = jnp.concatenate(
        [
            pick(w_query, head, q_cols, 1),
            pick(w_key, head, kv_cols, 1),
            pick(w_value, head, kv_cols, 1),
        ],
        axis=1,
    )
    inputs = hidden_in.astype(f32)
    normed_f, norm_one_pull = jax.vjp(rms_norm, inputs, gain_one.astype(f32))
    normed = normed_f.astype(bf16)
    compact = replicas == group

    def on_grid(x, pairs):
        return lax.ppermute(x, ("dp", "expert"), pairs)

    if compact:
        seq, qkv, out_slice = attention_entry(normed, qkv_slice, w_out, group)
    else:
        seq = seq_gather(normed, group, 3, "gather_normed")
        qkv = over_dp(qkv_slice, 0)
        out_slice = pick(lax.all_gather(w_out, "dp", axis=0, tiled=True), head, q_cols, 0)

    lin = mm("td,dc->ct", seq, qkv)
    cosine, sine = rope_tables(jnp.arange(length, dtype=f32))
    queries = turned(lin[:q_cols], cosine, sine).astype(bf16) * jnp.asarray(SCORE_SCALE, bf16)
    keys = turned(lin[q_cols : q_cols + kv_cols], cosine, sine).astype(bf16)
    values = lin[q_cols + kv_cols :].astype(bf16)
    context = attend(queries, keys, values)
    branch = mm("ct,cd->td", context, out_slice).astype(bf16)
    if compact:
        summed, gate_up_w, down_w = seq_scatter_weights(branch, group, (0,), w_gate_up, w_down)
    else:
        summed = seq_scatter(branch, group, 4, "scatter_branch")
        gate_up_all = lax.all_gather(w_gate_up, "dp", axis=1, tiled=True)
        gate_up_w = jnp.concatenate(
            [pick(gate_up_all, p * 2 + side, ff_half, 2) for p in range(2)], axis=2
        )
        down_w = pick(lax.all_gather(w_down, "dp", axis=1, tiled=True), side, ff_half, 1)
    mid = inputs + RESIDUAL * summed
    moe_f, norm_two_pull = jax.vjp(rms_norm, mid, gain_two.astype(f32))
    moe_input = moe_f.astype(bf16)

    if compact:
        blocks, (gate_up_w, down_w) = plane_gather(
            [moe_input, names],
            half,
            12,
            "gather_all",
            (1, 2),
            (w_gate_up, w_down),
            (gate_up_w, down_w),
        )
    else:
        blocks, _ = plane_gather([moe_input, names], half, 13, "gather_names")
    (near, far), (near_names, far_names) = blocks
    near_parts, near_kept, near_count = experts_forward(
        me_ref, near_names, router_t, near, gate_up_w, down_w
    )
    far_parts, far_kept, far_count = experts_forward(
        me_ref, far_names, router_t, far, gate_up_w, down_w
    )
    valid_count = near_count[0, :1] + far_count[0, :1]
    mask = 1
    while mask < half:
        valid_count = valid_count + send(valid_count, "dp", mask)
        mask *= 2
    valid_count = valid_count[0].astype(f32)
    final_state = mid + RESIDUAL * plane_scatter(near_parts, far_parts, half, 6, "scatter_outputs")[0]
    activations = final_state.astype(bf16)
    mismatch = final_state - teacher.astype(f32)
    squares = jnp.sum(0.5 * valid_float[:, None] * mismatch * mismatch)
    tokens_all = tok * replicas * owners
    grad_final = tokens_all / valid_count * valid_float[:, None] * mismatch

    ((grad_near, grad_far),), _ = plane_gather([grad_final.astype(bf16)], half, 5, "gather_tokens")

    def back(kept, blocks):
        arrived, lin, weighted, slot, gate = kept
        parts, (grads, lin_grad) = experts_backward(
            me_ref, slot, gate, lin, blocks, gate_up_w, down_w
        )
        return parts, (arrived, lin_grad, weighted, grads)

    near_grads, near_chunk = back(near_kept, grad_near)
    far_grads, far_chunk = back(far_kept, grad_far)
    grad_gate_up, grad_down = expert_weights(me_ref, [near_chunk, far_chunk])
    done = []
    if compact:
        returned, *part = plane_scatter(
            near_grads, far_grads, half, 7, "scatter_grads", 0, (grad_gate_up, grad_down)
        )
        done.append(part)
    else:
        (returned,) = plane_scatter(near_grads, far_grads, half, 14, "scatter_rows")

    grad_gates = returned[:, width : width + experts_all]
    own_routed = jnp.any(
        routes[:, :, None] == jnp.arange(experts_all, dtype=jnp.int32), axis=1
    )
    own_logits = jnp.where(own_routed, mm("td,ed->te", moe_input, router_t), NEG)
    own_gates = jnp.where(own_routed, jax.nn.softmax(own_logits, axis=-1), 0.0)
    grad_logits = (
        own_gates * (grad_gates - jnp.sum(own_gates * grad_gates, axis=-1, keepdims=True))
    ).astype(bf16)
    grad_router_t = mm("td,te->ed", moe_input, grad_logits)
    grad_moe_input = returned[:, :width] + mm("te,ed->td", grad_logits, router_t)
    grad_mid_norm, grad_gain_two = norm_two_pull(grad_moe_input)
    grad_mid = grad_final + grad_mid_norm
    grad_branch = (RESIDUAL * grad_mid).astype(bf16)

    if compact:
        seq_grad, *part = seq_gather_grads(grad_branch, group, 1, grad_gate_up, grad_down)
        done.append(part)
    else:
        seq_grad = seq_gather(grad_branch, group, 3, "gather_normed")
    grad_out = mm("ct,td->cd", context, seq_grad).astype(bf16)
    if compact:
        out_sum = grad_out.astype(f32)
        for step in range(1, replicas):
            pairs = [
                (
                    ((i % group + step) % replicas) * owners + i,
                    (i % group) * owners + i,
                )
                for i in range(owners)
            ]
            out_sum = out_sum + on_grid(grad_out, pairs).astype(f32)
    grad_context = mm("td,cd->ct", seq_grad, out_slice).astype(bf16)
    grad_q, grad_k, grad_v = attend_back(queries, keys, values, grad_context)
    grad_lin = jnp.concatenate(
        [turned(grad_q, cosine, -sine), turned(grad_k, cosine, -sine), grad_v]
    ).astype(bf16)
    grad_qkv = mm("td,ct->dc", seq, grad_lin).astype(bf16)
    normed_parts = mm("ct,dc->td", grad_lin, qkv)
    normed_parts = normed_parts.astype(bf16)
    if compact:
        grad_normed, *part, out_sum = seq_scatter_grads(
            normed_parts, group, 2, grad_gate_up, grad_down, out_sum.astype(bf16)
        )
        done.append(part)
    else:
        grad_normed = seq_scatter(normed_parts, group, 4, "scatter_branch")
    grad_in_norm, grad_gain_one = norm_one_pull(grad_normed)
    grad_in = grad_mid + grad_in_norm

    def other_sequences(x):
        total = x.astype(f32)
        mask = group
        while mask < owners:
            total = total + send(total.astype(bf16), "expert", mask).astype(f32)
            mask *= 2
        return total

    lot = jnp.concatenate(
        [
            grad_router_t,
            grad_gain_one[None],
            grad_gain_two[None],
            jnp.full((6, width), squares),
        ]
    )
    if compact:
        lot = jnp.transpose(lot.reshape(32, replicas, slab), (1, 0, 2))
        by_head, lot, g_out = dense_reduce(grad_qkv, lot, out_sum, replicas)
        g_out = g_out.astype(f32)
        gate_up_out, down_out = [jnp.stack(x).astype(f32) for x in zip(*done)]
    else:
        out_sum = other_sequences(lax.psum(grad_out, "dp")).astype(bf16)
        g_out = pick(
            place(
                gather_blocks(out_sum, group), [head ^ j for j in range(group)], 0, group
            ),
            plane,
            slab,
            0,
        ).astype(f32)
        lot = lax.psum_scatter(lot, "dp", scatter_dimension=1, tiled=True)
        lot = lax.psum(lot, "expert")
        qkv_sum = lax.psum_scatter(
            grad_qkv.astype(f32), "dp", scatter_dimension=0, tiled=True
        )
        qkv_sum = other_sequences(qkv_sum).astype(bf16)
        by_head = place(
            gather_blocks(qkv_sum, group), [head ^ j for j in range(group)], 1, group
        )
        spread = lambda x: lax.psum_scatter(
            x.astype(f32), "dp", scatter_dimension=1, tiled=True
        )
        blank = jnp.zeros_like(grad_down)
        down_out = spread(
            jnp.where(
                side == 0,
                jnp.concatenate([grad_down, blank], axis=1),
                jnp.concatenate([blank, grad_down], axis=1),
            )
        )
        first = spread(jnp.where(side == 0, grad_gate_up, jnp.zeros((), bf16)))
        last = spread(jnp.where(side == 1, grad_gate_up, jnp.zeros((), bf16)))
        gate_up_out = jnp.concatenate(
            [
                first[:, :, :ff_half],
                last[:, :, :ff_half],
                first[:, :, ff_half:],
                last[:, :, ff_half:],
            ],
            axis=2,
        )

    def of_heads(first, count):
        wide = q_cols + 2 * kv_cols
        return jnp.concatenate(
            [by_head[:, h * wide + first : h * wide + first + count] for h in range(group)], axis=1
        ).astype(f32)

    g_query = of_heads(0, q_cols)
    g_key = of_heads(q_cols, kv_cols)
    g_value = of_heads(q_cols + kv_cols, kv_cols)
    g_router, g_one, g_two = (
        jnp.transpose(lot[:experts_all]),
        lot[experts_all],
        lot[experts_all + 1],
    )
    loss_value = lot[experts_all + 2, 0] / (valid_count * width)

    return (
        activations,
        loss_value,
        grad_in,
        g_one,
        g_two,
        g_query,
        g_key,
        g_value,
        g_out,
        g_router,
        gate_up_out,
        down_out,
    )


def solution(mesh):
    placed = (
        P(("dp", "expert"), None),
        P(("dp", "expert"), None),
        P(("dp", "expert")),
        P(("dp", "expert"), None),
        P("dp"),
        P("dp"),
        P("dp", None),
        P("dp", None),
        P("dp", None),
        P("dp", None),
        P("dp", None),
        P("expert", "dp", None),
        P("expert", "dp", None),
    )
    return jax.shard_map(
        body,
        mesh=mesh,
        in_specs=placed,
        out_specs=(
            P(("dp", "expert"), None),
            P(),
            P(("dp", "expert"), None),
            P("dp"),
            P("dp"),
            P("dp", None),
            P("dp", None),
            P("dp", None),
            P("dp", None),
            P("dp", None),
            P("expert", "dp", None),
            P("expert", "dp", None),
        ),
        check_vma=False,
    )
```
